32 devices in a mesh: orbits: 2 (over x), sector: 8 (over z, y), spec: 2 (over core).
Axes of the slice: x: 2, y: 2, z: 4, core: 2. Of those that a mesh axis runs over, the one named last changes fastest.
Arguments:
- absorption: bfloat16 [16, 64, 8192], P(('orbits', 'sector'), None, 'spec'), parts along dimension 0, may hold values from 0.025 to 4
- absorber: float32 [16, 64], P(('orbits', 'sector')), parts along dimension 0, may hold values from 0.3 to 3
- seg_level: int32 [16, 3, 128, 32], P(('orbits', 'sector')), parts along dimension 0, may hold values from 0 to 63
- seg_count: int32 [16, 3, 128], P(('orbits', 'sector')), parts along dimension 0, may hold values from 1 to 32
- seg_length: float32 [16, 3, 128, 32], P(('orbits', 'sector')), parts along dimension 0, may hold values from 0.01 to 0.1
- measured: float32 [16, 128, 8192], P(('orbits', 'sector'), None, 'spec'), parts along dimension 0, may hold values from 0 to 1
- window_mask: int32 [8192], P('spec'), may hold values 0 or 1
- prior_weight: float32 [64], replicated, may hold values from 0.05 to 0.5
Outputs:
- spectrum: float32 [16, 128, 8192], P(('orbits', 'sector'), None, 'spec'), parts along dimension 0
- state_step: float32 [16, 64], P(('orbits', 'sector')), parts along dimension 0
The draws below stay inside these ranges and needn't reach their ends.
There are 2 independent parts, one for each index of `orbits`. The reference program is written for one: setup_inputs(seed, part) draws one part's arguments, and reference() takes and returns one part's arrays. A program takes and returns all parts, laid end to end along the dimension named above; an argument that names none is the same for every part. Nothing has to cross between parts.
Inputs may be any that keep to these rules, and one draw needn't show every extreme that they name: Segments j >= seg_count of a ray in a sector are ignored.
All inputs are finite; a program needn't handle non-finite values. No bound on the sum of `window_mask` on one device may be relied on, other than what follows from the above.
Results may differ from the reference program's by a relative error of at most 0.0028.
Values may be sent and summed in bfloat16 or wider, within the bound.
No kernel may reach another device: no remote copies, remote signals or barrier semaphores. Data moves between devices by JAX's collectives and lax.ppermute only.
A program may use at most 64 MiB of HBM per device.

```python
import math
import jax
import jax.numpy as jnp
from jax import lax

LEVELS = 64
FREQ = 8192
RAYS = 128
SEGS = 32
SECTORS = 8


def draw_absorption(key, part):
    strength_key = jax.random.fold_in(key, 11)
    rough_key = jax.random.fold_in(key, 12)
    line_strength = jnp.exp(jax.random.uniform(strength_key, (FREQ,), jnp.float32, math.log(0.05), math.log(2.0)))
    rough_factor = jnp.exp(jax.random.uniform(rough_key, (SECTORS, LEVELS, FREQ), jnp.float32, math.log(0.5), math.log(2.0)))
    return (line_strength[None, None, :] * rough_factor).astype(jnp.bfloat16)


def touch_ends(result, own_key, least, high):
    longest = result.shape.index(max(result.shape))
    spots = []
    for shift in (0, 1):
        where = [jax.random.randint(jax.random.fold_in(own_key, axis), (), 0, length) for axis, length in enumerate(result.shape)]
        where[longest] = (where[longest] + shift) % result.shape[longest]
        spots.append(tuple(where))
    return result.at[spots[0]].set(least).at[spots[1]].set(high)


def steps_of(stream_key, extent, shards, smallest, top_value):
    def one(axis_at, shards_of):
        heights = jax.random.uniform(jax.random.fold_in(jax.random.fold_in(stream_key, 6), axis_at), (shards_of,), jnp.float32, smallest / len(shards), top_value / len(shards))
        return jnp.repeat(jnp.exp(heights), extent[axis_at] // shards_of).reshape((-1,) + (1,) * (len(extent) - axis_at - 1))

    gain = one(*shards[0])
    for cut in shards[1:]:
        gain = gain * one(*cut)
    return gain


def setup_inputs(seed: int = 0, part: int = 0) -> dict:
    key_of = jax.random.split(jax.random.key(seed), 9)
    part_keys = jax.random.split(jax.random.fold_in(key_of[8], part), 9)
    return {
        "absorption": draw_absorption(jax.random.fold_in(jax.random.fold_in(key_of[8], part), 71), part),
        "absorber": jnp.clip(jnp.exp(math.log(3.0) - 2.3025851 * jax.random.uniform(part_keys[1], (SECTORS, LEVELS), jnp.float32) ** steps_of(part_keys[1], (SECTORS, LEVELS), ((0, 8),), -0.2, 0.2)), 0.3, 3.0),
        "seg_level": touch_ends(jax.random.randint(part_keys[2], (SECTORS, 3, RAYS, SEGS), 0, LEVELS), jax.random.fold_in(part_keys[2], 1), 0, LEVELS - 1).astype(jnp.int32),
        "seg_count": touch_ends(jax.random.randint(part_keys[3], (SECTORS, 3, RAYS), 1, SEGS + 1), jax.random.fold_in(part_keys[3], 1), 1, SEGS).astype(jnp.int32),
        "seg_length": jnp.clip(jnp.exp(math.log(0.1) - 2.3025851 * jax.random.uniform(part_keys[4], (SECTORS, 3, RAYS, SEGS), jnp.float32) ** steps_of(part_keys[4], (SECTORS, 3, RAYS, SEGS), ((0, 8),), -0.2, 0.2)), 0.01, 0.1),
        "measured": jnp.clip(1.0 * jax.random.uniform(part_keys[5], (SECTORS, RAYS, FREQ), jnp.float32) ** steps_of(part_keys[5], (SECTORS, RAYS, FREQ), ((0, 8), (2, 2)), -0.2, 0.2), 0.0, 1.0),
        "window_mask": touch_ends((jax.random.randint(key_of[6], (FREQ,), 0, 2) < 1).astype(jnp.int32), jax.random.fold_in(key_of[6], 1), 0, 1),
        "prior_weight": jnp.clip(jnp.exp(jax.random.uniform(key_of[7], (LEVELS,), jnp.float32, math.log(0.05), math.log(0.5))), 0.05, 0.5),
    }


def ray_paths(seg_level, seg_count, seg_length, absorber):
    depth_levels = absorber.shape[-1]
    alive_mask = (lax.broadcasted_iota(jnp.int32, seg_level.shape, seg_level.ndim - 1) < seg_count[..., None]).astype(jnp.float32)
    onehot = (seg_level[..., None] == lax.broadcasted_iota(jnp.int32, seg_level.shape + (depth_levels,), seg_level.ndim)).astype(jnp.float32)
    return jnp.einsum('...j,...jl->...l', seg_length * alive_mask, onehot, precision=lax.Precision.HIGHEST)

def level_moments(absorb_table, sq_wide):
    level_count = absorb_table.shape[0]
    group_size = min(level_count, max(1, 512 // level_count))
    table_wide = absorb_table.astype(jnp.float32)
    grouped = table_wide.reshape(level_count // group_size, group_size, absorb_table.shape[1])

    def one_group(level_rows):
        pair_table = (level_rows[:, None, :] * table_wide[None, :, :]).astype(jnp.bfloat16)
        pair_table = lax.optimization_barrier(pair_table).astype(jnp.float32)
        pair_table = pair_table.reshape(group_size * level_count, absorb_table.shape[1])
        return jnp.dot(pair_table, sq_wide.T, precision=lax.Precision.HIGHEST)
    return lax.map(one_group, grouped).reshape(level_count, level_count, sq_wide.shape[0])

def damped_step(normal, gradient, prior_weight):
    diag_mean = jnp.mean(jnp.diagonal(normal)) + 1e-06
    damped = normal + jnp.diag(prior_weight * diag_mean)
    factor = jnp.linalg.cholesky(damped)
    return -jax.scipy.linalg.cho_solve((factor, True), gradient)

def reference(absorption, absorber, seg_level, seg_count, seg_length, measured, window_mask, prior_weight):
    path_len = ray_paths(seg_level, seg_count, seg_length, absorber)
    absorbed = (path_len * absorber[:, None, None, :]).astype(jnp.bfloat16)
    partial_value = jnp.einsum('skrl,slf->skrf', absorbed.astype(jnp.float32), absorption.astype(jnp.float32), precision=lax.Precision.HIGHEST)
    optical_depth = partial_value[:, 1] + jnp.roll(partial_value[:, 0], -1, axis=0) + jnp.roll(partial_value[:, 2], 1, axis=0)
    spectrum = jnp.exp(-optical_depth)
    weights = window_mask.astype(jnp.float32)[None, None, :]
    weight_sq = (weights * spectrum * spectrum).astype(jnp.bfloat16)
    weighted_err = (weights * (measured - spectrum) * spectrum).astype(jnp.bfloat16)
    sq_sets = jnp.stack([jnp.roll(weight_sq, 1, axis=0), weight_sq, jnp.roll(weight_sq, -1, axis=0)], axis=1)
    err_sets = jnp.stack([jnp.roll(weighted_err, 1, axis=0), weighted_err, jnp.roll(weighted_err, -1, axis=0)], axis=1)
    weight_scale = 1.0 / (RAYS * FREQ)

    def one_sector(items):
        absorbed_here, table_here, sq_here, err_here = items
        absorbed_wide = absorbed_here.reshape(3 * RAYS, LEVELS).astype(jnp.float32)
        sq_wide = sq_here.reshape(3 * RAYS, FREQ).astype(jnp.float32)
        err_wide = err_here.reshape(3 * RAYS, FREQ).astype(jnp.float32)
        moment = level_moments(table_here, sq_wide)
        normal = weight_scale * jnp.einsum('lmq,ql,qm->lm', moment, absorbed_wide, absorbed_wide, precision=lax.Precision.HIGHEST)
        projected = jnp.dot(err_wide, table_here.astype(jnp.float32).T, precision=lax.Precision.HIGHEST)
        gradient = weight_scale * jnp.sum(absorbed_wide * projected, axis=0)
        return damped_step(normal, gradient, prior_weight)
    state_step = lax.map(one_sector, (absorbed, absorption, sq_sets, err_sets))
    return (spectrum, state_step)
```

```python
import functools

import jax
import jax.numpy as jnp
from jax import lax
from jax.experimental import pallas as pl
from jax.experimental.pallas import tpu as pltpu
from jax.sharding import PartitionSpec as P

LANES = 128
ROWS = 16
STEP = 512
CHUNKS = 4
VMEM_BYTES = 56 << 20


def passed_along(block, axis, distance):
    devices = range(lax.axis_size(axis))
    route = [((i - distance) % len(devices), i) for i in devices]
    return lax.ppermute(block, axis, route)


def iota(shape, dim):
    return lax.broadcasted_iota(jnp.int32, shape, dim)


def nt_dot(a, b):
    return lax.dot_general(a, b, (((1,), (1,)), ((), ())), preferred_element_type=jnp.float32)


def prepare_kernel(level_ref, count_ref, length_ref, absorber_ref, mask_ref, rows_ref, cols_ref, place_ref, base_ref):
    levels = absorber_ref.shape[1]
    sets, rays, segs = level_ref.shape
    eye = iota((levels, levels), 0) == iota((levels, levels), 1)
    amount = jnp.sum(jnp.where(eye, absorber_ref[...], 0.0), axis=1, keepdims=True)
    level_of = iota((levels, rays), 0)
    for k in range(sets):
        level = level_ref[k].T
        length = jnp.where(iota((segs, rays), 0) < count_ref[k : k + 1, :], length_ref[k].T, 0.0)
        path = jnp.zeros((levels, rays), jnp.float32)
        for j in range(segs):
            path += jnp.where(level[j : j + 1, :] == level_of, length[j : j + 1, :], 0.0)
        absorbed = path * amount
        cols_ref[k] = absorbed.astype(jnp.bfloat16)
        rows_ref[k] = absorbed.T.astype(jnp.bfloat16)
    groups = mask_ref.shape[0]
    mask = mask_ref[...].astype(jnp.bfloat16)
    before = (iota((LANES, LANES), 0) < iota((LANES, LANES), 1)).astype(jnp.bfloat16)
    rank = jnp.dot(mask, before, preferred_element_type=jnp.float32)
    total = jnp.dot(mask, jnp.ones((LANES, LANES), jnp.bfloat16), preferred_element_type=jnp.float32)
    earlier = (iota((groups, groups), 1) < iota((groups, groups), 0)).astype(jnp.bfloat16)
    base = jnp.dot(earlier, total.astype(jnp.bfloat16), preferred_element_type=jnp.float32)
    place_ref[...] = jnp.where(mask_ref[...] > 0, (base + rank).astype(jnp.int32), -1)
    base_ref[pl.ds(0, groups), :] = base.astype(jnp.int32)
    last = base[groups - 1 : groups, :] + total[groups - 1 : groups, :]
    base_ref[pl.ds(groups, 8), :] = jnp.broadcast_to(last, (8, LANES)).astype(jnp.int32)


def prepare(level, count, length, absorber, mask):
    sets, rays, _ = level.shape
    levels = absorber.shape[1]
    groups = mask.shape[0]
    return pl.pallas_call(
        prepare_kernel,
        out_shape=(
            jax.ShapeDtypeStruct((sets, rays, levels), jnp.bfloat16),
            jax.ShapeDtypeStruct((sets, levels, rays), jnp.bfloat16),
            jax.ShapeDtypeStruct((groups, LANES), jnp.int32),
            jax.ShapeDtypeStruct((groups + 8, LANES), jnp.int32),
        ),
        name="prepare",
    )(level, count, length, absorber, mask)


def pair_rows(levels):
    spans = []
    offset = 0
    for m in range(levels):
        first = ROWS * (m // ROWS)
        spans.append((m, first, offset, levels - first))
        offset += levels - first
    return spans, offset


def chunk_kernel(
    base_ref, before_ref, here_ref, after_ref, rows_ref, cols_ref, measured_ref, place_ref, earlier_ref, filler_ref,
    spectrum_ref, terms_ref, table, packed, pairs, weights, moment, projected, *, first_group,
):
    del filler_ref
    step = pl.program_id(0)
    steps = pl.num_programs(0)
    levels = here_ref.shape[0]
    rays = measured_ref.shape[0]
    high = 3 * levels
    width = here_ref.shape[1]
    groups = width // LANES
    spans, pair_count = pair_rows(levels)

    @pl.when(step == 0)
    def _():
        moment[...] = jnp.zeros_like(moment)
        projected[...] = jnp.zeros_like(projected)
        packed[...] = jnp.zeros_like(packed)

    table[0:levels, :] = before_ref[...]
    table[levels : 2 * levels, :] = here_ref[...]
    table[2 * levels : high, :] = after_ref[...]
    depth = jnp.dot(rows_ref[...], table[0:high, :], preferred_element_type=jnp.float32)
    spectrum = jnp.exp(-depth)
    spectrum_ref[...] = spectrum
    table[high : high + rays, :] = (spectrum * spectrum).astype(jnp.bfloat16)
    table[high + rays :, :] = ((measured_ref[...] - spectrum) * spectrum).astype(jnp.bfloat16)

    start = base_ref[first_group, 0]
    for g in range(groups):
        group = first_group + step * groups + g
        at = (base_ref[group, 0] - start) // LANES
        chosen = (iota((2 * LANES, LANES), 0) + at * LANES + start == place_ref[g]).astype(jnp.bfloat16)
        moved = nt_dot(table[:, g * LANES : (g + 1) * LANES], chosen).astype(jnp.bfloat16)
        packed[at] = packed[at] + moved[:, :LANES]
        packed[at + 1] = moved[:, LANES:]

    def one_block(block, parts):
        wide = parts * LANES
        for p in range(parts):
            lane = slice(p * LANES, (p + 1) * LANES)
            weights[:, lane] = packed[block + p, high:, :]
            for k in range(3):
                rows = packed[block + p, k * levels : (k + 1) * levels, :]
                for m, first, offset, count in spans:
                    pairs[k, offset : offset + count, lane] = rows[first:, :] * rows[m : m + 1, :]
        for k in range(3):
            moment[k] += nt_dot(pairs[k, :, :wide], weights[:rays, :wide])
        tables = jnp.concatenate([packed[block + p, :high, :] for p in range(parts)], axis=1)
        projected[...] += nt_dot(tables, weights[rays:, :wide])

    def done_by(group):
        return (base_ref[group, 0] - start) // STEP

    parts = STEP // LANES
    done = done_by(first_group + step * groups)
    ready = done_by(first_group + (step + 1) * groups)
    lax.fori_loop(done, ready, lambda block, carry: (one_block(block * parts, parts), carry)[1], 0)

    @pl.when(step == steps - 1)
    def _():
        left = base_ref[first_group + steps * groups, 0] - start - ready * STEP

        @pl.when(left > 0)
        def _():
            one_block(ready * parts, parts)

        lane = iota((levels, LANES), 1)
        for k in range(3):
            cols = cols_ref[k].astype(jnp.float32)
            gradient = jnp.sum(cols * projected[k * levels : (k + 1) * levels, :], axis=1, keepdims=True)
            result = jnp.where(lane == levels, gradient, 0.0)
            for m, first, offset, count in spans:
                column = jnp.sum(
                    moment[k, offset : offset + count, :] * (cols[first:, :] * cols[m : m + 1, :]), axis=1, keepdims=True
                )
                if first:
                    column = jnp.concatenate([jnp.zeros((first, 1), jnp.float32), column], axis=0)
                result = jnp.where(lane == m, column, result)
            terms_ref[k] = result + earlier_ref[k]


def chunk(base, before, here, after, rows, cols, measured, place, earlier, filler, index, width):
    levels = here.shape[0]
    rays = measured.shape[0]
    steps = width // STEP
    groups = width // LANES
    step_groups = STEP // LANES
    _, pair_count = pair_rows(levels)
    offset = index * steps

    def whole(shape):
        return pl.BlockSpec(shape, lambda i, base: (0,) * len(shape))

    return pl.pallas_call(
        functools.partial(chunk_kernel, first_group=index * groups),
        grid_spec=pltpu.PrefetchScalarGridSpec(
            num_scalar_prefetch=1,
            grid=(steps,),
            in_specs=[
                pl.BlockSpec((levels, STEP), lambda i, base: (0, i)),
                pl.BlockSpec((levels, STEP), lambda i, base: (0, i + offset)),
                pl.BlockSpec((levels, STEP), lambda i, base: (0, i)),
                whole(rows.shape),
                whole(cols.shape),
                pl.BlockSpec((rays, STEP), lambda i, base: (0, i + offset)),
                pl.BlockSpec((step_groups, 1, LANES), lambda i, base: (i + offset, 0, 0)),
                whole(earlier.shape),
                pl.BlockSpec(memory_space=pl.ANY),
            ],
            out_specs=[
                pl.BlockSpec((rays, STEP), lambda i, base: (0, i + offset)),
                whole(earlier.shape),
            ],
            scratch_shapes=[
                pltpu.VMEM((3 * levels + 2 * rays, STEP), jnp.bfloat16),
                pltpu.VMEM((groups + step_groups + 2, 3 * levels + 2 * rays, LANES), jnp.bfloat16),
                pltpu.VMEM((3, pair_count, STEP), jnp.bfloat16),
                pltpu.VMEM((2 * rays, STEP), jnp.bfloat16),
                pltpu.VMEM((3, pair_count, rays), jnp.float32),
                pltpu.VMEM((3 * levels, rays), jnp.float32),
            ],
        ),
        out_shape=(
            jax.ShapeDtypeStruct(measured.shape, jnp.float32),
            jax.ShapeDtypeStruct(earlier.shape, jnp.float32),
        ),
        input_output_aliases={9: 0},
        compiler_params=pltpu.CompilerParams(vmem_limit_bytes=VMEM_BYTES),
        name="chunk",
    )(base, before, here, after, rows, cols, measured, place, earlier, filler)


def solve_kernel(mine_ref, other_ref, prior_ref, out_ref, *, scale):
    levels = prior_ref.shape[1]
    terms = (mine_ref[...] + other_ref[...]) * scale
    row = iota((levels, LANES), 0)
    lane = iota((levels, LANES), 1)
    square = terms[:, :levels]
    flipped = jnp.concatenate([square.T, jnp.zeros((levels, LANES - levels), jnp.float32)], axis=1)
    lower = row // ROWS >= lane // ROWS
    work = jnp.where(lower | (lane >= levels), terms, flipped)
    diagonal = jnp.sum(jnp.where(row == lane, work, 0.0), axis=1, keepdims=True)
    mean = jnp.sum(diagonal, axis=0, keepdims=True) * (1.0 / levels) + 1e-06
    eye = iota((levels, levels), 0) == iota((levels, levels), 1)
    prior = jnp.sum(jnp.where(eye, prior_ref[...], 0.0), axis=1, keepdims=True)
    work = work + jnp.where(row == lane, prior * mean, 0.0)
    for i in range(levels):
        pivot_row = work[i : i + 1, :]
        pivot = pivot_row[:, i : i + 1]
        scaled = pivot_row / pivot
        column = work[:, i : i + 1]
        factor = jnp.where(row[:, :1] == i, column - 1.0, column)
        work = work - factor * scaled
    column = work[:, levels : levels + 1]
    out_ref[...] = -jnp.sum(jnp.where(eye, column, 0.0), axis=0, keepdims=True)


def solve(mine, other, prior_weight, scale):
    return pl.pallas_call(
        functools.partial(solve_kernel, scale=scale),
        out_shape=jax.ShapeDtypeStruct((1, mine.shape[0]), jnp.float32),
        name="solve",
    )(mine, other, prior_weight)


def shards(absorption, absorber, seg_level, seg_count, seg_length, measured, window_mask, prior_weight):
    table = absorption[0]
    levels, points = table.shape
    rays = measured.shape[1]
    width = points // CHUNKS
    pieces = [table[:, c * width : (c + 1) * width] for c in range(CHUNKS)]
    below = []
    above = []
    for piece in pieces:
        below.append(passed_along(piece, "sector", 1))
        above.append(passed_along(piece, "sector", -1))
    mask = window_mask.reshape(points // LANES, LANES)
    rows, cols, place, base = prepare(seg_level[0], seg_count[0], seg_length[0], absorber, mask)
    place = place.reshape(points // LANES, 1, LANES)
    base = base[:, :1]
    both = jnp.stack
    cols_below = passed_along(cols[2], "sector", 1)
    cols_above = passed_along(cols[0], "sector", -1)
    all_cols = both([cols_below, cols[1], cols_above])
    all_rows = all_cols.reshape(3 * levels, rays).T
    terms = jnp.zeros((3, levels, LANES), jnp.float32)
    spectrum = jnp.zeros(measured.shape[1:], jnp.float32)
    for c in range(CHUNKS):
        spectrum, terms = chunk(
            base, below[c], table, above[c], all_rows, all_cols, measured[0], place, terms, spectrum, c, width
        )
    from_above = passed_along(terms[0], "sector", -1)
    from_below = passed_along(terms[2], "sector", 1)
    mine = terms[1] + from_above + from_below
    swap = [(i, 1 - i) for i in range(2)]
    other = lax.ppermute(mine, "spec", swap)
    scale = 1.0 / (rays * points * lax.axis_size("spec"))
    state_step = solve(mine, other, prior_weight[None, :], scale)
    return (spectrum[None], state_step)


def solution(mesh):
    return jax.shard_map(
        shards,
        mesh=mesh,
        in_specs=(
            P(("orbits", "sector"), None, "spec"),
            P(("orbits", "sector"), None),
            P(("orbits", "sector"), None, None, None),
            P(("orbits", "sector"), None, None),
            P(("orbits", "sector"), None, None, None),
            P(("orbits", "sector"), None, "spec"),
            P("spec"),
            P(),
        ),
        out_specs=(P(("orbits", "sector"), None, "spec"), P(("orbits", "sector"), None)),
        check_vma=False,
    )
```

```python
import functools

import jax
import jax.numpy as jnp
from jax import lax
from jax.experimental import pallas as pl
from jax.experimental.pallas import tpu as pltpu
from jax.sharding import PartitionSpec as P

LANES = 128
ROWS = 16
PIECE = 512
BLOCK = 512
WIDTHS = (3, 3, 2)
VMEM_BYTES = 56 << 20
CHEAP = pl.CostEstimate(flops=1, transcendentals=0, bytes_accessed=1)


def passed_along(block, axis, distance):
    devices = range(lax.axis_size(axis))
    route = [((i - distance) % len(devices), i) for i in devices]
    return lax.ppermute(block, axis, route)


def iota(shape, dim):
    return lax.broadcasted_iota(jnp.int32, shape, dim)


def nt_dot(a, b):
    return lax.dot_general(a, b, (((1,), (1,)), ((), ())), preferred_element_type=jnp.float32)


def prepare_kernel(level_ref, count_ref, length_ref, absorber_ref, mask_ref, *outs):
    cols_refs = outs[:3]
    place_ref, base_ref = outs[3:]
    levels = absorber_ref.shape[1]
    sets, segs, rays = level_ref.shape
    eye = iota((levels, levels), 0) == iota((levels, levels), 1)
    amount = jnp.sum(jnp.where(eye, absorber_ref[...], 0.0), axis=1, keepdims=True)
    level_of = iota((levels, rays), 0)
    for k in range(sets):
        length = jnp.where(iota((segs, rays), 0) < count_ref[k], length_ref[k], 0.0)
        level = level_ref[k]
        path = jnp.zeros((levels, rays), jnp.float32)
        for j in range(segs):
            path += jnp.where(level[j : j + 1, :] == level_of, length[j : j + 1, :], 0.0)
        cols_refs[k][...] = (path * amount).astype(jnp.bfloat16)
    groups = mask_ref.shape[0]
    mask = mask_ref[...].astype(jnp.bfloat16)
    before = (iota((LANES, LANES), 0) < iota((LANES, LANES), 1)).astype(jnp.bfloat16)
    rank = jnp.dot(mask, before, preferred_element_type=jnp.float32)
    total = jnp.dot(mask, jnp.ones((LANES, LANES), jnp.bfloat16), preferred_element_type=jnp.float32)
    earlier = (iota((groups, groups), 1) < iota((groups, groups), 0)).astype(jnp.bfloat16)
    base = jnp.dot(earlier, total.astype(jnp.bfloat16), preferred_element_type=jnp.float32)
    place_ref[...] = jnp.where(mask_ref[...] > 0, (base + rank).astype(jnp.int32), -1)
    base_ref[pl.ds(0, groups), :] = base.astype(jnp.int32)
    last = base[groups - 1 : groups, :] + total[groups - 1 : groups, :]
    base_ref[pl.ds(groups, 8), :] = jnp.broadcast_to(last, (8, LANES)).astype(jnp.int32)


def prepare(level, count, length, absorber, mask):
    rays = level.shape[2]
    levels = absorber.shape[1]
    groups = mask.shape[0]
    cols = jax.ShapeDtypeStruct((levels, rays), jnp.bfloat16)
    return pl.pallas_call(
        prepare_kernel,
        out_shape=(
            cols,
            cols,
            cols,
            jax.ShapeDtypeStruct((groups, LANES), jnp.int32),
            jax.ShapeDtypeStruct((groups + 8, LANES), jnp.int32),
        ),
        cost_estimate=CHEAP,
        name="prepare",
    )(level, count, length, absorber, mask)


def pair_rows(levels):
    spans = []
    offset = 0
    for m in range(levels):
        first = ROWS * (m // ROWS)
        spans.append((m, first, offset, levels - first))
        offset += levels - first
    return spans, offset


def chunk_kernel(*refs, first, width, follows):
    base_ref, before_ref, here_ref, after_ref, place_ref, measured_ref = refs[:6]
    cols_refs = refs[6:9]
    refs = refs[9:]
    if follows:
        earlier_refs = refs[:3]
        refs = refs[4:]
    spectrum_ref = refs[0]
    terms_refs = refs[1:4]
    table, observed, modelled, packed, pairs, weights, moment, in_sems, out_sems = refs[4:]
    levels = here_ref.shape[0]
    rays = measured_ref.shape[0]
    high = 3 * levels
    pieces = width // PIECE
    spans, pair_count = pair_rows(levels)

    def incoming(piece):
        local = pl.ds(piece * PIECE, PIECE)
        overall = pl.ds(first + piece * PIECE, PIECE)
        sources = (
            (before_ref.at[:, local], table.at[pl.ds(0, levels), local]),
            (here_ref.at[:, overall], table.at[pl.ds(levels, levels), local]),
            (after_ref.at[:, local], table.at[pl.ds(2 * levels, levels), local]),
            (measured_ref.at[:, overall], observed.at[:, local]),
        )
        return [pltpu.make_async_copy(a, b, in_sems.at[piece, n]) for n, (a, b) in enumerate(sources)]

    def outgoing(piece):
        return pltpu.make_async_copy(
            modelled.at[:, pl.ds(piece * PIECE, PIECE)],
            spectrum_ref.at[:, pl.ds(first + piece * PIECE, PIECE)],
            out_sems.at[piece],
        )

    for piece in range(pieces):
        for copy in incoming(piece):
            copy.start()

    cols = [ref[...].astype(jnp.float32) for ref in cols_refs]
    rows = jnp.concatenate([c.T for c in cols], axis=1).astype(jnp.bfloat16)
    moment[...] = jnp.zeros_like(moment)
    packed[...] = jnp.zeros_like(packed)
    start = base_ref[first // LANES, 0]
    projected = jnp.zeros((high, rays), jnp.float32)

    for piece in range(pieces):
        for copy in incoming(piece):
            copy.wait()
        lane = slice(piece * PIECE, (piece + 1) * PIECE)
        depth = jnp.dot(rows, table[:high, lane], preferred_element_type=jnp.float32)
        spectrum = jnp.exp(-depth)
        modelled[:, lane] = spectrum
        outgoing(piece).start()
        table[high:, lane] = (spectrum * spectrum).astype(jnp.bfloat16)
        groups = range(piece * PIECE // LANES, (piece + 1) * PIECE // LANES)
        places = [place_ref[first // LANES + g : first // LANES + g + 1, :] for g in groups]
        kept = jnp.concatenate(places, axis=1) >= 0
        error = jnp.where(kept, (observed[:, lane] - spectrum) * spectrum, 0.0).astype(jnp.bfloat16)
        projected += nt_dot(table[:high, lane], error)
        for g, place in zip(groups, places, strict=True):
            at = (base_ref[first // LANES + g, 0] - start) // LANES
            chosen = (iota((2 * LANES, LANES), 0) + (at * LANES + start) == place).astype(jnp.bfloat16)
            moved = nt_dot(table[:, g * LANES : (g + 1) * LANES], chosen).astype(jnp.bfloat16)
            packed[at] = packed[at] + moved[:, :LANES]
            packed[at + 1] = moved[:, LANES:]

    def one_block(block, parts):
        wide = parts * LANES
        for p in range(parts):
            lane = slice(p * LANES, (p + 1) * LANES)
            weights[:, lane] = packed[block + p, high:, :]
            for k in range(3):
                level_rows = packed[block + p, k * levels : (k + 1) * levels, :]
                for m, low, offset, count in spans:
                    pairs[k, offset : offset + count, lane] = level_rows[low:, :] * level_rows[m : m + 1, :]
        for k in range(3):
            moment[k] += nt_dot(pairs[k, :, :wide], weights[:, :wide])

    count = base_ref[(first + width) // LANES, 0] - start
    ready = count // BLOCK
    parts = BLOCK // LANES
    lax.fori_loop(0, ready, lambda block, carry: (one_block(block * parts, parts), carry)[1], 0)
    left = count - ready * BLOCK

    @pl.when(left > BLOCK // 2)
    def _():
        one_block(ready * parts, parts)

    @pl.when((left > 0) & (left <= BLOCK // 2))
    def _():
        one_block(ready * parts, parts // 2)

    lane = iota((levels, LANES), 1)
    for k in range(3):
        gradient = jnp.sum(cols[k] * projected[k * levels : (k + 1) * levels, :], axis=1, keepdims=True)
        result = jnp.where(lane == levels, gradient, 0.0)
        for m, low, offset, count in spans:
            column = jnp.sum(
                moment[k, offset : offset + count, :] * (cols[k][low:, :] * cols[k][m : m + 1, :]), axis=1, keepdims=True
            )
            if low:
                column = jnp.concatenate([jnp.zeros((low, 1), jnp.float32), column], axis=0)
            result = jnp.where(lane == m, column, result)
        if follows:
            result = result + earlier_refs[k][...]
        terms_refs[k][...] = result
    for piece in range(pieces):
        outgoing(piece).wait()


def chunk(base, before, here, after, place, measured, cols, earlier, spectrum, first, width):
    levels = here.shape[0]
    rays = measured.shape[0]
    pieces = width // PIECE
    _, pair_count = pair_rows(levels)
    follows = earlier is not None
    smem = pl.BlockSpec(memory_space=pltpu.SMEM)
    vmem = pl.BlockSpec(memory_space=pltpu.VMEM)
    left = pl.BlockSpec(memory_space=pl.ANY)
    terms = jax.ShapeDtypeStruct((levels, LANES), jnp.float32)
    args = [base, before, here, after, place, measured, *cols]
    specs = [smem, left, left, left, vmem, left, vmem, vmem, vmem]
    if follows:
        args += [*earlier, spectrum]
        specs += [vmem, vmem, vmem, left]
    outs = pl.pallas_call(
        functools.partial(chunk_kernel, first=first, width=width, follows=follows),
        in_specs=specs,
        out_specs=[left, vmem, vmem, vmem],
        out_shape=(jax.ShapeDtypeStruct(measured.shape, jnp.float32), terms, terms, terms),
        scratch_shapes=[
            pltpu.VMEM((3 * levels + rays, width), jnp.bfloat16),
            pltpu.VMEM((rays, width), jnp.float32),
            pltpu.VMEM((rays, width), jnp.float32),
            pltpu.VMEM(((width + BLOCK) // LANES + 2, 3 * levels + rays, LANES), jnp.bfloat16),
            pltpu.VMEM((3, pair_count, BLOCK), jnp.bfloat16),
            pltpu.VMEM((rays, BLOCK), jnp.bfloat16),
            pltpu.VMEM((3, pair_count, rays), jnp.float32),
            pltpu.SemaphoreType.DMA((pieces, 4)),
            pltpu.SemaphoreType.DMA((pieces,)),
        ],
        input_output_aliases={12: 0} if follows else {},
        compiler_params=pltpu.CompilerParams(vmem_limit_bytes=VMEM_BYTES),
        cost_estimate=CHEAP,
        name="chunk",
    )(*args)
    return outs[0], outs[1:]


def solve_kernel(*refs, scale):
    parts = refs[:6]
    prior_ref, out_ref = refs[6:]
    levels = prior_ref.shape[1]
    total = parts[0][...]
    for part in parts[1:]:
        total = total + part[...]
    terms = total * scale
    row = iota((levels, LANES), 0)
    lane = iota((levels, LANES), 1)
    square = terms[:, :levels]
    flipped = jnp.concatenate([square.T, jnp.zeros((levels, LANES - levels), jnp.float32)], axis=1)
    lower = row // ROWS >= lane // ROWS
    work = jnp.where(lower | (lane >= levels), terms, flipped)
    diagonal = jnp.sum(jnp.where(row == lane, work, 0.0), axis=1, keepdims=True)
    mean = jnp.sum(diagonal, axis=0, keepdims=True) * (1.0 / levels) + 1e-06
    eye = iota((levels, levels), 0) == iota((levels, levels), 1)
    prior = jnp.sum(jnp.where(eye, prior_ref[...], 0.0), axis=1, keepdims=True)
    work = work + jnp.where(row == lane, prior * mean, 0.0)
    for i in range(levels):
        pivot_row = work[i : i + 1, :]
        scaled = pivot_row * (1.0 / pivot_row[:, i : i + 1])
        column = work[:, i : i + 1]
        factor = jnp.where(row[:, :1] == i, column - 1.0, column)
        work = work - factor * scaled
    column = work[:, levels : levels + 1]
    out_ref[...] = -jnp.sum(jnp.where(eye, column, 0.0), axis=0, keepdims=True)


def solve(parts, prior_weight, scale):
    return pl.pallas_call(
        functools.partial(solve_kernel, scale=scale),
        out_shape=jax.ShapeDtypeStruct((1, prior_weight.shape[1]), jnp.float32),
        cost_estimate=CHEAP,
        name="solve",
    )(*parts, prior_weight)


def swapped(block, axis):
    size = lax.axis_size(axis)
    return lax.ppermute(block, axis, [(i, size - 1 - i) for i in range(size)])


def shards(absorption, absorber, seg_level, seg_count, seg_length, measured, window_mask, prior_weight):
    table = absorption[0]
    levels, points = table.shape
    rays = measured.shape[1]
    widths = [w * points // sum(WIDTHS) for w in WIDTHS]
    firsts = [sum(widths[:c]) for c in range(len(widths))]
    below = []
    above = []
    for first, width in zip(firsts, widths, strict=True):
        piece = table[:, first : first + width]
        below.append(passed_along(piece, "sector", 1))
        above.append(passed_along(piece, "sector", -1))
    mask = window_mask.reshape(points // LANES, LANES)
    level = jnp.swapaxes(seg_level[0], 1, 2)
    length = jnp.swapaxes(seg_length[0], 1, 2)
    count = seg_count.reshape(3, 1, rays)
    cols_low, cols_here, cols_high, place, base = prepare(level, count, length, absorber, mask)
    base = base[:, :1]
    cols = (passed_along(cols_high, "sector", 1), cols_here, passed_along(cols_low, "sector", -1))
    terms = spectrum = None
    for c, (first, width) in enumerate(zip(firsts, widths, strict=True)):
        spectrum, terms = chunk(base, below[c], table, above[c], place, measured[0], cols, terms, spectrum, first, width)
    mine = (terms[1], passed_along(terms[0], "sector", -1), passed_along(terms[2], "sector", 1))
    others = tuple(swapped(part, "spec") for part in mine)
    scale = 1.0 / (rays * points * lax.axis_size("spec"))
    state_step = solve(mine + others, prior_weight[None, :], scale)
    return (spectrum[None], state_step)


def solution(mesh):
    return jax.shard_map(
        shards,
        mesh=mesh,
        in_specs=(
            P(("orbits", "sector"), None, "spec"),
            P(("orbits", "sector"), None),
            P(("orbits", "sector"), None, None, None),
            P(("orbits", "sector"), None, None),
            P(("orbits", "sector"), None, None, None),
            P(("orbits", "sector"), None, "spec"),
            P("spec"),
            P(),
        ),
        out_specs=(P(("orbits", "sector"), None, "spec"), P(("orbits", "sector"), None)),
        check_vma=False,
    )
```

```python
import functools

import jax
import jax.numpy as jnp
from jax import lax
from jax.experimental import pallas as pl
from jax.experimental.pallas import tpu as pltpu
from jax.sharding import PartitionSpec as P

LANES = 128
ROWS = 16
PIECE = 512
BLOCK = 512
WIDTHS = (2, 2, 2, 2)
GROUPS = ((0, 1), (2,), (3,))
CARRIER = 1
SMALL_BYTES = 4 << 20
CHUNK_BYTES = 16 << 20
CHEAP = pl.CostEstimate(flops=1, transcendentals=0, bytes_accessed=1)


def passed_along(block, axis, distance):
    devices = range(lax.axis_size(axis))
    route = [((i - distance) % len(devices), i) for i in devices]
    return lax.ppermute(block, axis, route)


def iota(shape, dim):
    return lax.broadcasted_iota(jnp.int32, shape, dim)


def nt_dot(a, b):
    return lax.dot_general(a, b, (((1,), (1,)), ((), ())), preferred_element_type=jnp.float32)


def prepare_kernel(level_ref, count_ref, length_ref, absorber_ref, mask_ref, table_ref, *outs, first, width):
    up_ref, down_ref, cols_ref, place_ref, base_ref, sems = outs
    levels = absorber_ref.shape[1]
    sets, segs, rays = level_ref.shape
    copies = [
        pltpu.make_async_copy(table_ref.at[:, pl.ds(first, width)], ref.at[:, pl.ds(0, width)], sems.at[n])
        for n, ref in enumerate((up_ref, down_ref))
    ]
    for copy in copies:
        copy.start()
    eye = iota((levels, levels), 0) == iota((levels, levels), 1)
    amount = jnp.sum(jnp.where(eye, absorber_ref[...], 0.0), axis=1, keepdims=True)
    level_of = iota((levels, rays), 0)
    for k in range(sets):
        length = jnp.where(iota((segs, rays), 0) < count_ref[k], length_ref[k], 0.0)
        level = level_ref[k]
        path = jnp.zeros((levels, rays), jnp.float32)
        for j in range(segs):
            path += jnp.where(level[j : j + 1, :] == level_of, length[j : j + 1, :], 0.0)
        absorbed = (path * amount).astype(jnp.bfloat16)
        if k == 0:
            down_ref[:, width:] = absorbed
        elif k == 1:
            cols_ref[...] = absorbed
        else:
            up_ref[:, width:] = absorbed
    groups = mask_ref.shape[0]
    mask = mask_ref[...].astype(jnp.bfloat16)
    before = (iota((LANES, LANES), 0) < iota((LANES, LANES), 1)).astype(jnp.bfloat16)
    rank = jnp.dot(mask, before, preferred_element_type=jnp.float32)
    total = jnp.dot(mask, jnp.ones((LANES, LANES), jnp.bfloat16), preferred_element_type=jnp.float32)
    earlier = (iota((groups, groups), 1) < iota((groups, groups), 0)).astype(jnp.bfloat16)
    base = jnp.dot(earlier, total.astype(jnp.bfloat16), preferred_element_type=jnp.float32)
    place_ref[...] = jnp.where(mask_ref[...] > 0, (base + rank).astype(jnp.int32), -1)
    base_ref[pl.ds(0, groups), :] = base.astype(jnp.int32)
    last = base[groups - 1 : groups, :] + total[groups - 1 : groups, :]
    base_ref[pl.ds(groups, 8), :] = jnp.broadcast_to(last, (8, LANES)).astype(jnp.int32)
    for copy in copies:
        copy.wait()


def prepare(level, count, length, absorber, mask, table, first, width):
    rays = level.shape[2]
    levels = absorber.shape[1]
    groups = mask.shape[0]
    send = jax.ShapeDtypeStruct((levels, width + rays), jnp.bfloat16)
    vmem = pl.BlockSpec(memory_space=pltpu.VMEM)
    return pl.pallas_call(
        functools.partial(prepare_kernel, first=first, width=width),
        in_specs=[vmem] * 5 + [pl.BlockSpec(memory_space=pl.ANY)],
        out_shape=(
            send,
            send,
            jax.ShapeDtypeStruct((levels, rays), jnp.bfloat16),
            jax.ShapeDtypeStruct((groups, LANES), jnp.int32),
            jax.ShapeDtypeStruct((groups + 8, LANES), jnp.int32),
        ),
        scratch_shapes=[pltpu.SemaphoreType.DMA((2,))],
        compiler_params=pltpu.CompilerParams(vmem_limit_bytes=SMALL_BYTES),
        cost_estimate=CHEAP,
        name="prepare",
    )(level, count, length, absorber, mask, table)


def pair_rows(levels):
    spans = []
    offset = 0
    for m in range(levels):
        first = ROWS * (m // ROWS)
        spans.append((m, first, offset, levels - first))
        offset += levels - first
    return spans, offset


def chunk_kernel(*refs, spans_of, carrier, opens, closes):
    base_ref, place_ref, here_ref, measured_ref, cols_ref, carried_before, carried_after = refs[:7]
    refs = refs[7:]
    sources = []
    for _ in spans_of:
        sources.append(refs[:2])
        refs = refs[2:]
    if not opens:
        refs = refs[4:]
    spectrum_ref, packed, moment, projected = refs[:4]
    refs = refs[4:]
    if closes:
        terms_refs = refs[:3]
        refs = refs[3:]
    table, modelled, pairs, weights, sems = refs
    levels = here_ref.shape[0]
    rays = measured_ref.shape[0]
    high = 3 * levels
    begin = spans_of[0][0]
    end = spans_of[-1][0] + spans_of[-1][1]
    spans, pair_count = pair_rows(levels)
    cols = [ref.astype(jnp.float32) for ref in (carried_before[:, carrier:], cols_ref[...], carried_after[:, carrier:])]
    rows = jnp.concatenate([c.T for c in cols], axis=1).astype(jnp.bfloat16)

    if opens:
        moment[...] = jnp.zeros_like(moment)
        projected[...] = jnp.zeros_like(projected)
        packed[0] = jnp.zeros(packed.shape[1:], packed.dtype)

    copies = []
    for (first, width), (before_ref, after_ref) in zip(spans_of, sources, strict=True):
        for low_lane in range(0, width, PIECE):
            size = min(PIECE, width - low_lane)
            local = slice(low_lane, low_lane + size)
            overall = slice(first + low_lane, first + low_lane + size)
            table[0:levels, :size] = before_ref[:, local]
            table[levels : 2 * levels, :size] = here_ref[:, overall]
            table[2 * levels : high, :size] = after_ref[:, local]
            depth = jnp.dot(rows, table[:high, :size], preferred_element_type=jnp.float32)
            spectrum = jnp.exp(-depth)
            inside = slice(first + low_lane - begin, first + low_lane - begin + size)
            modelled[:, inside] = spectrum
            copy = pltpu.make_async_copy(modelled.at[:, inside], spectrum_ref.at[:, overall], sems.at[len(copies)])
            copy.start()
            copies.append(copy)
            table[high:, :size] = (spectrum * spectrum).astype(jnp.bfloat16)
            groups = range(overall.start // LANES, overall.stop // LANES)
            places = [place_ref[g : g + 1, :] for g in groups]
            kept = jnp.concatenate(places, axis=1) >= 0
            error = jnp.where(kept, (measured_ref[:, overall] - spectrum) * spectrum, 0.0).astype(jnp.bfloat16)
            projected[...] += nt_dot(table[:high, :size], error)
            for n, (g, place) in enumerate(zip(groups, places, strict=True)):
                at = base_ref[g, 0] // LANES
                chosen = (iota((2 * LANES, LANES), 0) + at * LANES == place).astype(jnp.bfloat16)
                moved = nt_dot(table[:, n * LANES : (n + 1) * LANES], chosen).astype(jnp.bfloat16)
                packed[at] = packed[at] + moved[:, :LANES]
                packed[at + 1] = moved[:, LANES:]

    def one_block(block, parts):
        wide = parts * LANES
        for p in range(parts):
            lane = slice(p * LANES, (p + 1) * LANES)
            weights[:, lane] = packed[block + p, high:, :]
            for k in range(3):
                level_rows = packed[block + p, k * levels : (k + 1) * levels, :]
                for m, low, offset, count in spans:
                    pairs[k, offset : offset + count, lane] = level_rows[low:, :] * level_rows[m : m + 1, :]
        for k in range(3):
            moment[k] += nt_dot(pairs[k, :, :wide], weights[:, :wide])

    parts = BLOCK // LANES
    done = base_ref[begin // LANES, 0] // BLOCK
    count = base_ref[end // LANES, 0]
    ready = count // BLOCK
    lax.fori_loop(done, ready, lambda block, carry: (one_block(block * parts, parts), carry)[1], 0)

    if closes:
        last = base_ref[end // LANES - 1, 0] // LANES
        for d in range(2, parts + 1):
            packed[last + d] = jnp.zeros(packed.shape[1:], packed.dtype)
        left = count - ready * BLOCK

        @pl.when(left > BLOCK // 2)
        def _():
            one_block(ready * parts, parts)

        @pl.when((left > 0) & (left <= BLOCK // 2))
        def _():
            one_block(ready * parts, parts // 2)

        lane = iota((levels, LANES), 1)
        for k in range(3):
            gradient = jnp.sum(cols[k] * projected[k * levels : (k + 1) * levels, :], axis=1, keepdims=True)
            result = jnp.where(lane == levels, gradient, 0.0)
            for m, low, offset, count in spans:
                column = jnp.sum(
                    moment[k, offset : offset + count, :] * (cols[k][low:, :] * cols[k][m : m + 1, :]),
                    axis=1,
                    keepdims=True,
                )
                if low:
                    column = jnp.concatenate([jnp.zeros((low, 1), jnp.float32), column], axis=0)
                result = jnp.where(lane == m, column, result)
            terms_refs[k][...] = result
    for copy in copies:
        copy.wait()


def chunk(base, place, here, measured, cols, carried, carrier, spans_of, sources, state, closes):
    levels, points = here.shape
    rays = measured.shape[0]
    _, pair_count = pair_rows(levels)
    opens = state is None
    smem = pl.BlockSpec(memory_space=pltpu.SMEM)
    vmem = pl.BlockSpec(memory_space=pltpu.VMEM)
    hbm = pl.BlockSpec(memory_space=pltpu.HBM)
    width = sum(w for _, w in spans_of)
    args = [base, place, here, measured, cols, *carried]
    specs = [smem] + [vmem] * 6
    for pair in sources:
        args += pair
        specs += [vmem, vmem]
    aliases = {}
    if not opens:
        aliases = {len(args) + n: n for n in range(4)}
        args += state
        specs += [hbm, vmem, vmem, vmem]
    shapes = [
        jax.ShapeDtypeStruct(measured.shape, jnp.float32),
        jax.ShapeDtypeStruct(((points + BLOCK) // LANES + 2, 3 * levels + rays, LANES), jnp.bfloat16),
        jax.ShapeDtypeStruct((3, pair_count, rays), jnp.float32),
        jax.ShapeDtypeStruct((3 * levels, rays), jnp.float32),
    ]
    out_specs = [hbm, vmem, vmem, vmem]
    if closes:
        shapes += [jax.ShapeDtypeStruct((levels, LANES), jnp.float32)] * 3
        out_specs += [vmem] * 3
    outs = pl.pallas_call(
        functools.partial(chunk_kernel, spans_of=spans_of, carrier=carrier, opens=opens, closes=closes),
        in_specs=specs,
        out_specs=out_specs,
        out_shape=shapes,
        scratch_shapes=[
            pltpu.VMEM((3 * levels + rays, PIECE), jnp.bfloat16),
            pltpu.VMEM((rays, width), jnp.float32),
            pltpu.VMEM((3, pair_count, BLOCK), jnp.bfloat16),
            pltpu.VMEM((rays, BLOCK), jnp.bfloat16),
            pltpu.SemaphoreType.DMA((sum(pl.cdiv(w, PIECE) for _, w in spans_of),)),
        ],
        input_output_aliases=aliases,
        compiler_params=pltpu.CompilerParams(vmem_limit_bytes=CHUNK_BYTES),
        cost_estimate=CHEAP,
        name="chunk",
    )(*args)
    return outs[:4], outs[4:]


def solve_kernel(*refs, scale):
    parts = refs[:6]
    prior_ref, out_ref = refs[6:]
    levels = prior_ref.shape[1]
    total = parts[0][...]
    for part in parts[1:]:
        total = total + part[...]
    terms = total * scale
    row = iota((levels, LANES), 0)
    lane = iota((levels, LANES), 1)
    square = terms[:, :levels]
    flipped = jnp.concatenate([square.T, jnp.zeros((levels, LANES - levels), jnp.float32)], axis=1)
    lower = row // ROWS >= lane // ROWS
    work = jnp.where(lower | (lane >= levels), terms, flipped)
    diagonal = jnp.sum(jnp.where(row == lane, work, 0.0), axis=1, keepdims=True)
    mean = jnp.sum(diagonal, axis=0, keepdims=True) * (1.0 / levels) + 1e-06
    eye = iota((levels, levels), 0) == iota((levels, levels), 1)
    prior = jnp.sum(jnp.where(eye, prior_ref[...], 0.0), axis=1, keepdims=True)
    work = work + jnp.where(row == lane, prior * mean, 0.0)
    for i in range(levels):
        pivot_row = work[i : i + 1, :]
        scaled = pivot_row * (1.0 / pivot_row[:, i : i + 1])
        column = work[:, i : i + 1]
        factor = jnp.where(row[:, :1] == i, column - 1.0, column)
        work = work - factor * scaled
    column = work[:, levels : levels + 1]
    out_ref[...] = -jnp.sum(jnp.where(eye, column, 0.0), axis=0, keepdims=True)


def solve(parts, prior_weight, scale):
    return pl.pallas_call(
        functools.partial(solve_kernel, scale=scale),
        out_shape=jax.ShapeDtypeStruct((1, prior_weight.shape[1]), jnp.float32),
        compiler_params=pltpu.CompilerParams(vmem_limit_bytes=SMALL_BYTES),
        cost_estimate=CHEAP,
        name="solve",
    )(*parts, prior_weight)


def swapped(block, axis):
    size = lax.axis_size(axis)
    return lax.ppermute(block, axis, [(i, size - 1 - i) for i in range(size)])


def shards(absorption, absorber, seg_level, seg_count, seg_length, measured, window_mask, prior_weight):
    table = absorption[0]
    levels, points = table.shape
    rays = measured.shape[1]
    unit = points // sum(WIDTHS)
    widths = [w * unit for w in WIDTHS]
    firsts = [sum(widths[:c]) for c in range(len(widths))]
    mask = window_mask.reshape(points // LANES, LANES)
    level = jnp.swapaxes(seg_level[0], 1, 2)
    length = jnp.swapaxes(seg_length[0], 1, 2)
    count = seg_count.reshape(3, 1, rays)
    upward, downward, cols, place, base = prepare(
        level, count, length, absorber, mask, table, firsts[CARRIER], widths[CARRIER]
    )
    base = base[:, :1]
    below = []
    above = []
    for c, (first, width) in enumerate(zip(firsts, widths, strict=True)):
        piece = table[:, first : first + width]
        below.append(passed_along(upward if c == CARRIER else piece, "sector", 1))
        above.append(passed_along(downward if c == CARRIER else piece, "sector", -1))
    state = None
    carried = (below[CARRIER], above[CARRIER])
    for n, group in enumerate(GROUPS):
        spans_of = tuple((firsts[c], widths[c]) for c in group)
        sources = [(below[c], above[c]) for c in group]
        closes = n == len(GROUPS) - 1
        state, terms = chunk(
            base, place, table, measured[0], cols, carried, widths[CARRIER], spans_of, sources, state, closes
        )
    spectrum = state[0]
    mine = (terms[1], passed_along(terms[0], "sector", -1), passed_along(terms[2], "sector", 1))
    others = tuple(swapped(part, "spec") for part in mine)
    scale = 1.0 / (rays * points * lax.axis_size("spec"))
    state_step = solve(mine + others, prior_weight[None, :], scale)
    return (spectrum[None], state_step)


def solution(mesh):
    return jax.shard_map(
        shards,
        mesh=mesh,
        in_specs=(
            P(("orbits", "sector"), None, "spec"),
            P(("orbits", "sector"), None),
            P(("orbits", "sector"), None, None, None),
            P(("orbits", "sector"), None, None),
            P(("orbits", "sector"), None, None, None),
            P(("orbits", "sector"), None, "spec"),
            P("spec"),
            P(),
        ),
        out_specs=(P(("orbits", "sector"), None, "spec"), P(("orbits", "sector"), None)),
        check_vma=False,
    )
```

```python
import functools

import jax
import jax.numpy as jnp
from jax import lax
from jax.experimental import pallas as pl
from jax.experimental.pallas import tpu as pltpu
from jax.sharding import PartitionSpec as P

LANES = 128
ROWS = 16
PIECE = 512
BLOCK = 512
WIDTHS = (20, 12)
GROUPS = ((0,), (1,))
CARRIER = 0
SMALL_BYTES = 4 << 20
CHUNK_BYTES = 16 << 20
CHEAP = pl.CostEstimate(flops=1, transcendentals=0, bytes_accessed=1)


def passed_along(block, axis, distance):
    devices = range(lax.axis_size(axis))
    route = [((i - distance) % len(devices), i) for i in devices]
    return lax.ppermute(block, axis, route)


def iota(shape, dim):
    return lax.broadcasted_iota(jnp.int32, shape, dim)


def nt_dot(a, b):
    return lax.dot_general(a, b, (((1,), (1,)), ((), ())), preferred_element_type=jnp.float32)


def pinned(*arrays):
    return [pltpu.with_memory_space_constraint(array, pltpu.HBM) for array in arrays]


def prepare_kernel(level_hbm, count_hbm, length_hbm, absorber_hbm, table_hbm, *outs, first, width):
    up_ref, down_ref, cols_ref, level_ref, count_ref, length_ref, absorber_ref, sems = outs
    levels = absorber_ref.shape[1]
    sets, segs, rays = level_ref.shape
    arguments = ((level_hbm, level_ref), (length_hbm, length_ref), (count_hbm, count_ref), (absorber_hbm, absorber_ref))
    copies = [pltpu.make_async_copy(a, b, sems.at[n]) for n, (a, b) in enumerate(arguments)]
    for n, ref in enumerate((up_ref, down_ref)):
        source = table_hbm.at[:, pl.ds(first, width)]
        copies.append(pltpu.make_async_copy(source, ref.at[:, pl.ds(0, width)], sems.at[len(arguments) + n]))
    for copy in copies:
        copy.start()
    for copy in copies[: len(arguments)]:
        copy.wait()
    eye = iota((levels, levels), 0) == iota((levels, levels), 1)
    amount = jnp.sum(jnp.where(eye, absorber_ref[...], 0.0), axis=1, keepdims=True)
    level_of = iota((levels, rays), 0)
    for k in range(sets):
        length = jnp.where(iota((segs, rays), 0) < count_ref[k], length_ref[k], 0.0)
        level = level_ref[k]
        path = jnp.zeros((levels, rays), jnp.float32)
        for j in range(segs):
            path += jnp.where(level[j : j + 1, :] == level_of, length[j : j + 1, :], 0.0)
        absorbed = (path * amount).astype(jnp.bfloat16)
        if k == 0:
            down_ref[:, width:] = absorbed
        elif k == 1:
            cols_ref[...] = absorbed
        else:
            up_ref[:, width:] = absorbed
    for copy in copies[len(arguments) :]:
        copy.wait()


def prepare(level, count, length, absorber, table, first, width):
    rays = level.shape[2]
    levels = absorber.shape[1]
    send = jax.ShapeDtypeStruct((levels, width + rays), jnp.bfloat16)
    hbm = pl.BlockSpec(memory_space=pltpu.HBM)
    return pl.pallas_call(
        functools.partial(prepare_kernel, first=first, width=width),
        in_specs=[hbm] * 5,
        out_shape=(send, send, jax.ShapeDtypeStruct((levels, rays), jnp.bfloat16)),
        scratch_shapes=[
            pltpu.VMEM(level.shape, level.dtype),
            pltpu.VMEM(count.shape, count.dtype),
            pltpu.VMEM(length.shape, length.dtype),
            pltpu.VMEM(absorber.shape, absorber.dtype),
            pltpu.SemaphoreType.DMA((6,)),
        ],
        compiler_params=pltpu.CompilerParams(vmem_limit_bytes=SMALL_BYTES),
        cost_estimate=CHEAP,
        name="prepare",
    )(*pinned(level, count, length, absorber, table))


def stage_kernel(cols_ref, mask_hbm, table_hbm, measured_hbm, place_ref, base_ref, table_ref, measured_ref, mask_ref, sems):
    del cols_ref
    moves = ((mask_hbm, mask_ref), (table_hbm, table_ref), (measured_hbm, measured_ref))
    copies = [pltpu.make_async_copy(a, b, sems.at[n]) for n, (a, b) in enumerate(moves)]
    for copy in copies:
        copy.start()
    copies[0].wait()
    groups = mask_ref.shape[0]
    mask = mask_ref[...].astype(jnp.bfloat16)
    before = (iota((LANES, LANES), 0) < iota((LANES, LANES), 1)).astype(jnp.bfloat16)
    rank = jnp.dot(mask, before, preferred_element_type=jnp.float32)
    total = jnp.dot(mask, jnp.ones((LANES, LANES), jnp.bfloat16), preferred_element_type=jnp.float32)
    earlier = (iota((groups, groups), 1) < iota((groups, groups), 0)).astype(jnp.bfloat16)
    base = jnp.dot(earlier, total.astype(jnp.bfloat16), preferred_element_type=jnp.float32)
    place_ref[...] = jnp.where(mask_ref[...] > 0, (base + rank).astype(jnp.int32), -1)
    base_ref[pl.ds(0, groups), :] = base.astype(jnp.int32)
    last = base[groups - 1 : groups, :] + total[groups - 1 : groups, :]
    base_ref[pl.ds(groups, 8), :] = jnp.broadcast_to(last, (8, LANES)).astype(jnp.int32)
    for copy in copies[1:]:
        copy.wait()


def stage(cols, mask, table, measured):
    groups = mask.shape[0]
    vmem = pl.BlockSpec(memory_space=pltpu.VMEM)
    hbm = pl.BlockSpec(memory_space=pltpu.HBM)
    return pl.pallas_call(
        stage_kernel,
        in_specs=[vmem, hbm, hbm, hbm],
        out_shape=(
            jax.ShapeDtypeStruct((groups, LANES), jnp.int32),
            jax.ShapeDtypeStruct((groups + 8, LANES), jnp.int32),
            jax.ShapeDtypeStruct(table.shape, table.dtype),
            jax.ShapeDtypeStruct(measured.shape, measured.dtype),
        ),
        scratch_shapes=[pltpu.VMEM(mask.shape, mask.dtype), pltpu.SemaphoreType.DMA((3,))],
        compiler_params=pltpu.CompilerParams(vmem_limit_bytes=SMALL_BYTES),
        cost_estimate=CHEAP,
        name="stage",
    )(cols, *pinned(mask, table, measured))


def pair_rows(levels):
    spans = []
    offset = 0
    for m in range(levels):
        first = ROWS * (m // ROWS)
        spans.append((m, first, offset, levels - first))
        offset += levels - first
    return spans, offset


def chunk_kernel(*refs, spans_of, carrier, opens, closes):
    base_ref, place_ref, here_ref, measured_ref, cols_ref, carried_before, carried_after = refs[:7]
    refs = refs[7:]
    sources = []
    for _ in spans_of:
        sources.append(refs[:2])
        refs = refs[2:]
    if not opens:
        refs = refs[4:]
    spectrum_ref, packed, moment, projected = refs[:4]
    refs = refs[4:]
    if closes:
        terms_refs = refs[:3]
        refs = refs[3:]
    table, modelled, pairs, weights, sems = refs
    levels = here_ref.shape[0]
    rays = measured_ref.shape[0]
    high = 3 * levels
    begin = spans_of[0][0]
    end = spans_of[-1][0] + spans_of[-1][1]
    spans, pair_count = pair_rows(levels)
    cols = [ref.astype(jnp.float32) for ref in (carried_before[:, carrier:], cols_ref[...], carried_after[:, carrier:])]
    rows = jnp.concatenate([c.T for c in cols], axis=1).astype(jnp.bfloat16)

    if opens:
        moment[...] = jnp.zeros_like(moment)
        projected[...] = jnp.zeros_like(projected)
        packed[0] = jnp.zeros(packed.shape[1:], packed.dtype)

    copies = []
    for (first, width), (before_ref, after_ref) in zip(spans_of, sources, strict=True):
        for low_lane in range(0, width, PIECE):
            size = min(PIECE, width - low_lane)
            local = slice(low_lane, low_lane + size)
            overall = slice(first + low_lane, first + low_lane + size)
            table[0:levels, :size] = before_ref[:, local]
            table[levels : 2 * levels, :size] = here_ref[:, overall]
            table[2 * levels : high, :size] = after_ref[:, local]
            depth = jnp.dot(rows, table[:high, :size], preferred_element_type=jnp.float32)
            spectrum = jnp.exp(-depth)
            inside = slice(first + low_lane - begin, first + low_lane - begin + size)
            modelled[:, inside] = spectrum
            copy = pltpu.make_async_copy(modelled.at[:, inside], spectrum_ref.at[:, overall], sems.at[len(copies)])
            copy.start()
            copies.append(copy)
            table[high:, :size] = (spectrum * spectrum).astype(jnp.bfloat16)
            groups = range(overall.start // LANES, overall.stop // LANES)
            places = [place_ref[g : g + 1, :] for g in groups]
            kept = jnp.concatenate(places, axis=1) >= 0
            error = jnp.where(kept, (measured_ref[:, overall] - spectrum) * spectrum, 0.0).astype(jnp.bfloat16)
            projected[...] += nt_dot(table[:high, :size], error)
            for n, (g, place) in enumerate(zip(groups, places, strict=True)):
                at = base_ref[g, 0] // LANES
                chosen = (iota((2 * LANES, LANES), 0) + at * LANES == place).astype(jnp.bfloat16)
                moved = nt_dot(table[:, n * LANES : (n + 1) * LANES], chosen).astype(jnp.bfloat16)
                packed[at] = packed[at] + moved[:, :LANES]
                packed[at + 1] = moved[:, LANES:]

    def one_block(block, parts):
        wide = parts * LANES
        for p in range(parts):
            lane = slice(p * LANES, (p + 1) * LANES)
            weights[:, lane] = packed[block + p, high:, :]
            for k in range(3):
                level_rows = packed[block + p, k * levels : (k + 1) * levels, :]
                for m, low, offset, count in spans:
                    pairs[k, offset : offset + count, lane] = level_rows[low:, :] * level_rows[m : m + 1, :]
        for k in range(3):
            moment[k] += nt_dot(pairs[k, :, :wide], weights[:, :wide])

    parts = BLOCK // LANES
    done = base_ref[begin // LANES, 0] // BLOCK
    count = base_ref[end // LANES, 0]
    ready = count // BLOCK
    lax.fori_loop(done, ready, lambda block, carry: (one_block(block * parts, parts), carry)[1], 0)

    if closes:
        last = base_ref[end // LANES - 1, 0] // LANES
        for d in range(2, parts + 1):
            packed[last + d] = jnp.zeros(packed.shape[1:], packed.dtype)
        left = count - ready * BLOCK

        @pl.when(left > BLOCK // 2)
        def _():
            one_block(ready * parts, parts)

        @pl.when((left > 0) & (left <= BLOCK // 2))
        def _():
            one_block(ready * parts, parts // 2)

        lane = iota((levels, LANES), 1)
        for k in range(3):
            gradient = jnp.sum(cols[k] * projected[k * levels : (k + 1) * levels, :], axis=1, keepdims=True)
            result = jnp.where(lane == levels, gradient, 0.0)
            for m, low, offset, count in spans:
                column = jnp.sum(
                    moment[k, offset : offset + count, :] * (cols[k][low:, :] * cols[k][m : m + 1, :]),
                    axis=1,
                    keepdims=True,
                )
                if low:
                    column = jnp.concatenate([jnp.zeros((low, 1), jnp.float32), column], axis=0)
                result = jnp.where(lane == m, column, result)
            terms_refs[k][...] = result
    for copy in copies:
        copy.wait()


def chunk(base, place, here, measured, cols, carried, carrier, spans_of, sources, state, closes):
    levels, points = here.shape
    rays = measured.shape[0]
    _, pair_count = pair_rows(levels)
    opens = state is None
    smem = pl.BlockSpec(memory_space=pltpu.SMEM)
    vmem = pl.BlockSpec(memory_space=pltpu.VMEM)
    hbm = pl.BlockSpec(memory_space=pltpu.HBM)
    width = sum(w for _, w in spans_of)
    args = [base, place, here, measured, cols, *carried]
    specs = [smem] + [vmem] * 6
    for pair in sources:
        args += pair
        specs += [vmem, vmem]
    aliases = {}
    if not opens:
        aliases = {len(args) + n: n for n in range(4)}
        args += state
        specs += [hbm, vmem, vmem, vmem]
    shapes = [
        jax.ShapeDtypeStruct(measured.shape, jnp.float32),
        jax.ShapeDtypeStruct(((points + BLOCK) // LANES + 2, 3 * levels + rays, LANES), jnp.bfloat16),
        jax.ShapeDtypeStruct((3, pair_count, rays), jnp.float32),
        jax.ShapeDtypeStruct((3 * levels, rays), jnp.float32),
    ]
    out_specs = [hbm, vmem, vmem, vmem]
    if closes:
        shapes += [jax.ShapeDtypeStruct((levels, LANES), jnp.float32)] * 3
        out_specs += [vmem] * 3
    outs = pl.pallas_call(
        functools.partial(chunk_kernel, spans_of=spans_of, carrier=carrier, opens=opens, closes=closes),
        in_specs=specs,
        out_specs=out_specs,
        out_shape=shapes,
        scratch_shapes=[
            pltpu.VMEM((3 * levels + rays, PIECE), jnp.bfloat16),
            pltpu.VMEM((rays, width), jnp.float32),
            pltpu.VMEM((3, pair_count, BLOCK), jnp.bfloat16),
            pltpu.VMEM((rays, BLOCK), jnp.bfloat16),
            pltpu.SemaphoreType.DMA((sum(pl.cdiv(w, PIECE) for _, w in spans_of),)),
        ],
        input_output_aliases=aliases,
        compiler_params=pltpu.CompilerParams(vmem_limit_bytes=CHUNK_BYTES),
        cost_estimate=CHEAP,
        name="chunk",
    )(*args)
    return outs[:4], outs[4:]


def quad_step(work, row, p):
    r = [work[p + i : p + i + 1, :] for i in range(4)]

    def entry(i, j):
        return jnp.broadcast_to(r[i][:, p + j : p + j + 1], r[i].shape)

    a, b, d = entry(0, 0), entry(0, 1), entry(1, 1)
    f0, f1, g0, g1 = entry(0, 2), entry(0, 3), entry(1, 2), entry(1, 3)
    h, q, v = entry(2, 2), entry(2, 3), entry(3, 3)
    inverse = 1.0 / (a * d - b * b)
    a, b, d = d * inverse, -b * inverse, a * inverse
    w00, w01 = a * f0 + b * g0, a * f1 + b * g1
    w10, w11 = b * f0 + d * g0, b * f1 + d * g1
    h, q, v = h - (f0 * w00 + g0 * w10), q - (f0 * w01 + g0 * w11), v - (f1 * w01 + g1 * w11)
    inverse = 1.0 / (h * v - q * q)
    h, q, v = v * inverse, -q * inverse, h * inverse
    t0, t1 = a * r[0] + b * r[1], b * r[0] + d * r[1]
    u0, u1 = r[2] - (f0 * t0 + g0 * t1), r[3] - (f1 * t0 + g1 * t1)
    s2, s3 = h * u0 + q * u1, q * u0 + v * u1
    s0, s1 = t0 - (w00 * s2 + w01 * s3), t1 - (w10 * s2 + w11 * s3)
    update = None
    for i, s in enumerate((s0, s1, s2, s3)):
        column = work[:, p + i : p + i + 1]
        term = jnp.where(row[:, :1] == p + i, column - 1.0, column) * s
        update = term if update is None else update + term
    return work - update


def solve_kernel(*refs, scale):
    parts = refs[:6]
    prior_ref, out_ref = refs[6:]
    levels = prior_ref.shape[1]
    total = parts[0][...]
    for part in parts[1:]:
        total = total + part[...]
    terms = total * scale
    row = iota((levels, LANES), 0)
    lane = iota((levels, LANES), 1)
    square = terms[:, :levels]
    flipped = jnp.concatenate([square.T, jnp.zeros((levels, LANES - levels), jnp.float32)], axis=1)
    lower = row // ROWS >= lane // ROWS
    work = jnp.where(lower | (lane >= levels), terms, flipped)
    diagonal = jnp.sum(jnp.where(row == lane, work, 0.0), axis=1, keepdims=True)
    mean = jnp.sum(diagonal, axis=0, keepdims=True) * (1.0 / levels) + 1e-06
    eye = iota((levels, levels), 0) == iota((levels, levels), 1)
    prior = jnp.sum(jnp.where(eye, prior_ref[...], 0.0), axis=1, keepdims=True)
    work = work + jnp.where(row == lane, prior * mean, 0.0)
    for p in range(0, levels, 4):
        work = quad_step(work, row, p)
    column = work[:, levels : levels + 1]
    out_ref[...] = -jnp.sum(jnp.where(eye, column, 0.0), axis=0, keepdims=True)


def solve(parts, prior_weight, scale):
    return pl.pallas_call(
        functools.partial(solve_kernel, scale=scale),
        out_shape=jax.ShapeDtypeStruct((1, prior_weight.shape[1]), jnp.float32),
        compiler_params=pltpu.CompilerParams(vmem_limit_bytes=SMALL_BYTES),
        cost_estimate=CHEAP,
        name="solve",
    )(*parts, prior_weight)


def swapped(block, axis):
    size = lax.axis_size(axis)
    return lax.ppermute(block, axis, [(i, size - 1 - i) for i in range(size)])


def shards(absorption, absorber, seg_level, seg_count, seg_length, measured, window_mask, prior_weight):
    table = absorption[0]
    levels, points = table.shape
    rays = measured.shape[1]
    unit = points // sum(WIDTHS)
    widths = [w * unit for w in WIDTHS]
    firsts = [sum(widths[:c]) for c in range(len(widths))]
    mask = window_mask.reshape(points // LANES, LANES)
    level = jnp.swapaxes(seg_level[0], 1, 2)
    length = jnp.swapaxes(seg_length[0], 1, 2)
    count = seg_count.reshape(3, 1, rays)
    upward, downward, cols = prepare(level, count, length, absorber, table, firsts[CARRIER], widths[CARRIER])
    place, base, table_here, measured_here = stage(cols, mask, table, measured[0])
    base = base[:, :1]
    below = []
    above = []
    for c, (first, width) in enumerate(zip(firsts, widths, strict=True)):
        piece = table[:, first : first + width]
        below.append(passed_along(upward if c == CARRIER else piece, "sector", 1))
        above.append(passed_along(downward if c == CARRIER else piece, "sector", -1))
    state = None
    carried = (below[CARRIER], above[CARRIER])
    for n, group in enumerate(GROUPS):
        spans_of = tuple((firsts[c], widths[c]) for c in group)
        sources = [(below[c], above[c]) for c in group]
        closes = n == len(GROUPS) - 1
        state, terms = chunk(
            base, place, table_here, measured_here, cols, carried, widths[CARRIER], spans_of, sources, state, closes
        )
    spectrum = state[0]
    mine = (terms[1], passed_along(terms[0], "sector", -1), passed_along(terms[2], "sector", 1))
    others = tuple(swapped(part, "spec") for part in mine)
    scale = 1.0 / (rays * points * lax.axis_size("spec"))
    state_step = solve(mine + others, prior_weight[None, :], scale)
    return (spectrum[None], state_step)


def solution(mesh):
    return jax.shard_map(
        shards,
        mesh=mesh,
        in_specs=(
            P(("orbits", "sector"), None, "spec"),
            P(("orbits", "sector"), None),
            P(("orbits", "sector"), None, None, None),
            P(("orbits", "sector"), None, None),
            P(("orbits", "sector"), None, None, None),
            P(("orbits", "sector"), None, "spec"),
            P("spec"),
            P(),
        ),
        out_specs=(P(("orbits", "sector"), None, "spec"), P(("orbits", "sector"), None)),
        check_vma=False,
    )
```

```python
import functools

import jax
import jax.numpy as jnp
from jax import lax
from jax.experimental import pallas as pl
from jax.experimental.pallas import tpu as pltpu
from jax.sharding import PartitionSpec as P

LANES = 128
ROWS = 16
PIECE = 512
BLOCK = 512
WIDTHS = (14, 12, 6)
GROUPS = ((0,), (1,), (2,))
CARRIER = 0
SMALL_BYTES = 4 << 20
CHUNK_BYTES = 16 << 20
CHEAP = pl.CostEstimate(flops=1, transcendentals=0, bytes_accessed=1)


def traded(block, axis, side):
    size = lax.axis_size(axis)
    steps = [1 if (i + side) % 2 == 0 else -1 for i in range(size)]
    return lax.ppermute(block, axis, [(i, (i + step) % size) for i, step in enumerate(steps)])


def iota(shape, dim):
    return lax.broadcasted_iota(jnp.int32, shape, dim)


def nt_dot(a, b):
    return lax.dot_general(a, b, (((1,), (1,)), ((), ())), preferred_element_type=jnp.float32)


def pinned(*arrays):
    return [pltpu.with_memory_space_constraint(array, pltpu.HBM) for array in arrays]


def prepare_kernel(level_hbm, count_hbm, length_hbm, absorber_hbm, table_hbm, *outs, first, width):
    first_ref, second_ref, cols_ref, level_ref, count_ref, length_ref, absorber_ref, sems = outs
    levels = absorber_ref.shape[1]
    sets, segs, rays = level_ref.shape
    arguments = ((level_hbm, level_ref), (length_hbm, length_ref), (count_hbm, count_ref), (absorber_hbm, absorber_ref))
    copies = [pltpu.make_async_copy(a, b, sems.at[n]) for n, (a, b) in enumerate(arguments)]
    for n, ref in enumerate((first_ref, second_ref)):
        source = table_hbm.at[:, pl.ds(first, width)]
        copies.append(pltpu.make_async_copy(source, ref.at[:, pl.ds(0, width)], sems.at[len(arguments) + n]))
    for copy in copies:
        copy.start()
    for copy in copies[: len(arguments)]:
        copy.wait()
    eye = iota((levels, levels), 0) == iota((levels, levels), 1)
    amount = jnp.sum(jnp.where(eye, absorber_ref[...], 0.0), axis=1, keepdims=True)
    level_of = iota((levels, rays), 0)
    odd = lax.axis_index("sector") % 2
    absorbed = []
    for k in range(sets):
        length = jnp.where(iota((segs, rays), 0) < count_ref[k], length_ref[k], 0.0)
        level = level_ref[k]
        path = jnp.zeros((levels, rays), jnp.float32)
        for j in range(segs):
            path += jnp.where(level[j : j + 1, :] == level_of, length[j : j + 1, :], 0.0)
        absorbed.append(path * amount)
    low, here, high = absorbed
    cols_ref[...] = here.astype(jnp.bfloat16)
    first_ref[:, width:] = jnp.where(odd == 1, low, high).astype(jnp.bfloat16)
    second_ref[:, width:] = jnp.where(odd == 1, high, low).astype(jnp.bfloat16)
    for copy in copies[len(arguments) :]:
        copy.wait()


def prepare(level, count, length, absorber, table, first, width):
    rays = level.shape[2]
    levels = absorber.shape[1]
    send = jax.ShapeDtypeStruct((levels, width + rays), jnp.bfloat16)
    hbm = pl.BlockSpec(memory_space=pltpu.HBM)
    return pl.pallas_call(
        functools.partial(prepare_kernel, first=first, width=width),
        in_specs=[hbm] * 5,
        out_shape=(send, send, jax.ShapeDtypeStruct((levels, rays), jnp.bfloat16)),
        scratch_shapes=[
            pltpu.VMEM(level.shape, level.dtype),
            pltpu.VMEM(count.shape, count.dtype),
            pltpu.VMEM(length.shape, length.dtype),
            pltpu.VMEM(absorber.shape, absorber.dtype),
            pltpu.SemaphoreType.DMA((6,)),
        ],
        compiler_params=pltpu.CompilerParams(vmem_limit_bytes=SMALL_BYTES),
        cost_estimate=CHEAP,
        name="prepare",
    )(*pinned(level, count, length, absorber, table))


def stage_kernel(cols_ref, mask_hbm, table_hbm, measured_hbm, place_ref, base_ref, table_ref, measured_ref, mask_ref, sems):
    del cols_ref
    moves = ((mask_hbm, mask_ref), (table_hbm, table_ref), (measured_hbm, measured_ref))
    copies = [pltpu.make_async_copy(a, b, sems.at[n]) for n, (a, b) in enumerate(moves)]
    for copy in copies:
        copy.start()
    copies[0].wait()
    groups = mask_ref.shape[0]
    mask = mask_ref[...].astype(jnp.bfloat16)
    before = (iota((LANES, LANES), 0) < iota((LANES, LANES), 1)).astype(jnp.bfloat16)
    rank = jnp.dot(mask, before, preferred_element_type=jnp.float32)
    total = jnp.dot(mask, jnp.ones((LANES, LANES), jnp.bfloat16), preferred_element_type=jnp.float32)
    earlier = (iota((groups, groups), 1) < iota((groups, groups), 0)).astype(jnp.bfloat16)
    base = jnp.dot(earlier, total.astype(jnp.bfloat16), preferred_element_type=jnp.float32)
    place_ref[...] = jnp.where(mask_ref[...] > 0, (base + rank).astype(jnp.int32), -1)
    base_ref[pl.ds(0, groups), :] = base.astype(jnp.int32)
    last = base[groups - 1 : groups, :] + total[groups - 1 : groups, :]
    base_ref[pl.ds(groups, 8), :] = jnp.broadcast_to(last, (8, LANES)).astype(jnp.int32)
    for copy in copies[1:]:
        copy.wait()


def stage(cols, mask, table, measured):
    groups = mask.shape[0]
    vmem = pl.BlockSpec(memory_space=pltpu.VMEM)
    hbm = pl.BlockSpec(memory_space=pltpu.HBM)
    return pl.pallas_call(
        stage_kernel,
        in_specs=[vmem, hbm, hbm, hbm],
        out_shape=(
            jax.ShapeDtypeStruct((groups, LANES), jnp.int32),
            jax.ShapeDtypeStruct((groups + 8, LANES), jnp.int32),
            jax.ShapeDtypeStruct(table.shape, table.dtype),
            jax.ShapeDtypeStruct(measured.shape, measured.dtype),
        ),
        scratch_shapes=[pltpu.VMEM(mask.shape, mask.dtype), pltpu.SemaphoreType.DMA((3,))],
        compiler_params=pltpu.CompilerParams(vmem_limit_bytes=SMALL_BYTES),
        cost_estimate=CHEAP,
        name="stage",
    )(cols, *pinned(mask, table, measured))


def pair_rows(levels):
    spans = []
    offset = 0
    for m in range(levels):
        first = ROWS * (m // ROWS)
        spans.append((m, first, offset, levels - first))
        offset += levels - first
    return spans, offset


def chunk_kernel(*refs, spans_of, carrier, opens, closes):
    base_ref, place_ref, here_ref, measured_ref, cols_ref, carried_before, carried_after = refs[:7]
    refs = refs[7:]
    sources = []
    for _ in spans_of:
        sources.append(refs[:2])
        refs = refs[2:]
    if not opens:
        refs = refs[4:]
    spectrum_ref, packed, moment, projected = refs[:4]
    refs = refs[4:]
    if closes:
        terms_refs = refs[:3]
        refs = refs[3:]
    table, modelled, pairs, weights, sems = refs
    levels = here_ref.shape[0]
    rays = measured_ref.shape[0]
    high = 3 * levels
    begin = spans_of[0][0]
    end = spans_of[-1][0] + spans_of[-1][1]
    spans, pair_count = pair_rows(levels)
    cols = [ref.astype(jnp.float32) for ref in (carried_before[:, carrier:], cols_ref[...], carried_after[:, carrier:])]
    rows = jnp.concatenate([c.T for c in cols], axis=1).astype(jnp.bfloat16)

    if opens:
        moment[...] = jnp.zeros_like(moment)
        projected[...] = jnp.zeros_like(projected)
        packed[0] = jnp.zeros(packed.shape[1:], packed.dtype)

    copies = []
    for (first, width), (before_ref, after_ref) in zip(spans_of, sources, strict=True):
        for low_lane in range(0, width, PIECE):
            size = min(PIECE, width - low_lane)
            local = slice(low_lane, low_lane + size)
            overall = slice(first + low_lane, first + low_lane + size)
            table[0:levels, :size] = before_ref[:, local]
            table[levels : 2 * levels, :size] = here_ref[:, overall]
            table[2 * levels : high, :size] = after_ref[:, local]
            depth = jnp.dot(rows, table[:high, :size], preferred_element_type=jnp.float32)
            spectrum = jnp.exp(-depth)
            inside = slice(first + low_lane - begin, first + low_lane - begin + size)
            modelled[:, inside] = spectrum
            copy = pltpu.make_async_copy(modelled.at[:, inside], spectrum_ref.at[:, overall], sems.at[len(copies)])
            copy.start()
            copies.append(copy)
            table[high:, :size] = (spectrum * spectrum).astype(jnp.bfloat16)
            groups = range(overall.start // LANES, overall.stop // LANES)
            places = [place_ref[g : g + 1, :] for g in groups]
            kept = jnp.concatenate(places, axis=1) >= 0
            error = jnp.where(kept, (measured_ref[:, overall] - spectrum) * spectrum, 0.0).astype(jnp.bfloat16)
            projected[...] += nt_dot(table[:high, :size], error)
            for n, (g, place) in enumerate(zip(groups, places, strict=True)):
                at = base_ref[g, 0] // LANES
                chosen = (iota((2 * LANES, LANES), 0) + at * LANES == place).astype(jnp.bfloat16)
                moved = nt_dot(table[:, n * LANES : (n + 1) * LANES], chosen).astype(jnp.bfloat16)
                packed[at] = packed[at] + moved[:, :LANES]
                packed[at + 1] = moved[:, LANES:]

    def one_block(block, parts):
        wide = parts * LANES
        for p in range(parts):
            lane = slice(p * LANES, (p + 1) * LANES)
            weights[:, lane] = packed[block + p, high:, :]
            for k in range(3):
                level_rows = packed[block + p, k * levels : (k + 1) * levels, :]
                for m, low, offset, count in spans:
                    pairs[k, offset : offset + count, lane] = level_rows[low:, :] * level_rows[m : m + 1, :]
        for k in range(3):
            moment[k] += nt_dot(pairs[k, :, :wide], weights[:, :wide])

    parts = BLOCK // LANES
    done = base_ref[begin // LANES, 0] // BLOCK
    count = base_ref[end // LANES, 0]
    ready = count // BLOCK
    lax.fori_loop(done, ready, lambda block, carry: (one_block(block * parts, parts), carry)[1], 0)

    if closes:
        last = base_ref[end // LANES - 1, 0] // LANES
        for d in range(2, parts + 1):
            packed[last + d] = jnp.zeros(packed.shape[1:], packed.dtype)
        left = count - ready * BLOCK

        @pl.when(left > BLOCK // 2)
        def _():
            one_block(ready * parts, parts)

        @pl.when((left > 0) & (left <= BLOCK // 2))
        def _():
            one_block(ready * parts, parts // 2)

        lane = iota((levels, LANES), 1)
        for k in range(3):
            gradient = jnp.sum(cols[k] * projected[k * levels : (k + 1) * levels, :], axis=1, keepdims=True)
            result = jnp.where(lane == levels, gradient, 0.0)
            for m, low, offset, count in spans:
                column = jnp.sum(
                    moment[k, offset : offset + count, :] * (cols[k][low:, :] * cols[k][m : m + 1, :]),
                    axis=1,
                    keepdims=True,
                )
                if low:
                    column = jnp.concatenate([jnp.zeros((low, 1), jnp.float32), column], axis=0)
                result = jnp.where(lane == m, column, result)
            terms_refs[k][...] = result
    for copy in copies:
        copy.wait()


def chunk(base, place, here, measured, cols, carried, carrier, spans_of, sources, state, closes):
    levels, points = here.shape
    rays = measured.shape[0]
    _, pair_count = pair_rows(levels)
    opens = state is None
    smem = pl.BlockSpec(memory_space=pltpu.SMEM)
    vmem = pl.BlockSpec(memory_space=pltpu.VMEM)
    hbm = pl.BlockSpec(memory_space=pltpu.HBM)
    width = sum(w for _, w in spans_of)
    args = [base, place, here, measured, cols, *carried]
    specs = [smem] + [vmem] * 6
    for pair in sources:
        args += pair
        specs += [vmem, vmem]
    aliases = {}
    if not opens:
        aliases = {len(args) + n: n for n in range(4)}
        args += state
        specs += [hbm, vmem, vmem, vmem]
    shapes = [
        jax.ShapeDtypeStruct(measured.shape, jnp.float32),
        jax.ShapeDtypeStruct(((points + BLOCK) // LANES + 2, 3 * levels + rays, LANES), jnp.bfloat16),
        jax.ShapeDtypeStruct((3, pair_count, rays), jnp.float32),
        jax.ShapeDtypeStruct((3 * levels, rays), jnp.float32),
    ]
    out_specs = [hbm, vmem, vmem, vmem]
    if closes:
        shapes += [jax.ShapeDtypeStruct((levels, LANES), jnp.float32)] * 3
        out_specs += [vmem] * 3
    outs = pl.pallas_call(
        functools.partial(chunk_kernel, spans_of=spans_of, carrier=carrier, opens=opens, closes=closes),
        in_specs=specs,
        out_specs=out_specs,
        out_shape=shapes,
        scratch_shapes=[
            pltpu.VMEM((3 * levels + rays, PIECE), jnp.bfloat16),
            pltpu.VMEM((rays, width), jnp.float32),
            pltpu.VMEM((3, pair_count, BLOCK), jnp.bfloat16),
            pltpu.VMEM((rays, BLOCK), jnp.bfloat16),
            pltpu.SemaphoreType.DMA((sum(pl.cdiv(w, PIECE) for _, w in spans_of),)),
        ],
        input_output_aliases=aliases,
        compiler_params=pltpu.CompilerParams(vmem_limit_bytes=CHUNK_BYTES),
        cost_estimate=CHEAP,
        name="chunk",
    )(*args)
    return outs[:4], outs[4:]


def quad_step(work, row, p):
    r = [work[p + i : p + i + 1, :] for i in range(4)]

    def entry(i, j):
        return jnp.broadcast_to(r[i][:, p + j : p + j + 1], r[i].shape)

    a, b, d = entry(0, 0), entry(0, 1), entry(1, 1)
    f0, f1, g0, g1 = entry(0, 2), entry(0, 3), entry(1, 2), entry(1, 3)
    h, q, v = entry(2, 2), entry(2, 3), entry(3, 3)
    inverse = 1.0 / (a * d - b * b)
    a, b, d = d * inverse, -b * inverse, a * inverse
    w00, w01 = a * f0 + b * g0, a * f1 + b * g1
    w10, w11 = b * f0 + d * g0, b * f1 + d * g1
    h, q, v = h - (f0 * w00 + g0 * w10), q - (f0 * w01 + g0 * w11), v - (f1 * w01 + g1 * w11)
    inverse = 1.0 / (h * v - q * q)
    h, q, v = v * inverse, -q * inverse, h * inverse
    t0, t1 = a * r[0] + b * r[1], b * r[0] + d * r[1]
    u0, u1 = r[2] - (f0 * t0 + g0 * t1), r[3] - (f1 * t0 + g1 * t1)
    s2, s3 = h * u0 + q * u1, q * u0 + v * u1
    s0, s1 = t0 - (w00 * s2 + w01 * s3), t1 - (w10 * s2 + w11 * s3)
    update = None
    for i, s in enumerate((s0, s1, s2, s3)):
        column = work[:, p + i : p + i + 1]
        term = jnp.where(row[:, :1] == p + i, column - 1.0, column) * s
        update = term if update is None else update + term
    return work - update


def solve_kernel(*refs, scale):
    parts = refs[:6]
    prior_ref, out_ref = refs[6:]
    levels = prior_ref.shape[1]
    total = parts[0][...]
    for part in parts[1:]:
        total = total + part[...]
    terms = total * scale
    row = iota((levels, LANES), 0)
    lane = iota((levels, LANES), 1)
    square = terms[:, :levels]
    flipped = jnp.concatenate([square.T, jnp.zeros((levels, LANES - levels), jnp.float32)], axis=1)
    lower = row // ROWS >= lane // ROWS
    work = jnp.where(lower | (lane >= levels), terms, flipped)
    diagonal = jnp.sum(jnp.where(row == lane, work, 0.0), axis=1, keepdims=True)
    mean = jnp.sum(diagonal, axis=0, keepdims=True) * (1.0 / levels) + 1e-06
    eye = iota((levels, levels), 0) == iota((levels, levels), 1)
    prior = jnp.sum(jnp.where(eye, prior_ref[...], 0.0), axis=1, keepdims=True)
    work = work + jnp.where(row == lane, prior * mean, 0.0)
    for p in range(0, levels, 4):
        work = quad_step(work, row, p)
    column = work[:, levels : levels + 1]
    out_ref[...] = -jnp.sum(jnp.where(eye, column, 0.0), axis=0, keepdims=True)


def solve(parts, prior_weight, scale):
    return pl.pallas_call(
        functools.partial(solve_kernel, scale=scale),
        out_shape=jax.ShapeDtypeStruct((1, prior_weight.shape[1]), jnp.float32),
        compiler_params=pltpu.CompilerParams(vmem_limit_bytes=SMALL_BYTES),
        cost_estimate=CHEAP,
        name="solve",
    )(*parts, prior_weight)


def swapped(block, axis):
    size = lax.axis_size(axis)
    return lax.ppermute(block, axis, [(i, size - 1 - i) for i in range(size)])


def shards(absorption, absorber, seg_level, seg_count, seg_length, measured, window_mask, prior_weight):
    table = absorption[0]
    levels, points = table.shape
    rays = measured.shape[1]
    unit = points // sum(WIDTHS)
    widths = [w * unit for w in WIDTHS]
    firsts = [sum(widths[:c]) for c in range(len(widths))]
    mask = window_mask.reshape(points // LANES, LANES)
    level = jnp.swapaxes(seg_level[0], 1, 2)
    length = jnp.swapaxes(seg_length[0], 1, 2)
    count = seg_count.reshape(3, 1, rays)
    first_send, second_send, cols = prepare(level, count, length, absorber, table, firsts[CARRIER], widths[CARRIER])
    place, base, table_here, measured_here = stage(cols, mask, table, measured[0])
    base = base[:, :1]
    first_tables = []
    second_tables = []
    for c, (first, width) in enumerate(zip(firsts, widths, strict=True)):
        piece = table[:, first : first + width]
        first_tables.append(traded(first_send if c == CARRIER else piece, "sector", 0))
        second_tables.append(traded(second_send if c == CARRIER else piece, "sector", 1))
    state = None
    carried = (first_tables[CARRIER], second_tables[CARRIER])
    for n, group in enumerate(GROUPS):
        spans_of = tuple((firsts[c], widths[c]) for c in group)
        sources = [(first_tables[c], second_tables[c]) for c in group]
        closes = n == len(GROUPS) - 1
        state, terms = chunk(
            base, place, table_here, measured_here, cols, carried, widths[CARRIER], spans_of, sources, state, closes
        )
    spectrum = state[0]
    mine = (terms[1], traded(terms[0], "sector", 0), traded(terms[2], "sector", 1))
    others = tuple(swapped(part, "spec") for part in mine)
    scale = 1.0 / (rays * points * lax.axis_size("spec"))
    state_step = solve(mine + others, prior_weight[None, :], scale)
    return (spectrum[None], state_step)


def solution(mesh):
    return jax.shard_map(
        shards,
        mesh=mesh,
        in_specs=(
            P(("orbits", "sector"), None, "spec"),
            P(("orbits", "sector"), None),
            P(("orbits", "sector"), None, None, None),
            P(("orbits", "sector"), None, None),
            P(("orbits", "sector"), None, None, None),
            P(("orbits", "sector"), None, "spec"),
            P("spec"),
            P(),
        ),
        out_specs=(P(("orbits", "sector"), None, "spec"), P(("orbits", "sector"), None)),
        check_vma=False,
    )
```

```python
import functools

import jax
import jax.numpy as jnp
from jax import lax
from jax.experimental import pallas as pl
from jax.experimental.pallas import tpu as pltpu
from jax.sharding import PartitionSpec as P

LANES = 128
ROWS = 16
PIECE = 512
BLOCK = 512
WIDTHS = (12, 14, 6)
SMALL_BYTES = 4 << 20
CHUNK_BYTES = 16 << 20
CHEAP = pl.CostEstimate(flops=1, transcendentals=0, bytes_accessed=1)


def traded(block, axis, side):
    size = lax.axis_size(axis)
    steps = [1 if (i + side) % 2 == 0 else -1 for i in range(size)]
    return lax.ppermute(block, axis, [(i, (i + step) % size) for i, step in enumerate(steps)])


def iota(shape, dim):
    return lax.broadcasted_iota(jnp.int32, shape, dim)


def nt_dot(a, b):
    return lax.dot_general(a, b, (((1,), (1,)), ((), ())), preferred_element_type=jnp.float32)


def pinned(*arrays):
    return [pltpu.with_memory_space_constraint(array, pltpu.HBM) for array in arrays]


def prepare_kernel(level_hbm, count_hbm, length_hbm, absorber_hbm, table_hbm, *outs, first, width):
    first_ref, second_ref, cols_ref, level_ref, count_ref, length_ref, absorber_ref, sems = outs
    levels = absorber_ref.shape[1]
    sets, segs, rays = level_ref.shape
    arguments = ((level_hbm, level_ref), (length_hbm, length_ref), (count_hbm, count_ref), (absorber_hbm, absorber_ref))
    copies = [pltpu.make_async_copy(a, b, sems.at[n]) for n, (a, b) in enumerate(arguments)]
    for n, ref in enumerate((first_ref, second_ref)):
        source = table_hbm.at[:, pl.ds(first, width)]
        copies.append(pltpu.make_async_copy(source, ref.at[:, pl.ds(0, width)], sems.at[len(arguments) + n]))
    for copy in copies:
        copy.start()
    for copy in copies[: len(arguments)]:
        copy.wait()
    eye = iota((levels, levels), 0) == iota((levels, levels), 1)
    amount = jnp.sum(jnp.where(eye, absorber_ref[...], 0.0), axis=1, keepdims=True)
    level_of = iota((levels, rays), 0)
    odd = lax.axis_index("sector") % 2
    absorbed = []
    for k in range(sets):
        length = jnp.where(iota((segs, rays), 0) < count_ref[k], length_ref[k], 0.0)
        level = level_ref[k]
        path = jnp.zeros((levels, rays), jnp.float32)
        for j in range(segs):
            path += jnp.where(level[j : j + 1, :] == level_of, length[j : j + 1, :], 0.0)
        absorbed.append(path * amount)
    low, here, high = absorbed
    cols_ref[...] = here.astype(jnp.bfloat16)
    first_ref[:, width:] = jnp.where(odd == 1, low, high).astype(jnp.bfloat16)
    second_ref[:, width:] = jnp.where(odd == 1, high, low).astype(jnp.bfloat16)
    for copy in copies[len(arguments) :]:
        copy.wait()


def prepare(level, count, length, absorber, table, first, width):
    rays = level.shape[2]
    levels = absorber.shape[1]
    send = jax.ShapeDtypeStruct((levels, width + rays), jnp.bfloat16)
    hbm = pl.BlockSpec(memory_space=pltpu.HBM)
    return pl.pallas_call(
        functools.partial(prepare_kernel, first=first, width=width),
        in_specs=[hbm] * 5,
        out_shape=(send, send, jax.ShapeDtypeStruct((levels, rays), jnp.bfloat16)),
        scratch_shapes=[
            pltpu.VMEM(level.shape, level.dtype),
            pltpu.VMEM(count.shape, count.dtype),
            pltpu.VMEM(length.shape, length.dtype),
            pltpu.VMEM(absorber.shape, absorber.dtype),
            pltpu.SemaphoreType.DMA((6,)),
        ],
        compiler_params=pltpu.CompilerParams(vmem_limit_bytes=SMALL_BYTES),
        cost_estimate=CHEAP,
        name="prepare",
    )(*pinned(level, count, length, absorber, table))


def stage_kernel(cols_ref, mask_hbm, table_hbm, measured_hbm, place_ref, base_ref, table_ref, measured_ref, send_ref, mask_ref, sems, *, first):
    del cols_ref
    part = table_hbm.at[:, pl.ds(first, send_ref.shape[1])]
    moves = ((mask_hbm, mask_ref), (part, send_ref), (table_hbm, table_ref), (measured_hbm, measured_ref))
    copies = [pltpu.make_async_copy(a, b, sems.at[n]) for n, (a, b) in enumerate(moves)]
    for copy in copies:
        copy.start()
    copies[0].wait()
    groups = mask_ref.shape[0]
    mask = mask_ref[...].astype(jnp.bfloat16)
    before = (iota((LANES, LANES), 0) < iota((LANES, LANES), 1)).astype(jnp.bfloat16)
    rank = jnp.dot(mask, before, preferred_element_type=jnp.float32)
    total = jnp.dot(mask, jnp.ones((LANES, LANES), jnp.bfloat16), preferred_element_type=jnp.float32)
    earlier = (iota((groups, groups), 1) < iota((groups, groups), 0)).astype(jnp.bfloat16)
    base = jnp.dot(earlier, total.astype(jnp.bfloat16), preferred_element_type=jnp.float32)
    place_ref[...] = jnp.where(mask_ref[...] > 0, (base + rank).astype(jnp.int32), -1)
    base_ref[pl.ds(0, groups), :] = base.astype(jnp.int32)
    last = base[groups - 1 : groups, :] + total[groups - 1 : groups, :]
    base_ref[pl.ds(groups, 8), :] = jnp.broadcast_to(last, (8, LANES)).astype(jnp.int32)
    for copy in copies[1:]:
        copy.wait()


def stage(cols, mask, table, measured, first, width):
    groups = mask.shape[0]
    vmem = pl.BlockSpec(memory_space=pltpu.VMEM)
    hbm = pl.BlockSpec(memory_space=pltpu.HBM)
    return pl.pallas_call(
        functools.partial(stage_kernel, first=first),
        in_specs=[vmem, hbm, hbm, hbm],
        out_shape=(
            jax.ShapeDtypeStruct((groups, LANES), jnp.int32),
            jax.ShapeDtypeStruct((groups + 8, LANES), jnp.int32),
            jax.ShapeDtypeStruct(table.shape, table.dtype),
            jax.ShapeDtypeStruct(measured.shape, measured.dtype),
            jax.ShapeDtypeStruct((table.shape[0], width), table.dtype),
        ),
        scratch_shapes=[pltpu.VMEM(mask.shape, mask.dtype), pltpu.SemaphoreType.DMA((4,))],
        compiler_params=pltpu.CompilerParams(vmem_limit_bytes=SMALL_BYTES),
        cost_estimate=CHEAP,
        name="stage",
    )(cols, *pinned(mask, table, measured))


def pair_rows(levels):
    spans = []
    offset = 0
    for m in range(levels):
        first = ROWS * (m // ROWS)
        spans.append((m, first, offset, levels - first))
        offset += levels - first
    return spans, offset


def chunk_kernel(*refs, spans_of, carrier, opens, closes, onward):
    base_ref, place_ref, here_ref, measured_ref, cols_ref, carried_before, carried_after = refs[:7]
    refs = refs[7:]
    sources = []
    for _ in spans_of:
        sources.append(refs[:2])
        refs = refs[2:]
    if not opens:
        refs = refs[4:]
    spectrum_ref, packed, moment, projected = refs[:4]
    refs = refs[4:]
    if closes:
        terms_refs = refs[:3]
        refs = refs[3:]
    if onward:
        refs[0][...] = here_ref[:, onward[0] : onward[0] + onward[1]]
        refs = refs[1:]
    table, modelled, pairs, weights, sems = refs
    levels = here_ref.shape[0]
    rays = measured_ref.shape[0]
    high = 3 * levels
    begin = spans_of[0][0]
    end = spans_of[-1][0] + spans_of[-1][1]
    spans, pair_count = pair_rows(levels)
    cols = [ref.astype(jnp.float32) for ref in (carried_before[:, carrier:], cols_ref[...], carried_after[:, carrier:])]
    rows = jnp.concatenate([c.T for c in cols], axis=1).astype(jnp.bfloat16)

    if opens:
        moment[...] = jnp.zeros_like(moment)
        projected[...] = jnp.zeros_like(projected)
        packed[0] = jnp.zeros(packed.shape[1:], packed.dtype)

    copies = []
    for (first, width), (before_ref, after_ref) in zip(spans_of, sources, strict=True):
        for low_lane in range(0, width, PIECE):
            size = min(PIECE, width - low_lane)
            local = slice(low_lane, low_lane + size)
            overall = slice(first + low_lane, first + low_lane + size)
            table[0:levels, :size] = before_ref[:, local]
            table[levels : 2 * levels, :size] = here_ref[:, overall]
            table[2 * levels : high, :size] = after_ref[:, local]
            depth = jnp.dot(rows, table[:high, :size], preferred_element_type=jnp.float32)
            spectrum = jnp.exp(-depth)
            inside = slice(first + low_lane - begin, first + low_lane - begin + size)
            modelled[:, inside] = spectrum
            copy = pltpu.make_async_copy(modelled.at[:, inside], spectrum_ref.at[:, overall], sems.at[len(copies)])
            copy.start()
            copies.append(copy)
            table[high:, :size] = (spectrum * spectrum).astype(jnp.bfloat16)
            groups = range(overall.start // LANES, overall.stop // LANES)
            places = [place_ref[g : g + 1, :] for g in groups]
            kept = jnp.concatenate(places, axis=1) >= 0
            error = jnp.where(kept, (measured_ref[:, overall] - spectrum) * spectrum, 0.0).astype(jnp.bfloat16)
            projected[...] += nt_dot(table[:high, :size], error)
            for n, (g, place) in enumerate(zip(groups, places, strict=True)):
                at = base_ref[g, 0] // LANES
                chosen = (iota((2 * LANES, LANES), 0) + at * LANES == place).astype(jnp.bfloat16)
                moved = nt_dot(table[:, n * LANES : (n + 1) * LANES], chosen).astype(jnp.bfloat16)
                packed[at] = packed[at] + moved[:, :LANES]
                packed[at + 1] = moved[:, LANES:]

    def one_block(block, parts):
        wide = parts * LANES
        for p in range(parts):
            lane = slice(p * LANES, (p + 1) * LANES)
            weights[:, lane] = packed[block + p, high:, :]
            for k in range(3):
                level_rows = packed[block + p, k * levels : (k + 1) * levels, :]
                for m, low, offset, count in spans:
                    pairs[k, offset : offset + count, lane] = level_rows[low:, :] * level_rows[m : m + 1, :]
        for k in range(3):
            moment[k] += nt_dot(pairs[k, :, :wide], weights[:, :wide])

    parts = BLOCK // LANES
    done = base_ref[begin // LANES, 0] // BLOCK
    count = base_ref[end // LANES, 0]
    ready = count // BLOCK
    lax.fori_loop(done, ready, lambda block, carry: (one_block(block * parts, parts), carry)[1], 0)

    if closes:
        last = base_ref[end // LANES - 1, 0] // LANES
        for d in range(2, parts + 1):
            packed[last + d] = jnp.zeros(packed.shape[1:], packed.dtype)
        left = count - ready * BLOCK

        @pl.when(left > BLOCK // 2)
        def _():
            one_block(ready * parts, parts)

        @pl.when((left > 0) & (left <= BLOCK // 2))
        def _():
            one_block(ready * parts, parts // 2)

        lane = iota((levels, LANES), 1)
        for k in range(3):
            gradient = jnp.sum(cols[k] * projected[k * levels : (k + 1) * levels, :], axis=1, keepdims=True)
            result = jnp.where(lane == levels, gradient, 0.0)
            for m, low, offset, count in spans:
                column = jnp.sum(
                    moment[k, offset : offset + count, :] * (cols[k][low:, :] * cols[k][m : m + 1, :]),
                    axis=1,
                    keepdims=True,
                )
                if low:
                    column = jnp.concatenate([jnp.zeros((low, 1), jnp.float32), column], axis=0)
                result = jnp.where(lane == m, column, result)
            terms_refs[k][...] = result
    for copy in copies:
        copy.wait()


def chunk(base, place, here, measured, cols, carried, carrier, spans_of, sources, state, closes, onward):
    levels, points = here.shape
    rays = measured.shape[0]
    _, pair_count = pair_rows(levels)
    opens = state is None
    smem = pl.BlockSpec(memory_space=pltpu.SMEM)
    vmem = pl.BlockSpec(memory_space=pltpu.VMEM)
    hbm = pl.BlockSpec(memory_space=pltpu.HBM)
    width = sum(w for _, w in spans_of)
    args = [base, place, here, measured, cols, *carried]
    specs = [smem] + [vmem] * 6
    for pair in sources:
        args += pair
        specs += [vmem, vmem]
    aliases = {}
    if not opens:
        aliases = {len(args) + n: n for n in range(4)}
        args += state
        specs += [hbm, vmem, vmem, vmem]
    shapes = [
        jax.ShapeDtypeStruct(measured.shape, jnp.float32),
        jax.ShapeDtypeStruct(((points + BLOCK) // LANES + 2, 3 * levels + rays, LANES), jnp.bfloat16),
        jax.ShapeDtypeStruct((3, pair_count, rays), jnp.float32),
        jax.ShapeDtypeStruct((3 * levels, rays), jnp.float32),
    ]
    out_specs = [hbm, vmem, vmem, vmem]
    if closes:
        shapes += [jax.ShapeDtypeStruct((levels, LANES), jnp.float32)] * 3
        out_specs += [vmem] * 3
    if onward:
        shapes.append(jax.ShapeDtypeStruct((levels, onward[1]), here.dtype))
        out_specs.append(vmem)
    outs = pl.pallas_call(
        functools.partial(chunk_kernel, spans_of=spans_of, carrier=carrier, opens=opens, closes=closes, onward=onward),
        in_specs=specs,
        out_specs=out_specs,
        out_shape=shapes,
        scratch_shapes=[
            pltpu.VMEM((3 * levels + rays, PIECE), jnp.bfloat16),
            pltpu.VMEM((rays, width), jnp.float32),
            pltpu.VMEM((3, pair_count, BLOCK), jnp.bfloat16),
            pltpu.VMEM((rays, BLOCK), jnp.bfloat16),
            pltpu.SemaphoreType.DMA((sum(pl.cdiv(w, PIECE) for _, w in spans_of),)),
        ],
        input_output_aliases=aliases,
        compiler_params=pltpu.CompilerParams(vmem_limit_bytes=CHUNK_BYTES),
        cost_estimate=CHEAP,
        name="chunk",
    )(*args)
    return outs[:4], outs[4:]


def quad_step(work, row, p):
    r = [work[p + i : p + i + 1, :] for i in range(4)]

    def entry(i, j):
        return jnp.broadcast_to(r[i][:, p + j : p + j + 1], r[i].shape)

    a, b, d = entry(0, 0), entry(0, 1), entry(1, 1)
    f0, f1, g0, g1 = entry(0, 2), entry(0, 3), entry(1, 2), entry(1, 3)
    h, q, v = entry(2, 2), entry(2, 3), entry(3, 3)
    inverse = 1.0 / (a * d - b * b)
    a, b, d = d * inverse, -b * inverse, a * inverse
    w00, w01 = a * f0 + b * g0, a * f1 + b * g1
    w10, w11 = b * f0 + d * g0, b * f1 + d * g1
    h, q, v = h - (f0 * w00 + g0 * w10), q - (f0 * w01 + g0 * w11), v - (f1 * w01 + g1 * w11)
    inverse = 1.0 / (h * v - q * q)
    h, q, v = v * inverse, -q * inverse, h * inverse
    t0, t1 = a * r[0] + b * r[1], b * r[0] + d * r[1]
    u0, u1 = r[2] - (f0 * t0 + g0 * t1), r[3] - (f1 * t0 + g1 * t1)
    s2, s3 = h * u0 + q * u1, q * u0 + v * u1
    s0, s1 = t0 - (w00 * s2 + w01 * s3), t1 - (w10 * s2 + w11 * s3)
    update = None
    for i, s in enumerate((s0, s1, s2, s3)):
        column = work[:, p + i : p + i + 1]
        term = jnp.where(row[:, :1] == p + i, column - 1.0, column) * s
        update = term if update is None else update + term
    return work - update


def solve_kernel(*refs, scale):
    parts = refs[:6]
    prior_ref, out_ref = refs[6:]
    levels = prior_ref.shape[1]
    total = parts[0][...]
    for part in parts[1:]:
        total = total + part[...]
    terms = total * scale
    row = iota((levels, LANES), 0)
    lane = iota((levels, LANES), 1)
    square = terms[:, :levels]
    flipped = jnp.concatenate([square.T, jnp.zeros((levels, LANES - levels), jnp.float32)], axis=1)
    lower = row // ROWS >= lane // ROWS
    work = jnp.where(lower | (lane >= levels), terms, flipped)
    diagonal = jnp.sum(jnp.where(row == lane, work, 0.0), axis=1, keepdims=True)
    mean = jnp.sum(diagonal, axis=0, keepdims=True) * (1.0 / levels) + 1e-06
    eye = iota((levels, levels), 0) == iota((levels, levels), 1)
    prior = jnp.sum(jnp.where(eye, prior_ref[...], 0.0), axis=1, keepdims=True)
    work = work + jnp.where(row == lane, prior * mean, 0.0)
    for p in range(0, levels, 4):
        work = quad_step(work, row, p)
    column = work[:, levels : levels + 1]
    out_ref[...] = -jnp.sum(jnp.where(eye, column, 0.0), axis=0, keepdims=True)


def solve(parts, prior_weight, scale):
    return pl.pallas_call(
        functools.partial(solve_kernel, scale=scale),
        out_shape=jax.ShapeDtypeStruct((1, prior_weight.shape[1]), jnp.float32),
        compiler_params=pltpu.CompilerParams(vmem_limit_bytes=SMALL_BYTES),
        cost_estimate=CHEAP,
        name="solve",
    )(*parts, prior_weight)


def swapped(block, axis):
    size = lax.axis_size(axis)
    return lax.ppermute(block, axis, [(i, size - 1 - i) for i in range(size)])


def shards(absorption, absorber, seg_level, seg_count, seg_length, measured, window_mask, prior_weight):
    table = absorption[0]
    levels, points = table.shape
    rays = measured.shape[1]
    unit = points // sum(WIDTHS)
    widths = [w * unit for w in WIDTHS]
    firsts = [sum(widths[:c]) for c in range(len(widths))]
    mask = window_mask.reshape(points // LANES, LANES)
    level = jnp.swapaxes(seg_level[0], 1, 2)
    length = jnp.swapaxes(seg_length[0], 1, 2)
    count = seg_count.reshape(3, 1, rays)
    first_send, second_send, cols = prepare(level, count, length, absorber, table, firsts[0], widths[0])
    carried = (traded(first_send, "sector", 0), traded(second_send, "sector", 1))
    place, base, table_here, measured_here, send = stage(cols, mask, table, measured[0], firsts[1], widths[1])
    base = base[:, :1]
    state = None
    sources = carried
    for c, span in enumerate(zip(firsts, widths, strict=True)):
        closes = c == len(widths) - 1
        onward = (firsts[c + 2], widths[c + 2]) if c + 2 < len(widths) else None
        following = None if closes else (traded(send, "sector", 0), traded(send, "sector", 1))
        state, rest = chunk(
            base, place, table_here, measured_here, cols, carried, widths[0], (span,), [sources], state, closes, onward
        )
        sources = following
        if onward:
            send = rest[0]
    terms = rest
    spectrum = state[0]
    mine = (terms[1], traded(terms[0], "sector", 0), traded(terms[2], "sector", 1))
    others = tuple(swapped(part, "spec") for part in mine)
    scale = 1.0 / (rays * points * lax.axis_size("spec"))
    state_step = solve(mine + others, prior_weight[None, :], scale)
    return (spectrum[None], state_step)


def solution(mesh):
    return jax.shard_map(
        shards,
        mesh=mesh,
        in_specs=(
            P(("orbits", "sector"), None, "spec"),
            P(("orbits", "sector"), None),
            P(("orbits", "sector"), None, None, None),
            P(("orbits", "sector"), None, None),
            P(("orbits", "sector"), None, None, None),
            P(("orbits", "sector"), None, "spec"),
            P("spec"),
            P(),
        ),
        out_specs=(P(("orbits", "sector"), None, "spec"), P(("orbits", "sector"), None)),
        check_vma=False,
    )
```

```python
import functools

import jax
import jax.numpy as jnp
from jax import lax
from jax.experimental import pallas as pl
from jax.experimental.pallas import tpu as pltpu
from jax.sharding import PartitionSpec as P

LANES = 128
ROWS = 16
HALF = 8
PIECE = 512
BLOCK = 512
WIDTHS = (8, 8, 10, 6)
SMALL_BYTES = 4 << 20
CHUNK_BYTES = 16 << 20
CHEAP = pl.CostEstimate(flops=1, transcendentals=0, bytes_accessed=1)


def traded(block, axis, side):
    size = lax.axis_size(axis)
    steps = [1 if (i + side) % 2 == 0 else -1 for i in range(size)]
    return lax.ppermute(block, axis, [(i, (i + step) % size) for i, step in enumerate(steps)])


def iota(shape, dim):
    return lax.broadcasted_iota(jnp.int32, shape, dim)


def nt_dot(a, b):
    return lax.dot_general(a, b, (((1,), (1,)), ((), ())), preferred_element_type=jnp.float32)


def pinned(*arrays):
    return [pltpu.with_memory_space_constraint(array, pltpu.HBM) for array in arrays]


def prepare_kernel(level_hbm, count_hbm, length_hbm, absorber_hbm, table_hbm, *outs, first, width):
    first_ref, second_ref, cols_ref, level_ref, count_ref, length_ref, absorber_ref, sems = outs
    levels = absorber_ref.shape[1]
    sets, segs, rays = level_ref.shape
    arguments = ((level_hbm, level_ref), (length_hbm, length_ref), (count_hbm, count_ref), (absorber_hbm, absorber_ref))
    copies = [pltpu.make_async_copy(a, b, sems.at[n]) for n, (a, b) in enumerate(arguments)]
    for n, ref in enumerate((first_ref, second_ref)):
        source = table_hbm.at[:, pl.ds(first, width)]
        copies.append(pltpu.make_async_copy(source, ref.at[:, pl.ds(0, width)], sems.at[len(arguments) + n]))
    for copy in copies:
        copy.start()
    for copy in copies[: len(arguments)]:
        copy.wait()
    eye = iota((levels, levels), 0) == iota((levels, levels), 1)
    amount = jnp.sum(jnp.where(eye, absorber_ref[...], 0.0), axis=1, keepdims=True)
    level_of = iota((levels, rays), 0)
    odd = lax.axis_index("sector") % 2
    absorbed = []
    for k in range(sets):
        length = jnp.where(iota((segs, rays), 0) < count_ref[k], length_ref[k], 0.0)
        level = level_ref[k]
        path = jnp.zeros((levels, rays), jnp.float32)
        for j in range(segs):
            path += jnp.where(level[j : j + 1, :] == level_of, length[j : j + 1, :], 0.0)
        absorbed.append(path * amount)
    low, here, high = absorbed
    cols_ref[...] = here.astype(jnp.bfloat16)
    first_ref[:, width:] = jnp.where(odd == 1, low, high).astype(jnp.bfloat16)
    second_ref[:, width:] = jnp.where(odd == 1, high, low).astype(jnp.bfloat16)
    for copy in copies[len(arguments) :]:
        copy.wait()


def prepare(level, count, length, absorber, table, first, width):
    rays = level.shape[2]
    levels = absorber.shape[1]
    send = jax.ShapeDtypeStruct((levels, width + rays), jnp.bfloat16)
    hbm = pl.BlockSpec(memory_space=pltpu.HBM)
    return pl.pallas_call(
        functools.partial(prepare_kernel, first=first, width=width),
        in_specs=[hbm] * 5,
        out_shape=(send, send, jax.ShapeDtypeStruct((levels, rays), jnp.bfloat16)),
        scratch_shapes=[
            pltpu.VMEM(level.shape, level.dtype),
            pltpu.VMEM(count.shape, count.dtype),
            pltpu.VMEM(length.shape, length.dtype),
            pltpu.VMEM(absorber.shape, absorber.dtype),
            pltpu.SemaphoreType.DMA((6,)),
        ],
        compiler_params=pltpu.CompilerParams(vmem_limit_bytes=SMALL_BYTES),
        cost_estimate=CHEAP,
        name="prepare",
    )(*pinned(level, count, length, absorber, table))


def stage_kernel(cols_ref, mask_hbm, table_hbm, measured_hbm, place_ref, base_ref, table_ref, measured_ref, send_ref, mask_ref, sems, *, first):
    del cols_ref
    part = table_hbm.at[:, pl.ds(first, send_ref.shape[1])]
    moves = ((mask_hbm, mask_ref), (part, send_ref), (table_hbm, table_ref), (measured_hbm, measured_ref))
    copies = [pltpu.make_async_copy(a, b, sems.at[n]) for n, (a, b) in enumerate(moves)]
    for copy in copies:
        copy.start()
    copies[0].wait()
    groups = mask_ref.shape[0]
    mask = mask_ref[...].astype(jnp.bfloat16)
    before = (iota((LANES, LANES), 0) < iota((LANES, LANES), 1)).astype(jnp.bfloat16)
    rank = jnp.dot(mask, before, preferred_element_type=jnp.float32)
    total = jnp.dot(mask, jnp.ones((LANES, LANES), jnp.bfloat16), preferred_element_type=jnp.float32)
    earlier = (iota((groups, groups), 1) < iota((groups, groups), 0)).astype(jnp.bfloat16)
    base = jnp.dot(earlier, total.astype(jnp.bfloat16), preferred_element_type=jnp.float32)
    place_ref[...] = jnp.where(mask_ref[...] > 0, (base + rank).astype(jnp.int32), -1)
    base_ref[pl.ds(0, groups), :] = base.astype(jnp.int32)
    last = base[groups - 1 : groups, :] + total[groups - 1 : groups, :]
    base_ref[pl.ds(groups, 8), :] = jnp.broadcast_to(last, (8, LANES)).astype(jnp.int32)
    for copy in copies[1:]:
        copy.wait()


def stage(cols, mask, table, measured, first, width):
    groups = mask.shape[0]
    vmem = pl.BlockSpec(memory_space=pltpu.VMEM)
    hbm = pl.BlockSpec(memory_space=pltpu.HBM)
    return pl.pallas_call(
        functools.partial(stage_kernel, first=first),
        in_specs=[vmem, hbm, hbm, hbm],
        out_shape=(
            jax.ShapeDtypeStruct((groups, LANES), jnp.int32),
            jax.ShapeDtypeStruct((groups + 8, LANES), jnp.int32),
            jax.ShapeDtypeStruct(table.shape, table.dtype),
            jax.ShapeDtypeStruct(measured.shape, measured.dtype),
            jax.ShapeDtypeStruct((table.shape[0], width), table.dtype),
        ),
        scratch_shapes=[pltpu.VMEM(mask.shape, mask.dtype), pltpu.SemaphoreType.DMA((4,))],
        compiler_params=pltpu.CompilerParams(vmem_limit_bytes=SMALL_BYTES),
        cost_estimate=CHEAP,
        name="stage",
    )(cols, *pinned(mask, table, measured))


def pair_rows(levels):
    whole = []
    shared = []
    spans = []
    offset = 0
    for m in range(levels):
        tile = ROWS * (m // ROWS)
        low = tile if m % ROWS < HALF else tile + ROWS
        if low < levels:
            whole.append((m, low, offset))
            spans.append((m, low, offset, levels - low))
            offset += levels - low
    for m in range(0, levels, 2):
        if m % ROWS >= HALF:
            low = ROWS * (m // ROWS) + HALF
            shared.append((m, low, offset))
            for n in range(2):
                spans.append((m + n, low, offset + n * HALF, HALF))
            offset += ROWS
    return whole, shared, spans, offset


def fill_pairs(target, k, lane, rows):
    levels = rows.shape[0]
    whole, shared, _, _ = pair_rows(levels)
    for m, low, offset in whole:
        target[k, offset : offset + levels - low, lane] = rows[low:, :] * rows[m : m + 1, :]
    upper = iota((ROWS, rows.shape[1]), 0) < HALF
    for m, low, offset in shared:
        half = rows[low : low + HALF, :]
        both = jnp.concatenate([half, half], axis=0)
        target[k, offset : offset + ROWS, lane] = both * jnp.where(upper, rows[m : m + 1, :], rows[m + 1 : m + 2, :])


def chunk_kernel(*refs, spans_of, carrier, opens, closes, onward):
    base_ref, place_ref, here_ref, measured_ref, cols_ref, carried_before, carried_after = refs[:7]
    refs = refs[7:]
    sources = []
    for _ in spans_of:
        sources.append(refs[:2])
        refs = refs[2:]
    if not opens:
        refs = refs[4:]
    spectrum_ref, packed, moment, projected = refs[:4]
    refs = refs[4:]
    if closes:
        terms_refs = refs[:3]
        refs = refs[3:]
    if onward:
        refs[0][...] = here_ref[:, onward[0] : onward[0] + onward[1]]
        refs = refs[1:]
    table, modelled, pairs, weights, sems = refs
    levels = here_ref.shape[0]
    rays = measured_ref.shape[0]
    high = 3 * levels
    begin = spans_of[0][0]
    end = spans_of[-1][0] + spans_of[-1][1]
    _, _, spans, pair_count = pair_rows(levels)
    cols = [ref.astype(jnp.float32) for ref in (carried_before[:, carrier:], cols_ref[...], carried_after[:, carrier:])]
    rows = jnp.concatenate([c.T for c in cols], axis=1).astype(jnp.bfloat16)

    if opens:
        moment[...] = jnp.zeros_like(moment)
        projected[...] = jnp.zeros_like(projected)
        packed[0] = jnp.zeros(packed.shape[1:], packed.dtype)

    copies = []
    for (first, width), (before_ref, after_ref) in zip(spans_of, sources, strict=True):
        for low_lane in range(0, width, PIECE):
            size = min(PIECE, width - low_lane)
            local = slice(low_lane, low_lane + size)
            overall = slice(first + low_lane, first + low_lane + size)
            inside = slice(first + low_lane - begin, first + low_lane - begin + size)
            table[0:levels, inside] = before_ref[:, local]
            table[levels : 2 * levels, inside] = here_ref[:, overall]
            table[2 * levels : high, inside] = after_ref[:, local]
            depth = jnp.dot(rows, table[:high, inside], preferred_element_type=jnp.float32)
            spectrum = jnp.exp(-depth)
            modelled[:, inside] = spectrum
            copy = pltpu.make_async_copy(modelled.at[:, inside], spectrum_ref.at[:, overall], sems.at[len(copies)])
            copy.start()
            copies.append(copy)
            table[high:, inside] = (spectrum * spectrum).astype(jnp.bfloat16)
            groups = range(overall.start // LANES, overall.stop // LANES)
            places = [place_ref[g : g + 1, :] for g in groups]
            kept = jnp.concatenate(places, axis=1) >= 0
            error = jnp.where(kept, (measured_ref[:, overall] - spectrum) * spectrum, 0.0).astype(jnp.bfloat16)
            projected[...] += nt_dot(table[:high, inside], error)
            for n, (g, place) in enumerate(zip(groups, places, strict=True)):
                at = base_ref[g, 0] // LANES
                chosen = (iota((2 * LANES, LANES), 0) + at * LANES == place).astype(jnp.bfloat16)
                moved = nt_dot(table[:, inside.start + n * LANES : inside.start + (n + 1) * LANES], chosen).astype(jnp.bfloat16)
                packed[at] = packed[at] + moved[:, :LANES]
                packed[at + 1] = moved[:, LANES:]

    def one_block(block, parts, then=None):
        wide = parts * LANES
        for p in range(parts):
            lane = slice(p * LANES, (p + 1) * LANES)
            weights[:, lane] = packed[block + p, high:, :]
            for k in range(3):
                fill_pairs(pairs, k, lane, packed[block + p, k * levels : (k + 1) * levels, :])
        for k in range(3):
            moment[k] += nt_dot(pairs[k, :, :wide], weights[:, :wide])
            if then and k:
                then(k - 1)
        if then:
            then(2)

    parts = BLOCK // LANES
    done = base_ref[begin // LANES, 0] // BLOCK
    count = base_ref[end // LANES, 0]
    ready = count // BLOCK
    lax.fori_loop(done, ready, lambda block, carry: (one_block(block * parts, parts), carry)[1], 0)

    if closes:
        last = base_ref[end // LANES - 1, 0] // LANES
        for d in range(2, parts + 1):
            packed[last + d] = jnp.zeros(packed.shape[1:], packed.dtype)
        left = count - ready * BLOCK
        lane = iota((levels, LANES), 1)

        def contract(k):
            gradient = jnp.sum(cols[k] * projected[k * levels : (k + 1) * levels, :], axis=1, keepdims=True)
            result = jnp.where(lane == levels, gradient, 0.0)
            columns = {}
            for m, low, offset, size in spans:
                scaled = cols[k][low : low + size, :] * cols[k][m : m + 1, :]
                column = jnp.sum(moment[k, offset : offset + size, :] * scaled, axis=1, keepdims=True)
                columns.setdefault(m, []).append((low, column))
            for m, parts_of in columns.items():
                parts_of = sorted(parts_of, key=lambda part: part[0])
                low = parts_of[0][0]
                stack = [column for _, column in parts_of]
                if low:
                    stack = [jnp.zeros((low, 1), jnp.float32), *stack]
                result = jnp.where(lane == m, jnp.concatenate(stack, axis=0) if len(stack) > 1 else stack[0], result)
            terms_refs[k][...] = result

        @pl.when(left > BLOCK // 2)
        def _():
            one_block(ready * parts, parts, contract)

        @pl.when(left <= BLOCK // 2)
        def _():
            one_block(ready * parts, parts // 2, contract)

    for copy in copies:
        copy.wait()


def chunk(base, place, here, measured, cols, carried, carrier, spans_of, sources, state, closes, onward):
    levels, points = here.shape
    rays = measured.shape[0]
    _, _, _, pair_count = pair_rows(levels)
    opens = state is None
    smem = pl.BlockSpec(memory_space=pltpu.SMEM)
    vmem = pl.BlockSpec(memory_space=pltpu.VMEM)
    hbm = pl.BlockSpec(memory_space=pltpu.HBM)
    width = sum(w for _, w in spans_of)
    args = [base, place, here, measured, cols, *carried]
    specs = [smem] + [vmem] * 6
    for pair in sources:
        args += pair
        specs += [vmem, vmem]
    aliases = {}
    if not opens:
        aliases = {len(args) + n: n for n in range(4)}
        args += state
        specs += [hbm, vmem, vmem, vmem]
    shapes = [
        jax.ShapeDtypeStruct(measured.shape, jnp.float32),
        jax.ShapeDtypeStruct(((points + BLOCK) // LANES + 2, 3 * levels + rays, LANES), jnp.bfloat16),
        jax.ShapeDtypeStruct((3, pair_count, rays), jnp.float32),
        jax.ShapeDtypeStruct((3 * levels, rays), jnp.float32),
    ]
    out_specs = [hbm, vmem, vmem, vmem]
    if closes:
        shapes += [jax.ShapeDtypeStruct((levels, LANES), jnp.float32)] * 3
        out_specs += [vmem] * 3
    if onward:
        shapes.append(jax.ShapeDtypeStruct((levels, onward[1]), here.dtype))
        out_specs.append(vmem)
    outs = pl.pallas_call(
        functools.partial(chunk_kernel, spans_of=spans_of, carrier=carrier, opens=opens, closes=closes, onward=onward),
        in_specs=specs,
        out_specs=out_specs,
        out_shape=shapes,
        scratch_shapes=[
            pltpu.VMEM((3 * levels + rays, width), jnp.bfloat16),
            pltpu.VMEM((rays, width), jnp.float32),
            pltpu.VMEM((3, pair_count, BLOCK), jnp.bfloat16),
            pltpu.VMEM((rays, BLOCK), jnp.bfloat16),
            pltpu.SemaphoreType.DMA((sum(pl.cdiv(w, PIECE) for _, w in spans_of),)),
        ],
        input_output_aliases=aliases,
        compiler_params=pltpu.CompilerParams(vmem_limit_bytes=CHUNK_BYTES),
        cost_estimate=CHEAP,
        name="chunk",
    )(*args)
    return outs[:4], outs[4:]


def quad_step(work, row, p):
    r = [work[p + i : p + i + 1, :] for i in range(4)]

    def entry(i, j):
        return jnp.broadcast_to(r[i][:, p + j : p + j + 1], r[i].shape)

    a, b, d = entry(0, 0), entry(0, 1), entry(1, 1)
    f0, f1, g0, g1 = entry(0, 2), entry(0, 3), entry(1, 2), entry(1, 3)
    h, q, v = entry(2, 2), entry(2, 3), entry(3, 3)
    inverse = 1.0 / (a * d - b * b)
    a, b, d = d * inverse, -b * inverse, a * inverse
    w00, w01 = a * f0 + b * g0, a * f1 + b * g1
    w10, w11 = b * f0 + d * g0, b * f1 + d * g1
    h, q, v = h - (f0 * w00 + g0 * w10), q - (f0 * w01 + g0 * w11), v - (f1 * w01 + g1 * w11)
    inverse = 1.0 / (h * v - q * q)
    h, q, v = v * inverse, -q * inverse, h * inverse
    t0, t1 = a * r[0] + b * r[1], b * r[0] + d * r[1]
    u0, u1 = r[2] - (f0 * t0 + g0 * t1), r[3] - (f1 * t0 + g1 * t1)
    s2, s3 = h * u0 + q * u1, q * u0 + v * u1
    s0, s1 = t0 - (w00 * s2 + w01 * s3), t1 - (w10 * s2 + w11 * s3)
    update = None
    for i, s in enumerate((s0, s1, s2, s3)):
        column = work[:, p + i : p + i + 1]
        term = jnp.where(row[:, :1] == p + i, column - 1.0, column) * s
        update = term if update is None else update + term
    return work - update


def solve_kernel(*refs, scale):
    parts = refs[:6]
    prior_ref, out_ref = refs[6:]
    levels = prior_ref.shape[1]
    total = parts[0][...]
    for part in parts[1:]:
        total = total + part[...]
    terms = total * scale
    row = iota((levels, LANES), 0)
    lane = iota((levels, LANES), 1)
    square = terms[:, :levels]
    flipped = jnp.concatenate([square.T, jnp.zeros((levels, LANES - levels), jnp.float32)], axis=1)
    lower = row // HALF >= lane // HALF
    work = jnp.where(lower | (lane >= levels), terms, flipped)
    diagonal = jnp.sum(jnp.where(row == lane, work, 0.0), axis=1, keepdims=True)
    mean = jnp.sum(diagonal, axis=0, keepdims=True) * (1.0 / levels) + 1e-06
    eye = iota((levels, levels), 0) == iota((levels, levels), 1)
    prior = jnp.sum(jnp.where(eye, prior_ref[...], 0.0), axis=1, keepdims=True)
    work = work + jnp.where(row == lane, prior * mean, 0.0)
    for p in range(0, levels, 4):
        work = quad_step(work, row, p)
    column = work[:, levels : levels + 1]
    out_ref[...] = -jnp.sum(jnp.where(eye, column, 0.0), axis=0, keepdims=True)


def solve(parts, prior_weight, scale):
    return pl.pallas_call(
        functools.partial(solve_kernel, scale=scale),
        out_shape=jax.ShapeDtypeStruct((1, prior_weight.shape[1]), jnp.float32),
        compiler_params=pltpu.CompilerParams(vmem_limit_bytes=SMALL_BYTES),
        cost_estimate=CHEAP,
        name="solve",
    )(*parts, prior_weight)


def swapped(block, axis):
    size = lax.axis_size(axis)
    return lax.ppermute(block, axis, [(i, size - 1 - i) for i in range(size)])


def shards(absorption, absorber, seg_level, seg_count, seg_length, measured, window_mask, prior_weight):
    table = absorption[0]
    levels, points = table.shape
    rays = measured.shape[1]
    unit = points // sum(WIDTHS)
    widths = [w * unit for w in WIDTHS]
    firsts = [sum(widths[:c]) for c in range(len(widths))]
    mask = window_mask.reshape(points // LANES, LANES)
    level = jnp.swapaxes(seg_level[0], 1, 2)
    length = jnp.swapaxes(seg_length[0], 1, 2)
    count = seg_count.reshape(3, 1, rays)
    first_send, second_send, cols = prepare(level, count, length, absorber, table, firsts[0], widths[0])
    carried = (traded(first_send, "sector", 0), traded(second_send, "sector", 1))
    place, base, table_here, measured_here, send = stage(cols, mask, table, measured[0], firsts[1], widths[1])
    base = base[:, :1]
    state = None
    sources = carried
    for c, span in enumerate(zip(firsts, widths, strict=True)):
        closes = c == len(widths) - 1
        onward = (firsts[c + 2], widths[c + 2]) if c + 2 < len(widths) else None
        following = None if closes else (traded(send, "sector", 0), traded(send, "sector", 1))
        state, rest = chunk(
            base, place, table_here, measured_here, cols, carried, widths[0], (span,), [sources], state, closes, onward
        )
        sources = following
        if onward:
            send = rest[0]
    terms = rest
    spectrum = state[0]
    mine = (terms[1], traded(terms[0], "sector", 0), traded(terms[2], "sector", 1))
    others = tuple(swapped(part, "spec") for part in mine)
    scale = 1.0 / (rays * points * lax.axis_size("spec"))
    state_step = solve(mine + others, prior_weight[None, :], scale)
    return (spectrum[None], state_step)


def solution(mesh):
    return jax.shard_map(
        shards,
        mesh=mesh,
        in_specs=(
            P(("orbits", "sector"), None, "spec"),
            P(("orbits", "sector"), None),
            P(("orbits", "sector"), None, None, None),
            P(("orbits", "sector"), None, None),
            P(("orbits", "sector"), None, None, None),
            P(("orbits", "sector"), None, "spec"),
            P("spec"),
            P(),
        ),
        out_specs=(P(("orbits", "sector"), None, "spec"), P(("orbits", "sector"), None)),
        check_vma=False,
    )
```

```python
import functools

import jax
import jax.numpy as jnp
from jax import lax
from jax.experimental import pallas as pl
from jax.experimental.pallas import tpu as pltpu
from jax.sharding import PartitionSpec as P

LANES = 128
ROWS = 16
HALF = 8
PIECE = 512
BLOCK = 512
WIDTHS = (8, 12, 12)
SMALL_BYTES = 4 << 20
CHUNK_BYTES = 16 << 20
CHEAP = pl.CostEstimate(flops=1, transcendentals=0, bytes_accessed=1)


def traded(block, axis, side):
    size = lax.axis_size(axis)
    steps = [1 if (i + side) % 2 == 0 else -1 for i in range(size)]
    return lax.ppermute(block, axis, [(i, (i + step) % size) for i, step in enumerate(steps)])


def iota(shape, dim):
    return lax.broadcasted_iota(jnp.int32, shape, dim)


def nt_dot(a, b):
    return lax.dot_general(a, b, (((1,), (1,)), ((), ())), preferred_element_type=jnp.float32)


def pinned(*arrays):
    return [pltpu.with_memory_space_constraint(array, pltpu.HBM) for array in arrays]


def prepare_kernel(level_hbm, count_hbm, length_hbm, absorber_hbm, table_hbm, *outs, first, width):
    first_ref, second_ref, cols_ref, level_ref, count_ref, length_ref, absorber_ref, sems = outs
    levels = absorber_ref.shape[1]
    sets, segs, rays = level_ref.shape
    arguments = ((level_hbm, level_ref), (length_hbm, length_ref), (count_hbm, count_ref), (absorber_hbm, absorber_ref))
    copies = [pltpu.make_async_copy(a, b, sems.at[n]) for n, (a, b) in enumerate(arguments)]
    for n, ref in enumerate((first_ref, second_ref)):
        source = table_hbm.at[:, pl.ds(first, width)]
        copies.append(pltpu.make_async_copy(source, ref.at[:, pl.ds(0, width)], sems.at[len(arguments) + n]))
    for copy in copies:
        copy.start()
    for copy in copies[: len(arguments)]:
        copy.wait()
    eye = iota((levels, levels), 0) == iota((levels, levels), 1)
    amount = jnp.sum(jnp.where(eye, absorber_ref[...], 0.0), axis=1, keepdims=True)
    level_of = iota((levels, rays), 0)
    odd = lax.axis_index("sector") % 2
    absorbed = []
    for k in range(sets):
        length = jnp.where(iota((segs, rays), 0) < count_ref[k], length_ref[k], 0.0)
        level = level_ref[k]
        path = jnp.zeros((levels, rays), jnp.float32)
        for j in range(segs):
            path += jnp.where(level[j : j + 1, :] == level_of, length[j : j + 1, :], 0.0)
        absorbed.append(path * amount)
    low, here, high = absorbed
    cols_ref[...] = here.astype(jnp.bfloat16)
    first_ref[:, width:] = jnp.where(odd == 1, low, high).astype(jnp.bfloat16)
    second_ref[:, width:] = jnp.where(odd == 1, high, low).astype(jnp.bfloat16)
    for copy in copies[len(arguments) :]:
        copy.wait()


def prepare(level, count, length, absorber, table, first, width):
    rays = level.shape[2]
    levels = absorber.shape[1]
    send = jax.ShapeDtypeStruct((levels, width + rays), jnp.bfloat16)
    hbm = pl.BlockSpec(memory_space=pltpu.HBM)
    return pl.pallas_call(
        functools.partial(prepare_kernel, first=first, width=width),
        in_specs=[hbm] * 5,
        out_shape=(send, send, jax.ShapeDtypeStruct((levels, rays), jnp.bfloat16)),
        scratch_shapes=[
            pltpu.VMEM(level.shape, level.dtype),
            pltpu.VMEM(count.shape, count.dtype),
            pltpu.VMEM(length.shape, length.dtype),
            pltpu.VMEM(absorber.shape, absorber.dtype),
            pltpu.SemaphoreType.DMA((6,)),
        ],
        compiler_params=pltpu.CompilerParams(vmem_limit_bytes=SMALL_BYTES),
        cost_estimate=CHEAP,
        name="prepare",
    )(*pinned(level, count, length, absorber, table))


def stage_kernel(cols_ref, mask_hbm, table_hbm, measured_hbm, place_ref, base_ref, table_ref, measured_ref, *rest, firsts):
    del cols_ref
    *sends, mask_ref, sems = rest
    moves = [(mask_hbm, mask_ref)]
    moves += [(table_hbm.at[:, pl.ds(first, ref.shape[1])], ref) for first, ref in zip(firsts, sends, strict=True)]
    moves += [(table_hbm, table_ref), (measured_hbm, measured_ref)]
    copies = [pltpu.make_async_copy(a, b, sems.at[n]) for n, (a, b) in enumerate(moves)]
    for copy in copies:
        copy.start()
    copies[0].wait()
    groups = mask_ref.shape[0]
    mask = mask_ref[...].astype(jnp.bfloat16)
    before = (iota((LANES, LANES), 0) < iota((LANES, LANES), 1)).astype(jnp.bfloat16)
    rank = jnp.dot(mask, before, preferred_element_type=jnp.float32)
    total = jnp.dot(mask, jnp.ones((LANES, LANES), jnp.bfloat16), preferred_element_type=jnp.float32)
    earlier = (iota((groups, groups), 1) < iota((groups, groups), 0)).astype(jnp.bfloat16)
    base = jnp.dot(earlier, total.astype(jnp.bfloat16), preferred_element_type=jnp.float32)
    place_ref[...] = jnp.where(mask_ref[...] > 0, (base + rank).astype(jnp.int32), -1)
    base_ref[pl.ds(0, groups), :] = base.astype(jnp.int32)
    last = base[groups - 1 : groups, :] + total[groups - 1 : groups, :]
    base_ref[pl.ds(groups, 8), :] = jnp.broadcast_to(last, (8, LANES)).astype(jnp.int32)
    for copy in copies[1:]:
        copy.wait()


def stage(cols, mask, table, measured, firsts, widths):
    groups = mask.shape[0]
    vmem = pl.BlockSpec(memory_space=pltpu.VMEM)
    hbm = pl.BlockSpec(memory_space=pltpu.HBM)
    return pl.pallas_call(
        functools.partial(stage_kernel, firsts=firsts),
        in_specs=[vmem, hbm, hbm, hbm],
        out_shape=(
            jax.ShapeDtypeStruct((groups, LANES), jnp.int32),
            jax.ShapeDtypeStruct((groups + 8, LANES), jnp.int32),
            jax.ShapeDtypeStruct(table.shape, table.dtype),
            jax.ShapeDtypeStruct(measured.shape, measured.dtype),
            *[jax.ShapeDtypeStruct((table.shape[0], width), table.dtype) for width in widths],
        ),
        scratch_shapes=[pltpu.VMEM(mask.shape, mask.dtype), pltpu.SemaphoreType.DMA((3 + len(widths),))],
        compiler_params=pltpu.CompilerParams(vmem_limit_bytes=SMALL_BYTES),
        cost_estimate=CHEAP,
        name="stage",
    )(cols, *pinned(mask, table, measured))


def pair_rows(levels):
    whole = []
    shared = []
    spans = []
    offset = 0
    for m in range(levels):
        tile = ROWS * (m // ROWS)
        low = tile if m % ROWS < HALF else tile + ROWS
        if low < levels:
            whole.append((m, low, offset))
            spans.append((m, low, offset, levels - low))
            offset += levels - low
    for m in range(0, levels, 2):
        if m % ROWS >= HALF:
            low = ROWS * (m // ROWS) + HALF
            shared.append((m, low, offset))
            for n in range(2):
                spans.append((m + n, low, offset + n * HALF, HALF))
            offset += ROWS
    return whole, shared, spans, offset


def fill_pairs(target, k, lane, rows):
    levels = rows.shape[0]
    whole, shared, _, _ = pair_rows(levels)
    for m, low, offset in whole:
        target[k, offset : offset + levels - low, lane] = rows[low:, :] * rows[m : m + 1, :]
    upper = iota((ROWS, rows.shape[1]), 0) < HALF
    for m, low, offset in shared:
        half = rows[low : low + HALF, :]
        both = jnp.concatenate([half, half], axis=0)
        target[k, offset : offset + ROWS, lane] = both * jnp.where(upper, rows[m : m + 1, :], rows[m + 1 : m + 2, :])


def chunk_kernel(*refs, spans_of, carrier, opens, closes):
    base_ref, place_ref, here_ref, measured_ref, cols_ref, carried_before, carried_after = refs[:7]
    refs = refs[7:]
    sources = []
    for _ in spans_of:
        sources.append(refs[:2])
        refs = refs[2:]
    if not opens:
        refs = refs[4:]
    spectrum_ref, packed, moment, projected = refs[:4]
    refs = refs[4:]
    if closes:
        terms_refs = refs[:3]
        refs = refs[3:]
    table, modelled, pairs, weights, sems = refs
    levels = here_ref.shape[0]
    rays = measured_ref.shape[0]
    high = 3 * levels
    begin = spans_of[0][0]
    end = spans_of[-1][0] + spans_of[-1][1]
    _, _, spans, pair_count = pair_rows(levels)
    cols = [ref.astype(jnp.float32) for ref in (carried_before[:, carrier:], cols_ref[...], carried_after[:, carrier:])]
    rows = jnp.concatenate([c.T for c in cols], axis=1).astype(jnp.bfloat16)

    if opens:
        moment[...] = jnp.zeros_like(moment)
        projected[...] = jnp.zeros_like(projected)
        packed[0] = jnp.zeros(packed.shape[1:], packed.dtype)

    copies = []
    for (first, width), (before_ref, after_ref) in zip(spans_of, sources, strict=True):
        for low_lane in range(0, width, PIECE):
            size = min(PIECE, width - low_lane)
            local = slice(low_lane, low_lane + size)
            overall = slice(first + low_lane, first + low_lane + size)
            inside = slice(first + low_lane - begin, first + low_lane - begin + size)
            table[0:levels, inside] = before_ref[:, local]
            table[levels : 2 * levels, inside] = here_ref[:, overall]
            table[2 * levels : high, inside] = after_ref[:, local]
            depth = jnp.dot(rows, table[:high, inside], preferred_element_type=jnp.float32)
            spectrum = jnp.exp(-depth)
            modelled[:, inside] = spectrum
            copy = pltpu.make_async_copy(modelled.at[:, inside], spectrum_ref.at[:, overall], sems.at[len(copies)])
            copy.start()
            copies.append(copy)
            table[high:, inside] = (spectrum * spectrum).astype(jnp.bfloat16)
            groups = range(overall.start // LANES, overall.stop // LANES)
            places = [place_ref[g : g + 1, :] for g in groups]
            kept = jnp.concatenate(places, axis=1) >= 0
            error = jnp.where(kept, (measured_ref[:, overall] - spectrum) * spectrum, 0.0).astype(jnp.bfloat16)
            projected[...] += nt_dot(table[:high, inside], error)
            for n, (g, place) in enumerate(zip(groups, places, strict=True)):
                at = base_ref[g, 0] // LANES
                chosen = (iota((2 * LANES, LANES), 0) + at * LANES == place).astype(jnp.bfloat16)
                moved = nt_dot(table[:, inside.start + n * LANES : inside.start + (n + 1) * LANES], chosen).astype(jnp.bfloat16)
                packed[at] = packed[at] + moved[:, :LANES]
                packed[at + 1] = moved[:, LANES:]

    def one_block(block, parts):
        wide = parts * LANES
        for p in range(parts):
            lane = slice(p * LANES, (p + 1) * LANES)
            weights[:, lane] = packed[block + p, high:, :]
            for k in range(3):
                fill_pairs(pairs, k, lane, packed[block + p, k * levels : (k + 1) * levels, :])
        for k in range(3):
            moment[k] += nt_dot(pairs[k, :, :wide], weights[:, :wide])

    parts = BLOCK // LANES
    done = base_ref[begin // LANES, 0] // BLOCK
    count = base_ref[end // LANES, 0]
    ready = count // BLOCK
    lax.fori_loop(done, ready, lambda block, carry: (one_block(block * parts, parts), carry)[1], 0)

    if closes:
        last = base_ref[end // LANES - 1, 0] // LANES
        for d in range(2, parts + 1):
            packed[last + d] = jnp.zeros(packed.shape[1:], packed.dtype)
        left = count - ready * BLOCK
        lane = iota((levels, LANES), 1)

        def contract(k):
            gradient = jnp.sum(cols[k] * projected[k * levels : (k + 1) * levels, :], axis=1, keepdims=True)
            result = jnp.where(lane == levels, gradient, 0.0)
            columns = {}
            for m, low, offset, size in spans:
                scaled = cols[k][low : low + size, :] * cols[k][m : m + 1, :]
                column = jnp.sum(moment[k, offset : offset + size, :] * scaled, axis=1, keepdims=True)
                columns.setdefault(m, []).append((low, column))
            for m, parts_of in columns.items():
                parts_of = sorted(parts_of, key=lambda part: part[0])
                low = parts_of[0][0]
                stack = [column for _, column in parts_of]
                if low:
                    stack = [jnp.zeros((low, 1), jnp.float32), *stack]
                result = jnp.where(lane == m, jnp.concatenate(stack, axis=0) if len(stack) > 1 else stack[0], result)
            terms_refs[k][...] = result

        @pl.when(left > BLOCK // 2)
        def _():
            one_block(ready * parts, parts)

        @pl.when((left > 0) & (left <= BLOCK // 2))
        def _():
            one_block(ready * parts, parts // 2)

        for k in range(3):
            contract(k)
    for copy in copies:
        copy.wait()


def chunk(base, place, here, measured, cols, carried, carrier, spans_of, sources, state, closes):
    levels, points = here.shape
    rays = measured.shape[0]
    _, _, _, pair_count = pair_rows(levels)
    opens = state is None
    smem = pl.BlockSpec(memory_space=pltpu.SMEM)
    vmem = pl.BlockSpec(memory_space=pltpu.VMEM)
    hbm = pl.BlockSpec(memory_space=pltpu.HBM)
    width = sum(w for _, w in spans_of)
    args = [base, place, here, measured, cols, *carried]
    specs = [smem] + [vmem] * 6
    for pair in sources:
        args += pair
        specs += [vmem, vmem]
    aliases = {}
    if not opens:
        aliases = {len(args) + n: n for n in range(4)}
        args += state
        specs += [hbm, vmem, vmem, vmem]
    shapes = [
        jax.ShapeDtypeStruct(measured.shape, jnp.float32),
        jax.ShapeDtypeStruct(((points + BLOCK) // LANES + 2, 3 * levels + rays, LANES), jnp.bfloat16),
        jax.ShapeDtypeStruct((3, pair_count, rays), jnp.float32),
        jax.ShapeDtypeStruct((3 * levels, rays), jnp.float32),
    ]
    out_specs = [hbm, vmem, vmem, vmem]
    if closes:
        shapes += [jax.ShapeDtypeStruct((levels, LANES), jnp.float32)] * 3
        out_specs += [vmem] * 3
    outs = pl.pallas_call(
        functools.partial(chunk_kernel, spans_of=spans_of, carrier=carrier, opens=opens, closes=closes),
        in_specs=specs,
        out_specs=out_specs,
        out_shape=shapes,
        scratch_shapes=[
            pltpu.VMEM((3 * levels + rays, width), jnp.bfloat16),
            pltpu.VMEM((rays, width), jnp.float32),
            pltpu.VMEM((3, pair_count, BLOCK), jnp.bfloat16),
            pltpu.VMEM((rays, BLOCK), jnp.bfloat16),
            pltpu.SemaphoreType.DMA((sum(pl.cdiv(w, PIECE) for _, w in spans_of),)),
        ],
        input_output_aliases=aliases,
        compiler_params=pltpu.CompilerParams(vmem_limit_bytes=CHUNK_BYTES),
        cost_estimate=CHEAP,
        name="chunk",
    )(*args)
    return outs[:4], outs[4:]


def quad_step(work, row, p):
    r = [work[p + i : p + i + 1, :] for i in range(4)]

    def entry(i, j):
        return jnp.broadcast_to(r[i][:, p + j : p + j + 1], r[i].shape)

    a, b, d = entry(0, 0), entry(0, 1), entry(1, 1)
    f0, f1, g0, g1 = entry(0, 2), entry(0, 3), entry(1, 2), entry(1, 3)
    h, q, v = entry(2, 2), entry(2, 3), entry(3, 3)
    inverse = 1.0 / (a * d - b * b)
    a, b, d = d * inverse, -b * inverse, a * inverse
    w00, w01 = a * f0 + b * g0, a * f1 + b * g1
    w10, w11 = b * f0 + d * g0, b * f1 + d * g1
    h, q, v = h - (f0 * w00 + g0 * w10), q - (f0 * w01 + g0 * w11), v - (f1 * w01 + g1 * w11)
    inverse = 1.0 / (h * v - q * q)
    h, q, v = v * inverse, -q * inverse, h * inverse
    t0, t1 = a * r[0] + b * r[1], b * r[0] + d * r[1]
    u0, u1 = r[2] - (f0 * t0 + g0 * t1), r[3] - (f1 * t0 + g1 * t1)
    s2, s3 = h * u0 + q * u1, q * u0 + v * u1
    s0, s1 = t0 - (w00 * s2 + w01 * s3), t1 - (w10 * s2 + w11 * s3)
    update = None
    for i, s in enumerate((s0, s1, s2, s3)):
        column = work[:, p + i : p + i + 1]
        term = jnp.where(row[:, :1] == p + i, column - 1.0, column) * s
        update = term if update is None else update + term
    return work - update


def solve_kernel(*refs, scale):
    parts = refs[:6]
    prior_ref, out_ref = refs[6:]
    levels = prior_ref.shape[1]
    total = parts[0][...]
    for part in parts[1:]:
        total = total + part[...]
    terms = total * scale
    row = iota((levels, LANES), 0)
    lane = iota((levels, LANES), 1)
    square = terms[:, :levels]
    flipped = jnp.concatenate([square.T, jnp.zeros((levels, LANES - levels), jnp.float32)], axis=1)
    lower = row // HALF >= lane // HALF
    work = jnp.where(lower | (lane >= levels), terms, flipped)
    diagonal = jnp.sum(jnp.where(row == lane, work, 0.0), axis=1, keepdims=True)
    mean = jnp.sum(diagonal, axis=0, keepdims=True) * (1.0 / levels) + 1e-06
    eye = iota((levels, levels), 0) == iota((levels, levels), 1)
    prior = jnp.sum(jnp.where(eye, prior_ref[...], 0.0), axis=1, keepdims=True)
    work = work + jnp.where(row == lane, prior * mean, 0.0)
    for p in range(0, levels, 4):
        work = quad_step(work, row, p)
    column = work[:, levels : levels + 1]
    out_ref[...] = -jnp.sum(jnp.where(eye, column, 0.0), axis=0, keepdims=True)


def solve(parts, prior_weight, scale):
    return pl.pallas_call(
        functools.partial(solve_kernel, scale=scale),
        out_shape=jax.ShapeDtypeStruct((1, prior_weight.shape[1]), jnp.float32),
        compiler_params=pltpu.CompilerParams(vmem_limit_bytes=SMALL_BYTES),
        cost_estimate=CHEAP,
        name="solve",
    )(*parts, prior_weight)


def swapped(block, axis):
    size = lax.axis_size(axis)
    return lax.ppermute(block, axis, [(i, size - 1 - i) for i in range(size)])


def shards(absorption, absorber, seg_level, seg_count, seg_length, measured, window_mask, prior_weight):
    table = absorption[0]
    levels, points = table.shape
    rays = measured.shape[1]
    unit = points // sum(WIDTHS)
    widths = [w * unit for w in WIDTHS]
    firsts = [sum(widths[:c]) for c in range(len(widths))]
    mask = window_mask.reshape(points // LANES, LANES)
    level = jnp.swapaxes(seg_level[0], 1, 2)
    length = jnp.swapaxes(seg_length[0], 1, 2)
    count = seg_count.reshape(3, 1, rays)
    first_send, second_send, cols = prepare(level, count, length, absorber, table, firsts[0], widths[0])
    carried = (traded(first_send, "sector", 0), traded(second_send, "sector", 1))
    place, base, table_here, measured_here, *sends = stage(cols, mask, table, measured[0], firsts[1:], widths[1:])
    base = base[:, :1]
    received = [carried]
    for c, send in enumerate(sends):
        if c:
            send, *arrived = lax.optimization_barrier((send, *received[c - 1]))
            received[c - 1] = tuple(arrived)
        received.append((traded(send, "sector", 0), traded(send, "sector", 1)))
    state = None
    carried = received[0]
    for c, span in enumerate(zip(firsts, widths, strict=True)):
        closes = c == len(widths) - 1
        state, terms = chunk(
            base, place, table_here, measured_here, cols, carried, widths[0], (span,), [received[c]], state, closes
        )
    spectrum = state[0]
    mine = (terms[1], traded(terms[0], "sector", 0), traded(terms[2], "sector", 1))
    others = tuple(swapped(part, "spec") for part in mine)
    scale = 1.0 / (rays * points * lax.axis_size("spec"))
    state_step = solve(mine + others, prior_weight[None, :], scale)
    return (spectrum[None], state_step)


def solution(mesh):
    return jax.shard_map(
        shards,
        mesh=mesh,
        in_specs=(
            P(("orbits", "sector"), None, "spec"),
            P(("orbits", "sector"), None),
            P(("orbits", "sector"), None, None, None),
            P(("orbits", "sector"), None, None),
            P(("orbits", "sector"), None, None, None),
            P(("orbits", "sector"), None, "spec"),
            P("spec"),
            P(),
        ),
        out_specs=(P(("orbits", "sector"), None, "spec"), P(("orbits", "sector"), None)),
        check_vma=False,
    )
```

```python
import functools

import jax
import jax.numpy as jnp
from jax import lax
from jax.experimental import pallas as pl
from jax.experimental.pallas import tpu as pltpu
from jax.sharding import PartitionSpec as P

LANES = 128
ROWS = 16
HALF = 8
PIECE = 512
BLOCK = 512
WIDTHS = (9, 14, 9)
SMALL_BYTES = 4 << 20
CHUNK_BYTES = 16 << 20
CHEAP = pl.CostEstimate(flops=1, transcendentals=0, bytes_accessed=1)


def traded(block, side):
    size, cores = lax.axis_size("sector"), lax.axis_size("spec")
    route = []
    for i in range(size):
        for core in range(cores):
            step = 1 if (i + core + side) % 2 == 0 else -1
            route.append((i * cores + core, (i + step) % size * cores + core))
    return lax.ppermute(block, ("sector", "spec"), route)


def iota(shape, dim):
    return lax.broadcasted_iota(jnp.int32, shape, dim)


def nt_dot(a, b):
    return lax.dot_general(a, b, (((1,), (1,)), ((), ())), preferred_element_type=jnp.float32)


def pinned(*arrays):
    return [pltpu.with_memory_space_constraint(array, pltpu.HBM) for array in arrays]


def prepare_kernel(level_hbm, count_hbm, length_hbm, absorber_hbm, table_hbm, *outs, first, width):
    first_ref, second_ref, cols_ref, level_ref, count_ref, length_ref, absorber_ref, sems = outs
    levels = absorber_ref.shape[1]
    sets, segs, rays = level_ref.shape
    arguments = ((level_hbm, level_ref), (length_hbm, length_ref), (count_hbm, count_ref), (absorber_hbm, absorber_ref))
    copies = [pltpu.make_async_copy(a, b, sems.at[n]) for n, (a, b) in enumerate(arguments)]
    for n, ref in enumerate((first_ref, second_ref)):
        source = table_hbm.at[:, pl.ds(first, width)]
        copies.append(pltpu.make_async_copy(source, ref.at[:, pl.ds(0, width)], sems.at[len(arguments) + n]))
    for copy in copies:
        copy.start()
    for copy in copies[: len(arguments)]:
        copy.wait()
    eye = iota((levels, levels), 0) == iota((levels, levels), 1)
    amount = jnp.sum(jnp.where(eye, absorber_ref[...], 0.0), axis=1, keepdims=True)
    level_of = iota((levels, rays), 0)
    odd = (lax.axis_index("sector") + lax.axis_index("spec")) % 2
    absorbed = []
    for k in range(sets):
        length = jnp.where(iota((segs, rays), 0) < count_ref[k], length_ref[k], 0.0)
        level = level_ref[k]
        path = jnp.zeros((levels, rays), jnp.float32)
        for j in range(segs):
            path += jnp.where(level[j : j + 1, :] == level_of, length[j : j + 1, :], 0.0)
        absorbed.append(path * amount)
    low, here, high = absorbed
    cols_ref[...] = here.astype(jnp.bfloat16)
    first_ref[:, width:] = jnp.where(odd == 1, low, high).astype(jnp.bfloat16)
    second_ref[:, width:] = jnp.where(odd == 1, high, low).astype(jnp.bfloat16)
    for copy in copies[len(arguments) :]:
        copy.wait()


def prepare(level, count, length, absorber, table, first, width):
    rays = level.shape[2]
    levels = absorber.shape[1]
    send = jax.ShapeDtypeStruct((levels, width + rays), jnp.bfloat16)
    hbm = pl.BlockSpec(memory_space=pltpu.HBM)
    return pl.pallas_call(
        functools.partial(prepare_kernel, first=first, width=width),
        in_specs=[hbm] * 5,
        out_shape=(send, send, jax.ShapeDtypeStruct((levels, rays), jnp.bfloat16)),
        scratch_shapes=[
            pltpu.VMEM(level.shape, level.dtype),
            pltpu.VMEM(count.shape, count.dtype),
            pltpu.VMEM(length.shape, length.dtype),
            pltpu.VMEM(absorber.shape, absorber.dtype),
            pltpu.SemaphoreType.DMA((6,)),
        ],
        compiler_params=pltpu.CompilerParams(vmem_limit_bytes=SMALL_BYTES),
        cost_estimate=CHEAP,
        name="prepare",
    )(*pinned(level, count, length, absorber, table))


def stage_kernel(cols_ref, mask_hbm, table_hbm, measured_hbm, place_ref, base_ref, table_ref, measured_ref, *rest, firsts):
    del cols_ref
    *sends, moment_ref, projected_ref, mask_ref, sems = rest
    moves = [(mask_hbm, mask_ref)]
    moves += [(table_hbm.at[:, pl.ds(first, ref.shape[1])], ref) for first, ref in zip(firsts, sends, strict=True)]
    moves += [(table_hbm, table_ref), (measured_hbm, measured_ref)]
    copies = [pltpu.make_async_copy(a, b, sems.at[n]) for n, (a, b) in enumerate(moves)]
    for copy in copies:
        copy.start()
    moment_ref[...] = jnp.zeros_like(moment_ref)
    projected_ref[...] = jnp.zeros_like(projected_ref)
    copies[0].wait()
    groups = mask_ref.shape[0]
    mask = mask_ref[...].astype(jnp.bfloat16)
    before = (iota((LANES, LANES), 0) < iota((LANES, LANES), 1)).astype(jnp.bfloat16)
    rank = jnp.dot(mask, before, preferred_element_type=jnp.float32)
    total = jnp.dot(mask, jnp.ones((LANES, LANES), jnp.bfloat16), preferred_element_type=jnp.float32)
    earlier = (iota((groups, groups), 1) < iota((groups, groups), 0)).astype(jnp.bfloat16)
    base = jnp.dot(earlier, total.astype(jnp.bfloat16), preferred_element_type=jnp.float32)
    place_ref[...] = jnp.where(mask_ref[...] > 0, (base + rank).astype(jnp.int32), -1)
    base_ref[pl.ds(0, groups), :] = base.astype(jnp.int32)
    last = base[groups - 1 : groups, :] + total[groups - 1 : groups, :]
    base_ref[pl.ds(groups, 8), :] = jnp.broadcast_to(last, (8, LANES)).astype(jnp.int32)
    for copy in copies[1:]:
        copy.wait()


def stage(cols, mask, table, measured, firsts, widths):
    groups = mask.shape[0]
    vmem = pl.BlockSpec(memory_space=pltpu.VMEM)
    hbm = pl.BlockSpec(memory_space=pltpu.HBM)
    return pl.pallas_call(
        functools.partial(stage_kernel, firsts=firsts),
        in_specs=[vmem, hbm, hbm, hbm],
        out_shape=(
            jax.ShapeDtypeStruct((groups, LANES), jnp.int32),
            jax.ShapeDtypeStruct((groups + 8, LANES), jnp.int32),
            jax.ShapeDtypeStruct(table.shape, table.dtype),
            jax.ShapeDtypeStruct(measured.shape, measured.dtype),
            *[jax.ShapeDtypeStruct((table.shape[0], width), table.dtype) for width in widths],
            jax.ShapeDtypeStruct((3, pair_rows(table.shape[0])[-1], measured.shape[0]), jnp.float32),
            jax.ShapeDtypeStruct((3 * table.shape[0], measured.shape[0]), jnp.float32),
        ),
        scratch_shapes=[pltpu.VMEM(mask.shape, mask.dtype), pltpu.SemaphoreType.DMA((3 + len(widths),))],
        compiler_params=pltpu.CompilerParams(vmem_limit_bytes=SMALL_BYTES),
        cost_estimate=CHEAP,
        name="stage",
    )(cols, *pinned(mask, table, measured))


def pair_rows(levels):
    whole = []
    shared = []
    spans = []
    offset = 0
    for m in range(levels):
        tile = ROWS * (m // ROWS)
        low = tile if m % ROWS < HALF else tile + ROWS
        if low < levels:
            whole.append((m, low, offset))
            spans.append((m, low, offset, levels - low))
            offset += levels - low
    for m in range(0, levels, 2):
        if m % ROWS >= HALF:
            low = ROWS * (m // ROWS) + HALF
            shared.append((m, low, offset))
            for n in range(2):
                spans.append((m + n, low, offset + n * HALF, HALF))
            offset += ROWS
    return whole, shared, spans, offset


def fill_pairs(target, k, lane, rows):
    levels = rows.shape[0]
    whole, shared, _, _ = pair_rows(levels)
    for m, low, offset in whole:
        target[k, offset : offset + levels - low, lane] = rows[low:, :] * rows[m : m + 1, :]
    upper = iota((ROWS, rows.shape[1]), 0) < HALF
    for m, low, offset in shared:
        half = rows[low : low + HALF, :]
        both = jnp.concatenate([half, half], axis=0)
        target[k, offset : offset + ROWS, lane] = both * jnp.where(upper, rows[m : m + 1, :], rows[m + 1 : m + 2, :])


def chunk_kernel(*refs, spans_of, carrier, opens, closes):
    base_ref, place_ref, here_ref, measured_ref, cols_ref, carried_before, carried_after = refs[:7]
    refs = refs[7:]
    sources = []
    for _ in spans_of:
        sources.append(refs[:2])
        refs = refs[2:]
    refs = refs[2:] if opens else refs[4:]
    spectrum_ref, packed, moment, projected = refs[:4]
    refs = refs[4:]
    if closes:
        terms_refs = refs[:3]
        refs = refs[3:]
    table, modelled, pairs, weights, sems = refs
    levels = here_ref.shape[0]
    rays = measured_ref.shape[0]
    high = 3 * levels
    begin = spans_of[0][0]
    end = spans_of[-1][0] + spans_of[-1][1]
    _, _, spans, pair_count = pair_rows(levels)
    cols = [ref.astype(jnp.float32) for ref in (carried_before[:, carrier:], cols_ref[...], carried_after[:, carrier:])]
    rows = jnp.concatenate([c.T for c in cols], axis=1).astype(jnp.bfloat16)

    if opens:
        packed[0] = jnp.zeros(packed.shape[1:], packed.dtype)

    copies = []
    for (first, width), (before_ref, after_ref) in zip(spans_of, sources, strict=True):
        for low_lane in range(0, width, PIECE):
            size = min(PIECE, width - low_lane)
            local = slice(low_lane, low_lane + size)
            overall = slice(first + low_lane, first + low_lane + size)
            inside = slice(first + low_lane - begin, first + low_lane - begin + size)
            table[0:levels, inside] = before_ref[:, local]
            table[levels : 2 * levels, inside] = here_ref[:, overall]
            table[2 * levels : high, inside] = after_ref[:, local]
            depth = jnp.dot(rows, table[:high, inside], preferred_element_type=jnp.float32)
            spectrum = jnp.exp(-depth)
            modelled[:, inside] = spectrum
            copy = pltpu.make_async_copy(modelled.at[:, inside], spectrum_ref.at[:, overall], sems.at[len(copies)])
            copy.start()
            copies.append(copy)
            table[high:, inside] = (spectrum * spectrum).astype(jnp.bfloat16)
            groups = range(overall.start // LANES, overall.stop // LANES)
            places = [place_ref[g : g + 1, :] for g in groups]
            kept = jnp.concatenate(places, axis=1) >= 0
            error = jnp.where(kept, (measured_ref[:, overall] - spectrum) * spectrum, 0.0).astype(jnp.bfloat16)
            projected[...] += nt_dot(table[:high, inside], error)
            for n, (g, place) in enumerate(zip(groups, places, strict=True)):
                at = base_ref[g, 0] // LANES
                chosen = (iota((2 * LANES, LANES), 0) + at * LANES == place).astype(jnp.bfloat16)
                moved = nt_dot(table[:, inside.start + n * LANES : inside.start + (n + 1) * LANES], chosen).astype(jnp.bfloat16)
                packed[at] = packed[at] + moved[:, :LANES]
                packed[at + 1] = moved[:, LANES:]

    def one_block(block, parts):
        wide = parts * LANES
        for p in range(parts):
            lane = slice(p * LANES, (p + 1) * LANES)
            weights[:, lane] = packed[block + p, high:, :]
            for k in range(3):
                fill_pairs(pairs, k, lane, packed[block + p, k * levels : (k + 1) * levels, :])
        for k in range(3):
            moment[k] += nt_dot(pairs[k, :, :wide], weights[:, :wide])

    parts = BLOCK // LANES
    done = base_ref[begin // LANES, 0] // BLOCK
    count = base_ref[end // LANES, 0]
    ready = count // BLOCK
    lax.fori_loop(done, ready, lambda block, carry: (one_block(block * parts, parts), carry)[1], 0)

    if closes:
        last = base_ref[end // LANES - 1, 0] // LANES
        for d in range(2, parts + 1):
            packed[last + d] = jnp.zeros(packed.shape[1:], packed.dtype)
        left = count - ready * BLOCK
        lane = iota((levels, LANES), 1)

        def contract(k):
            gradient = jnp.sum(cols[k] * projected[k * levels : (k + 1) * levels, :], axis=1, keepdims=True)
            result = jnp.where(lane == levels, gradient, 0.0)
            columns = {}
            for m, low, offset, size in spans:
                scaled = cols[k][low : low + size, :] * cols[k][m : m + 1, :]
                column = jnp.sum(moment[k, offset : offset + size, :] * scaled, axis=1, keepdims=True)
                columns.setdefault(m, []).append((low, column))
            for m, parts_of in columns.items():
                parts_of = sorted(parts_of, key=lambda part: part[0])
                low = parts_of[0][0]
                stack = [column for _, column in parts_of]
                if low:
                    stack = [jnp.zeros((low, 1), jnp.float32), *stack]
                result = jnp.where(lane == m, jnp.concatenate(stack, axis=0) if len(stack) > 1 else stack[0], result)
            terms_refs[k][...] = result

        @pl.when(left > BLOCK // 2)
        def _():
            one_block(ready * parts, parts)

        @pl.when((left > 0) & (left <= BLOCK // 2))
        def _():
            one_block(ready * parts, parts // 2)

        for k in range(3):
            contract(k)
    for copy in copies:
        copy.wait()


def chunk(base, place, here, measured, cols, carried, carrier, spans_of, sources, state, closes):
    levels, points = here.shape
    rays = measured.shape[0]
    _, _, _, pair_count = pair_rows(levels)
    opens = len(state) == 2
    smem = pl.BlockSpec(memory_space=pltpu.SMEM)
    vmem = pl.BlockSpec(memory_space=pltpu.VMEM)
    hbm = pl.BlockSpec(memory_space=pltpu.HBM)
    width = sum(w for _, w in spans_of)
    args = [base, place, here, measured, cols, *carried]
    specs = [smem] + [vmem] * 6
    for pair in sources:
        args += pair
        specs += [vmem, vmem]
    aliases = {}
    aliases = {len(args) + n: 4 - len(state) + n for n in range(len(state))}
    args += state
    specs += [hbm, vmem, vmem, vmem][4 - len(state) :]
    shapes = [
        jax.ShapeDtypeStruct(measured.shape, jnp.float32),
        jax.ShapeDtypeStruct(((points + BLOCK) // LANES + 2, 3 * levels + rays, LANES), jnp.bfloat16),
        jax.ShapeDtypeStruct((3, pair_count, rays), jnp.float32),
        jax.ShapeDtypeStruct((3 * levels, rays), jnp.float32),
    ]
    out_specs = [hbm, vmem, vmem, vmem]
    if closes:
        shapes += [jax.ShapeDtypeStruct((levels, LANES), jnp.float32)] * 3
        out_specs += [vmem] * 3
    outs = pl.pallas_call(
        functools.partial(chunk_kernel, spans_of=spans_of, carrier=carrier, opens=opens, closes=closes),
        in_specs=specs,
        out_specs=out_specs,
        out_shape=shapes,
        scratch_shapes=[
            pltpu.VMEM((3 * levels + rays, width), jnp.bfloat16),
            pltpu.VMEM((rays, width), jnp.float32),
            pltpu.VMEM((3, pair_count, BLOCK), jnp.bfloat16),
            pltpu.VMEM((rays, BLOCK), jnp.bfloat16),
            pltpu.SemaphoreType.DMA((sum(pl.cdiv(w, PIECE) for _, w in spans_of),)),
        ],
        input_output_aliases=aliases,
        compiler_params=pltpu.CompilerParams(vmem_limit_bytes=CHUNK_BYTES),
        cost_estimate=CHEAP,
        name="chunk",
    )(*args)
    return outs[:4], outs[4:]


def quad_step(work, row, p):
    r = [work[p + i : p + i + 1, :] for i in range(4)]

    def entry(i, j):
        return jnp.broadcast_to(r[i][:, p + j : p + j + 1], r[i].shape)

    a, b, d = entry(0, 0), entry(0, 1), entry(1, 1)
    f0, f1, g0, g1 = entry(0, 2), entry(0, 3), entry(1, 2), entry(1, 3)
    h, q, v = entry(2, 2), entry(2, 3), entry(3, 3)
    inverse = 1.0 / (a * d - b * b)
    a, b, d = d * inverse, -b * inverse, a * inverse
    w00, w01 = a * f0 + b * g0, a * f1 + b * g1
    w10, w11 = b * f0 + d * g0, b * f1 + d * g1
    h, q, v = h - (f0 * w00 + g0 * w10), q - (f0 * w01 + g0 * w11), v - (f1 * w01 + g1 * w11)
    inverse = 1.0 / (h * v - q * q)
    h, q, v = v * inverse, -q * inverse, h * inverse
    t0, t1 = a * r[0] + b * r[1], b * r[0] + d * r[1]
    u0, u1 = r[2] - (f0 * t0 + g0 * t1), r[3] - (f1 * t0 + g1 * t1)
    s2, s3 = h * u0 + q * u1, q * u0 + v * u1
    s0, s1 = t0 - (w00 * s2 + w01 * s3), t1 - (w10 * s2 + w11 * s3)
    update = None
    for i, s in enumerate((s0, s1, s2, s3)):
        column = work[:, p + i : p + i + 1]
        term = jnp.where(row[:, :1] == p + i, column - 1.0, column) * s
        update = term if update is None else update + term
    return work - update


def solve_kernel(*refs, scale):
    parts = refs[:6]
    prior_ref, out_ref = refs[6:]
    levels = prior_ref.shape[1]
    total = parts[0][...]
    for part in parts[1:]:
        total = total + part[...]
    terms = total * scale
    row = iota((levels, LANES), 0)
    lane = iota((levels, LANES), 1)
    square = terms[:, :levels]
    flipped = jnp.concatenate([square.T, jnp.zeros((levels, LANES - levels), jnp.float32)], axis=1)
    lower = row // HALF >= lane // HALF
    work = jnp.where(lower | (lane >= levels), terms, flipped)
    diagonal = jnp.sum(jnp.where(row == lane, work, 0.0), axis=1, keepdims=True)
    mean = jnp.sum(diagonal, axis=0, keepdims=True) * (1.0 / levels) + 1e-06
    eye = iota((levels, levels), 0) == iota((levels, levels), 1)
    prior = jnp.sum(jnp.where(eye, prior_ref[...], 0.0), axis=1, keepdims=True)
    work = work + jnp.where(row == lane, prior * mean, 0.0)
    for p in range(0, levels, 4):
        work = quad_step(work, row, p)
    column = work[:, levels : levels + 1]
    out_ref[...] = -jnp.sum(jnp.where(eye, column, 0.0), axis=0, keepdims=True)


def solve(parts, prior_weight, scale):
    return pl.pallas_call(
        functools.partial(solve_kernel, scale=scale),
        out_shape=jax.ShapeDtypeStruct((1, prior_weight.shape[1]), jnp.float32),
        compiler_params=pltpu.CompilerParams(vmem_limit_bytes=SMALL_BYTES),
        cost_estimate=CHEAP,
        name="solve",
    )(*parts, prior_weight)


def swapped(block, axis):
    size = lax.axis_size(axis)
    return lax.ppermute(block, axis, [(i, size - 1 - i) for i in range(size)])


def shards(absorption, absorber, seg_level, seg_count, seg_length, measured, window_mask, prior_weight):
    table = absorption[0]
    levels, points = table.shape
    rays = measured.shape[1]
    unit = points // sum(WIDTHS)
    widths = [w * unit for w in WIDTHS]
    firsts = [sum(widths[:c]) for c in range(len(widths))]
    mask = window_mask.reshape(points // LANES, LANES)
    level = jnp.swapaxes(seg_level[0], 1, 2)
    length = jnp.swapaxes(seg_length[0], 1, 2)
    count = seg_count.reshape(3, 1, rays)
    first_send, second_send, cols = prepare(level, count, length, absorber, table, firsts[0], widths[0])
    carried = (traded(first_send, 0), traded(second_send, 1))
    place, base, table_here, measured_here, *sends, moment, projected = stage(cols, mask, table, measured[0], firsts[1:], widths[1:])
    base = base[:, :1]
    received = [carried, (traded(sends[0], 0), traded(sends[0], 1))]
    state = (moment, projected)
    for c, span in enumerate(zip(firsts, widths, strict=True)):
        closes = c == len(widths) - 1
        if c + 2 < len(widths):
            send, *arrived = lax.optimization_barrier((sends[c + 1], *received[c]))
            received[c] = tuple(arrived)
            received.append((traded(send, 0), traded(send, 1)))
        state, terms = chunk(
            base, place, table_here, measured_here, cols, received[0], widths[0], (span,), [received[c]], state, closes
        )
    spectrum = state[0]
    mine = (terms[1], traded(terms[0], 0), traded(terms[2], 1))
    others = tuple(swapped(part, "spec") for part in mine)
    scale = 1.0 / (rays * points * lax.axis_size("spec"))
    state_step = solve(mine + others, prior_weight[None, :], scale)
    return (spectrum[None], state_step)


def solution(mesh):
    return jax.shard_map(
        shards,
        mesh=mesh,
        in_specs=(
            P(("orbits", "sector"), None, "spec"),
            P(("orbits", "sector"), None),
            P(("orbits", "sector"), None, None, None),
            P(("orbits", "sector"), None, None),
            P(("orbits", "sector"), None, None, None),
            P(("orbits", "sector"), None, "spec"),
            P("spec"),
            P(),
        ),
        out_specs=(P(("orbits", "sector"), None, "spec"), P(("orbits", "sector"), None)),
        check_vma=False,
    )
```

```python
import functools

import jax
import jax.numpy as jnp
from jax import lax
from jax.experimental import pallas as pl
from jax.experimental.pallas import tpu as pltpu
from jax.sharding import PartitionSpec as P

LANES = 128
ROWS = 16
HALF = 8
HERE = 1
AWAY = (0, 2)
PIECE = 512
BLOCK = 512
WIDTHS = (9, 14, 9)
SMALL_BYTES = 4 << 20
CHUNK_BYTES = 16 << 20
CHEAP = pl.CostEstimate(flops=1, transcendentals=0, bytes_accessed=1)


def traded(block, side):
    size, cores = lax.axis_size("sector"), lax.axis_size("spec")
    route = []
    for i in range(size):
        for core in range(cores):
            step = 1 if (i + core + side) % 2 == 0 else -1
            route.append((i * cores + core, (i + step) % size * cores + core))
    return lax.ppermute(block, ("sector", "spec"), route)


def iota(shape, dim):
    return lax.broadcasted_iota(jnp.int32, shape, dim)


def nt_dot(a, b):
    return lax.dot_general(a, b, (((1,), (1,)), ((), ())), preferred_element_type=jnp.float32)


def pinned(*arrays):
    return [pltpu.with_memory_space_constraint(array, pltpu.HBM) for array in arrays]


def prepare_kernel(level_hbm, count_hbm, length_hbm, absorber_hbm, table_hbm, *outs, first, width):
    first_ref, second_ref, cols_ref, level_ref, count_ref, length_ref, absorber_ref, sems = outs
    levels = absorber_ref.shape[1]
    sets, segs, rays = level_ref.shape
    arguments = ((level_hbm, level_ref), (length_hbm, length_ref), (count_hbm, count_ref), (absorber_hbm, absorber_ref))
    copies = [pltpu.make_async_copy(a, b, sems.at[n]) for n, (a, b) in enumerate(arguments)]
    for n, ref in enumerate((first_ref, second_ref)):
        source = table_hbm.at[:, pl.ds(first, width)]
        copies.append(pltpu.make_async_copy(source, ref.at[:, pl.ds(0, width)], sems.at[len(arguments) + n]))
    for copy in copies:
        copy.start()
    for copy in copies[: len(arguments)]:
        copy.wait()
    eye = iota((levels, levels), 0) == iota((levels, levels), 1)
    amount = jnp.sum(jnp.where(eye, absorber_ref[...], 0.0), axis=1, keepdims=True)
    level_of = iota((levels, rays), 0)
    odd = (lax.axis_index("sector") + lax.axis_index("spec")) % 2
    absorbed = []
    for k in range(sets):
        length = jnp.where(iota((segs, rays), 0) < count_ref[k], length_ref[k], 0.0)
        level = level_ref[k]
        path = jnp.zeros((levels, rays), jnp.float32)
        for j in range(segs):
            path += jnp.where(level[j : j + 1, :] == level_of, length[j : j + 1, :], 0.0)
        absorbed.append(path * amount)
    low, here, high = absorbed
    cols_ref[...] = here.astype(jnp.bfloat16)
    first_ref[:, width:] = jnp.where(odd == 1, low, high).astype(jnp.bfloat16)
    second_ref[:, width:] = jnp.where(odd == 1, high, low).astype(jnp.bfloat16)
    for copy in copies[len(arguments) :]:
        copy.wait()


def prepare(level, count, length, absorber, table, first, width):
    rays = level.shape[2]
    levels = absorber.shape[1]
    send = jax.ShapeDtypeStruct((levels, width + rays), jnp.bfloat16)
    hbm = pl.BlockSpec(memory_space=pltpu.HBM)
    return pl.pallas_call(
        functools.partial(prepare_kernel, first=first, width=width),
        in_specs=[hbm] * 5,
        out_shape=(send, send, jax.ShapeDtypeStruct((levels, rays), jnp.bfloat16)),
        scratch_shapes=[
            pltpu.VMEM(level.shape, level.dtype),
            pltpu.VMEM(count.shape, count.dtype),
            pltpu.VMEM(length.shape, length.dtype),
            pltpu.VMEM(absorber.shape, absorber.dtype),
            pltpu.SemaphoreType.DMA((6,)),
        ],
        compiler_params=pltpu.CompilerParams(vmem_limit_bytes=SMALL_BYTES),
        cost_estimate=CHEAP,
        name="prepare",
    )(*pinned(level, count, length, absorber, table))


def stage_kernel(cols_ref, mask_hbm, table_hbm, measured_hbm, place_ref, base_ref, table_ref, measured_ref, *rest, firsts):
    del cols_ref
    *sends, moment_ref, projected_ref, mask_ref, sems = rest
    moves = [(mask_hbm, mask_ref)]
    moves += [(table_hbm.at[:, pl.ds(first, ref.shape[1])], ref) for first, ref in zip(firsts, sends, strict=True)]
    moves += [(table_hbm, table_ref), (measured_hbm, measured_ref)]
    copies = [pltpu.make_async_copy(a, b, sems.at[n]) for n, (a, b) in enumerate(moves)]
    for copy in copies:
        copy.start()
    moment_ref[...] = jnp.zeros_like(moment_ref)
    projected_ref[...] = jnp.zeros_like(projected_ref)
    copies[0].wait()
    groups = mask_ref.shape[0]
    mask = mask_ref[...].astype(jnp.bfloat16)
    before = (iota((LANES, LANES), 0) < iota((LANES, LANES), 1)).astype(jnp.bfloat16)
    rank = jnp.dot(mask, before, preferred_element_type=jnp.float32)
    total = jnp.dot(mask, jnp.ones((LANES, LANES), jnp.bfloat16), preferred_element_type=jnp.float32)
    earlier = (iota((groups, groups), 1) < iota((groups, groups), 0)).astype(jnp.bfloat16)
    base = jnp.dot(earlier, total.astype(jnp.bfloat16), preferred_element_type=jnp.float32)
    place_ref[...] = jnp.where(mask_ref[...] > 0, (base + rank).astype(jnp.int32), -1)
    base_ref[pl.ds(0, groups), :] = base.astype(jnp.int32)
    last = base[groups - 1 : groups, :] + total[groups - 1 : groups, :]
    base_ref[pl.ds(groups, 8), :] = jnp.broadcast_to(last, (8, LANES)).astype(jnp.int32)
    for copy in copies[1:]:
        copy.wait()


def stage(cols, mask, table, measured, firsts, widths):
    groups = mask.shape[0]
    vmem = pl.BlockSpec(memory_space=pltpu.VMEM)
    hbm = pl.BlockSpec(memory_space=pltpu.HBM)
    return pl.pallas_call(
        functools.partial(stage_kernel, firsts=firsts),
        in_specs=[vmem, hbm, hbm, hbm],
        out_shape=(
            jax.ShapeDtypeStruct((groups, LANES), jnp.int32),
            jax.ShapeDtypeStruct((groups + 8, LANES), jnp.int32),
            jax.ShapeDtypeStruct(table.shape, table.dtype),
            jax.ShapeDtypeStruct(measured.shape, measured.dtype),
            *[jax.ShapeDtypeStruct((table.shape[0], width), table.dtype) for width in widths],
            jax.ShapeDtypeStruct((3, pair_rows(table.shape[0])[-1], measured.shape[0]), jnp.float32),
            jax.ShapeDtypeStruct((3 * table.shape[0], measured.shape[0]), jnp.float32),
        ),
        scratch_shapes=[pltpu.VMEM(mask.shape, mask.dtype), pltpu.SemaphoreType.DMA((3 + len(widths),))],
        compiler_params=pltpu.CompilerParams(vmem_limit_bytes=SMALL_BYTES),
        cost_estimate=CHEAP,
        name="stage",
    )(cols, *pinned(mask, table, measured))


def pair_rows(levels):
    whole = []
    shared = []
    spans = []
    offset = 0
    for m in range(levels):
        tile = ROWS * (m // ROWS)
        low = tile if m % ROWS < HALF else tile + ROWS
        if low < levels:
            whole.append((m, low, offset))
            spans.append((m, low, offset, levels - low))
            offset += levels - low
    for m in range(0, levels, 2):
        if m % ROWS >= HALF:
            low = ROWS * (m // ROWS) + HALF
            shared.append((m, low, offset))
            for n in range(2):
                spans.append((m + n, low, offset + n * HALF, HALF))
            offset += ROWS
    return whole, shared, spans, offset


def fill_pairs(target, k, lane, rows):
    levels = rows.shape[0]
    whole, shared, _, _ = pair_rows(levels)
    for m, low, offset in whole:
        target[k, offset : offset + levels - low, lane] = rows[low:, :] * rows[m : m + 1, :]
    upper = iota((ROWS, rows.shape[1]), 0) < HALF
    for m, low, offset in shared:
        half = rows[low : low + HALF, :]
        both = jnp.concatenate([half, half], axis=0)
        target[k, offset : offset + ROWS, lane] = both * jnp.where(upper, rows[m : m + 1, :], rows[m + 1 : m + 2, :])


def contracted(cols, projected, moment, k):
    levels = cols.shape[0]
    _, _, spans, _ = pair_rows(levels)
    lane = iota((levels, LANES), 1)
    gradient = jnp.sum(cols * projected, axis=1, keepdims=True)
    result = jnp.where(lane == levels, gradient, 0.0)
    columns = {}
    for m, low, offset, size in spans:
        scaled = cols[low : low + size, :] * cols[m : m + 1, :]
        column = jnp.sum(moment[k, offset : offset + size, :] * scaled, axis=1, keepdims=True)
        columns.setdefault(m, []).append((low, column))
    for m, found in columns.items():
        found = sorted(found, key=lambda part: part[0])
        low = found[0][0]
        stack = [column for _, column in found]
        if low:
            stack = [jnp.zeros((low, 1), jnp.float32), *stack]
        result = jnp.where(lane == m, jnp.concatenate(stack, axis=0) if len(stack) > 1 else stack[0], result)
    return result


def finish_kernel(base_ref, cols_ref, packed, projected, out_ref, pairs, weights, moment, *, groups):
    levels = cols_ref.shape[0]
    high = 3 * levels
    parts = BLOCK // LANES
    moment[...] = jnp.zeros_like(moment)

    def one_block(block, parts):
        wide = parts * LANES
        for p in range(parts):
            lane = slice(p * LANES, (p + 1) * LANES)
            weights[:, lane] = packed[block + p, high:, :]
            fill_pairs(pairs, 0, lane, packed[block + p, HERE * levels : (HERE + 1) * levels, :])
        moment[0] += nt_dot(pairs[0, :, :wide], weights[:, :wide])

    count = base_ref[groups, 0]
    ready = count // BLOCK
    lax.fori_loop(0, ready, lambda block, carry: (one_block(block * parts, parts), carry)[1], 0)
    left = count - ready * BLOCK

    @pl.when(left > BLOCK // 2)
    def _():
        one_block(ready * parts, parts)

    @pl.when((left > 0) & (left <= BLOCK // 2))
    def _():
        one_block(ready * parts, parts // 2)

    cols = cols_ref[...].astype(jnp.float32)
    out_ref[...] = contracted(cols, projected[HERE * levels : (HERE + 1) * levels, :], moment, 0)


def finish(base, cols, packed, projected, groups):
    levels, rays = cols.shape
    _, _, _, pair_count = pair_rows(levels)
    vmem = pl.BlockSpec(memory_space=pltpu.VMEM)
    return pl.pallas_call(
        functools.partial(finish_kernel, groups=groups),
        in_specs=[pl.BlockSpec(memory_space=pltpu.SMEM), vmem, vmem, vmem],
        out_shape=jax.ShapeDtypeStruct((levels, LANES), jnp.float32),
        scratch_shapes=[
            pltpu.VMEM((1, pair_count, BLOCK), jnp.bfloat16),
            pltpu.VMEM((rays, BLOCK), jnp.bfloat16),
            pltpu.VMEM((1, pair_count, rays), jnp.float32),
        ],
        compiler_params=pltpu.CompilerParams(vmem_limit_bytes=CHUNK_BYTES),
        cost_estimate=CHEAP,
        name="finish",
    )(base, cols, packed, projected)


def chunk_kernel(*refs, spans_of, carrier, opens, closes):
    base_ref, place_ref, here_ref, measured_ref, cols_ref, carried_before, carried_after = refs[:7]
    refs = refs[7:]
    sources = []
    for _ in spans_of:
        sources.append(refs[:2])
        refs = refs[2:]
    refs = refs[2:] if opens else refs[4:]
    spectrum_ref, packed, moment, projected = refs[:4]
    refs = refs[4:]
    if closes:
        terms_refs = refs[:2]
        refs = refs[2:]
    table, modelled, pairs, weights, sems = refs
    levels = here_ref.shape[0]
    rays = measured_ref.shape[0]
    high = 3 * levels
    begin = spans_of[0][0]
    end = spans_of[-1][0] + spans_of[-1][1]
    _, _, spans, pair_count = pair_rows(levels)
    cols = [ref.astype(jnp.float32) for ref in (carried_before[:, carrier:], cols_ref[...], carried_after[:, carrier:])]
    rows = jnp.concatenate([c.T for c in cols], axis=1).astype(jnp.bfloat16)

    if opens:
        packed[0] = jnp.zeros(packed.shape[1:], packed.dtype)

    copies = []
    for (first, width), (before_ref, after_ref) in zip(spans_of, sources, strict=True):
        for low_lane in range(0, width, PIECE):
            size = min(PIECE, width - low_lane)
            local = slice(low_lane, low_lane + size)
            overall = slice(first + low_lane, first + low_lane + size)
            inside = slice(first + low_lane - begin, first + low_lane - begin + size)
            table[0:levels, inside] = before_ref[:, local]
            table[levels : 2 * levels, inside] = here_ref[:, overall]
            table[2 * levels : high, inside] = after_ref[:, local]
            depth = jnp.dot(rows, table[:high, inside], preferred_element_type=jnp.float32)
            spectrum = jnp.exp(-depth)
            modelled[:, inside] = spectrum
            copy = pltpu.make_async_copy(modelled.at[:, inside], spectrum_ref.at[:, overall], sems.at[len(copies)])
            copy.start()
            copies.append(copy)
            table[high:, inside] = (spectrum * spectrum).astype(jnp.bfloat16)
            groups = range(overall.start // LANES, overall.stop // LANES)
            places = [place_ref[g : g + 1, :] for g in groups]
            kept = jnp.concatenate(places, axis=1) >= 0
            error = jnp.where(kept, (measured_ref[:, overall] - spectrum) * spectrum, 0.0).astype(jnp.bfloat16)
            projected[...] += nt_dot(table[:high, inside], error)
            for n, (g, place) in enumerate(zip(groups, places, strict=True)):
                at = base_ref[g, 0] // LANES
                chosen = (iota((2 * LANES, LANES), 0) + at * LANES == place).astype(jnp.bfloat16)
                moved = nt_dot(table[:, inside.start + n * LANES : inside.start + (n + 1) * LANES], chosen).astype(jnp.bfloat16)
                packed[at] = packed[at] + moved[:, :LANES]
                packed[at + 1] = moved[:, LANES:]

    def one_block(block, parts):
        wide = parts * LANES
        for p in range(parts):
            lane = slice(p * LANES, (p + 1) * LANES)
            weights[:, lane] = packed[block + p, high:, :]
            for k in AWAY:
                fill_pairs(pairs, k, lane, packed[block + p, k * levels : (k + 1) * levels, :])
        for k in AWAY:
            moment[k] += nt_dot(pairs[k, :, :wide], weights[:, :wide])

    parts = BLOCK // LANES
    done = base_ref[begin // LANES, 0] // BLOCK
    count = base_ref[end // LANES, 0]
    ready = count // BLOCK
    lax.fori_loop(done, ready, lambda block, carry: (one_block(block * parts, parts), carry)[1], 0)

    if closes:
        last = base_ref[end // LANES - 1, 0] // LANES
        for d in range(2, parts + 1):
            packed[last + d] = jnp.zeros(packed.shape[1:], packed.dtype)
        left = count - ready * BLOCK
        @pl.when(left > BLOCK // 2)
        def _():
            one_block(ready * parts, parts)

        @pl.when((left > 0) & (left <= BLOCK // 2))
        def _():
            one_block(ready * parts, parts // 2)

        for terms_ref, k in zip(terms_refs, AWAY, strict=True):
            terms_ref[...] = contracted(cols[k], projected[k * levels : (k + 1) * levels, :], moment, k)
    for copy in copies:
        copy.wait()


def chunk(base, place, here, measured, cols, carried, carrier, spans_of, sources, state, closes):
    levels, points = here.shape
    rays = measured.shape[0]
    _, _, _, pair_count = pair_rows(levels)
    opens = len(state) == 2
    smem = pl.BlockSpec(memory_space=pltpu.SMEM)
    vmem = pl.BlockSpec(memory_space=pltpu.VMEM)
    hbm = pl.BlockSpec(memory_space=pltpu.HBM)
    width = sum(w for _, w in spans_of)
    args = [base, place, here, measured, cols, *carried]
    specs = [smem] + [vmem] * 6
    for pair in sources:
        args += pair
        specs += [vmem, vmem]
    aliases = {}
    aliases = {len(args) + n: 4 - len(state) + n for n in range(len(state))}
    args += state
    specs += [hbm, vmem, vmem, vmem][4 - len(state) :]
    shapes = [
        jax.ShapeDtypeStruct(measured.shape, jnp.float32),
        jax.ShapeDtypeStruct(((points + BLOCK) // LANES + 2, 3 * levels + rays, LANES), jnp.bfloat16),
        jax.ShapeDtypeStruct((3, pair_count, rays), jnp.float32),
        jax.ShapeDtypeStruct((3 * levels, rays), jnp.float32),
    ]
    out_specs = [hbm, vmem, vmem, vmem]
    if closes:
        shapes += [jax.ShapeDtypeStruct((levels, LANES), jnp.float32)] * 2
        out_specs += [vmem] * 2
    outs = pl.pallas_call(
        functools.partial(chunk_kernel, spans_of=spans_of, carrier=carrier, opens=opens, closes=closes),
        in_specs=specs,
        out_specs=out_specs,
        out_shape=shapes,
        scratch_shapes=[
            pltpu.VMEM((3 * levels + rays, width), jnp.bfloat16),
            pltpu.VMEM((rays, width), jnp.float32),
            pltpu.VMEM((3, pair_count, BLOCK), jnp.bfloat16),
            pltpu.VMEM((rays, BLOCK), jnp.bfloat16),
            pltpu.SemaphoreType.DMA((sum(pl.cdiv(w, PIECE) for _, w in spans_of),)),
        ],
        input_output_aliases=aliases,
        compiler_params=pltpu.CompilerParams(vmem_limit_bytes=CHUNK_BYTES),
        cost_estimate=CHEAP,
        name="chunk",
    )(*args)
    return outs[:4], outs[4:]


def quad_step(work, row, p):
    r = [work[p + i : p + i + 1, :] for i in range(4)]

    def entry(i, j):
        return jnp.broadcast_to(r[i][:, p + j : p + j + 1], r[i].shape)

    a, b, d = entry(0, 0), entry(0, 1), entry(1, 1)
    f0, f1, g0, g1 = entry(0, 2), entry(0, 3), entry(1, 2), entry(1, 3)
    h, q, v = entry(2, 2), entry(2, 3), entry(3, 3)
    inverse = 1.0 / (a * d - b * b)
    a, b, d = d * inverse, -b * inverse, a * inverse
    w00, w01 = a * f0 + b * g0, a * f1 + b * g1
    w10, w11 = b * f0 + d * g0, b * f1 + d * g1
    h, q, v = h - (f0 * w00 + g0 * w10), q - (f0 * w01 + g0 * w11), v - (f1 * w01 + g1 * w11)
    inverse = 1.0 / (h * v - q * q)
    h, q, v = v * inverse, -q * inverse, h * inverse
    t0, t1 = a * r[0] + b * r[1], b * r[0] + d * r[1]
    u0, u1 = r[2] - (f0 * t0 + g0 * t1), r[3] - (f1 * t0 + g1 * t1)
    s2, s3 = h * u0 + q * u1, q * u0 + v * u1
    s0, s1 = t0 - (w00 * s2 + w01 * s3), t1 - (w10 * s2 + w11 * s3)
    update = None
    for i, s in enumerate((s0, s1, s2, s3)):
        column = work[:, p + i : p + i + 1]
        term = jnp.where(row[:, :1] == p + i, column - 1.0, column) * s
        update = term if update is None else update + term
    return work - update


def solve_kernel(*refs, scale):
    parts = refs[:6]
    prior_ref, out_ref = refs[6:]
    levels = prior_ref.shape[1]
    total = parts[0][...]
    for part in parts[1:]:
        total = total + part[...]
    terms = total * scale
    row = iota((levels, LANES), 0)
    lane = iota((levels, LANES), 1)
    square = terms[:, :levels]
    flipped = jnp.concatenate([square.T, jnp.zeros((levels, LANES - levels), jnp.float32)], axis=1)
    lower = row // HALF >= lane // HALF
    work = jnp.where(lower | (lane >= levels), terms, flipped)
    diagonal = jnp.sum(jnp.where(row == lane, work, 0.0), axis=1, keepdims=True)
    mean = jnp.sum(diagonal, axis=0, keepdims=True) * (1.0 / levels) + 1e-06
    eye = iota((levels, levels), 0) == iota((levels, levels), 1)
    prior = jnp.sum(jnp.where(eye, prior_ref[...], 0.0), axis=1, keepdims=True)
    work = work + jnp.where(row == lane, prior * mean, 0.0)
    for p in range(0, levels, 4):
        work = quad_step(work, row, p)
    column = work[:, levels : levels + 1]
    out_ref[...] = -jnp.sum(jnp.where(eye, column, 0.0), axis=0, keepdims=True)


def solve(parts, prior_weight, scale):
    return pl.pallas_call(
        functools.partial(solve_kernel, scale=scale),
        out_shape=jax.ShapeDtypeStruct((1, prior_weight.shape[1]), jnp.float32),
        compiler_params=pltpu.CompilerParams(vmem_limit_bytes=SMALL_BYTES),
        cost_estimate=CHEAP,
        name="solve",
    )(*parts, prior_weight)


def swapped(block, axis):
    size = lax.axis_size(axis)
    return lax.ppermute(block, axis, [(i, size - 1 - i) for i in range(size)])


def shards(absorption, absorber, seg_level, seg_count, seg_length, measured, window_mask, prior_weight):
    table = absorption[0]
    levels, points = table.shape
    rays = measured.shape[1]
    unit = points // sum(WIDTHS)
    widths = [w * unit for w in WIDTHS]
    firsts = [sum(widths[:c]) for c in range(len(widths))]
    mask = window_mask.reshape(points // LANES, LANES)
    level = jnp.swapaxes(seg_level[0], 1, 2)
    length = jnp.swapaxes(seg_length[0], 1, 2)
    count = seg_count.reshape(3, 1, rays)
    first_send, second_send, cols = prepare(level, count, length, absorber, table, firsts[0], widths[0])
    carried = (traded(first_send, 0), traded(second_send, 1))
    place, base, table_here, measured_here, *sends, moment, projected = stage(cols, mask, table, measured[0], firsts[1:], widths[1:])
    base = base[:, :1]
    received = [carried, (traded(sends[0], 0), traded(sends[0], 1))]
    state = (moment, projected)
    for c, span in enumerate(zip(firsts, widths, strict=True)):
        closes = c == len(widths) - 1
        if c + 2 < len(widths):
            send, *arrived = lax.optimization_barrier((sends[c + 1], *received[c]))
            received[c] = tuple(arrived)
            received.append((traded(send, 0), traded(send, 1)))
        state, terms = chunk(
            base, place, table_here, measured_here, cols, received[0], widths[0], (span,), [received[c]], state, closes
        )
    spectrum = state[0]
    arriving = (traded(terms[0], 0), traded(terms[1], 1))
    mine = (finish(base, cols, state[1], state[3], points // LANES), *arriving)
    others = tuple(swapped(part, "spec") for part in mine)
    scale = 1.0 / (rays * points * lax.axis_size("spec"))
    state_step = solve(mine + others, prior_weight[None, :], scale)
    return (spectrum[None], state_step)


def solution(mesh):
    return jax.shard_map(
        shards,
        mesh=mesh,
        in_specs=(
            P(("orbits", "sector"), None, "spec"),
            P(("orbits", "sector"), None),
            P(("orbits", "sector"), None, None, None),
            P(("orbits", "sector"), None, None),
            P(("orbits", "sector"), None, None, None),
            P(("orbits", "sector"), None, "spec"),
            P("spec"),
            P(),
        ),
        out_specs=(P(("orbits", "sector"), None, "spec"), P(("orbits", "sector"), None)),
        check_vma=False,
    )
```

```python
import functools

import jax
import jax.numpy as jnp
from jax import lax
from jax.experimental import pallas as pl
from jax.experimental.pallas import tpu as pltpu
from jax.sharding import PartitionSpec as P

LANES = 128
ROWS = 16
HALF = 8
HERE = 1
AWAY = (0, 2)
PIECE = 512
BLOCK = 512
WIDTHS = (9, 14, 9)
SMALL_BYTES = 4 << 20
CHUNK_BYTES = 16 << 20
CHEAP = pl.CostEstimate(flops=1, transcendentals=0, bytes_accessed=1)


def traded(block, side):
    size, cores = lax.axis_size("sector"), lax.axis_size("spec")
    route = []
    for i in range(size):
        for core in range(cores):
            step = 1 if (i + core + side) % 2 == 0 else -1
            route.append((i * cores + core, (i + step) % size * cores + core))
    return lax.ppermute(block, ("sector", "spec"), route)


def iota(shape, dim):
    return lax.broadcasted_iota(jnp.int32, shape, dim)


def nt_dot(a, b):
    return lax.dot_general(a, b, (((1,), (1,)), ((), ())), preferred_element_type=jnp.float32)


def pinned(*arrays):
    return [pltpu.with_memory_space_constraint(array, pltpu.HBM) for array in arrays]


def prepare_kernel(level_hbm, count_hbm, length_hbm, absorber_hbm, table_hbm, *outs, first, width):
    first_ref, second_ref, cols_ref, level_ref, count_ref, length_ref, absorber_ref, sems = outs
    levels = absorber_ref.shape[1]
    sets, segs, rays = level_ref.shape
    arguments = ((level_hbm, level_ref), (length_hbm, length_ref), (count_hbm, count_ref), (absorber_hbm, absorber_ref))
    copies = [pltpu.make_async_copy(a, b, sems.at[n]) for n, (a, b) in enumerate(arguments)]
    for n, ref in enumerate((first_ref, second_ref)):
        source = table_hbm.at[:, pl.ds(first, width)]
        copies.append(pltpu.make_async_copy(source, ref.at[:, pl.ds(0, width)], sems.at[len(arguments) + n]))
    for copy in copies:
        copy.start()
    for copy in copies[: len(arguments)]:
        copy.wait()
    eye = iota((levels, levels), 0) == iota((levels, levels), 1)
    amount = jnp.sum(jnp.where(eye, absorber_ref[...], 0.0), axis=1, keepdims=True)
    level_of = iota((levels, rays), 0)
    odd = (lax.axis_index("sector") + lax.axis_index("spec")) % 2
    absorbed = []
    for k in range(sets):
        length = jnp.where(iota((segs, rays), 0) < count_ref[k], length_ref[k], 0.0)
        level = level_ref[k]
        path = jnp.zeros((levels, rays), jnp.float32)
        for j in range(segs):
            path += jnp.where(level[j : j + 1, :] == level_of, length[j : j + 1, :], 0.0)
        absorbed.append(path * amount)
    low, here, high = absorbed
    cols_ref[...] = here.astype(jnp.bfloat16)
    first_ref[:, width:] = jnp.where(odd == 1, low, high).astype(jnp.bfloat16)
    second_ref[:, width:] = jnp.where(odd == 1, high, low).astype(jnp.bfloat16)
    for copy in copies[len(arguments) :]:
        copy.wait()


def prepare(level, count, length, absorber, table, first, width):
    rays = level.shape[2]
    levels = absorber.shape[1]
    send = jax.ShapeDtypeStruct((levels, width + rays), jnp.bfloat16)
    hbm = pl.BlockSpec(memory_space=pltpu.HBM)
    return pl.pallas_call(
        functools.partial(prepare_kernel, first=first, width=width),
        in_specs=[hbm] * 5,
        out_shape=(send, send, jax.ShapeDtypeStruct((levels, rays), jnp.bfloat16)),
        scratch_shapes=[
            pltpu.VMEM(level.shape, level.dtype),
            pltpu.VMEM(count.shape, count.dtype),
            pltpu.VMEM(length.shape, length.dtype),
            pltpu.VMEM(absorber.shape, absorber.dtype),
            pltpu.SemaphoreType.DMA((6,)),
        ],
        compiler_params=pltpu.CompilerParams(vmem_limit_bytes=SMALL_BYTES),
        cost_estimate=CHEAP,
        name="prepare",
    )(*pinned(level, count, length, absorber, table))


def stage_kernel(cols_ref, mask_hbm, table_hbm, measured_hbm, place_ref, base_ref, table_ref, measured_ref, *rest, firsts):
    del cols_ref
    *sends, moment_ref, projected_ref, mask_ref, sems = rest
    moves = [(mask_hbm, mask_ref)]
    moves += [(table_hbm.at[:, pl.ds(first, ref.shape[1])], ref) for first, ref in zip(firsts, sends, strict=True)]
    moves += [(table_hbm, table_ref), (measured_hbm, measured_ref)]
    copies = [pltpu.make_async_copy(a, b, sems.at[n]) for n, (a, b) in enumerate(moves)]
    for copy in copies:
        copy.start()
    moment_ref[...] = jnp.zeros_like(moment_ref)
    projected_ref[...] = jnp.zeros_like(projected_ref)
    copies[0].wait()
    groups = mask_ref.shape[0]
    mask = mask_ref[...].astype(jnp.bfloat16)
    before = (iota((LANES, LANES), 0) < iota((LANES, LANES), 1)).astype(jnp.bfloat16)
    rank = jnp.dot(mask, before, preferred_element_type=jnp.float32)
    total = jnp.dot(mask, jnp.ones((LANES, LANES), jnp.bfloat16), preferred_element_type=jnp.float32)
    earlier = (iota((groups, groups), 1) < iota((groups, groups), 0)).astype(jnp.bfloat16)
    base = jnp.dot(earlier, total.astype(jnp.bfloat16), preferred_element_type=jnp.float32)
    place_ref[...] = jnp.where(mask_ref[...] > 0, (base + rank).astype(jnp.int32), -1)
    base_ref[pl.ds(0, groups), :] = base.astype(jnp.int32)
    last = base[groups - 1 : groups, :] + total[groups - 1 : groups, :]
    base_ref[pl.ds(groups, 8), :] = jnp.broadcast_to(last, (8, LANES)).astype(jnp.int32)
    for copy in copies[1:]:
        copy.wait()


def stage(cols, mask, table, measured, firsts, widths):
    groups = mask.shape[0]
    vmem = pl.BlockSpec(memory_space=pltpu.VMEM)
    hbm = pl.BlockSpec(memory_space=pltpu.HBM)
    return pl.pallas_call(
        functools.partial(stage_kernel, firsts=firsts),
        in_specs=[vmem, hbm, hbm, hbm],
        out_shape=(
            jax.ShapeDtypeStruct((groups, LANES), jnp.int32),
            jax.ShapeDtypeStruct((groups + 8, LANES), jnp.int32),
            jax.ShapeDtypeStruct(table.shape, table.dtype),
            jax.ShapeDtypeStruct(measured.shape, measured.dtype),
            *[jax.ShapeDtypeStruct((table.shape[0], width), table.dtype) for width in widths],
            jax.ShapeDtypeStruct((3, pair_rows(table.shape[0])[-1], measured.shape[0]), jnp.float32),
            jax.ShapeDtypeStruct((3 * table.shape[0], measured.shape[0]), jnp.float32),
        ),
        scratch_shapes=[pltpu.VMEM(mask.shape, mask.dtype), pltpu.SemaphoreType.DMA((3 + len(widths),))],
        compiler_params=pltpu.CompilerParams(vmem_limit_bytes=SMALL_BYTES),
        cost_estimate=CHEAP,
        name="stage",
    )(cols, *pinned(mask, table, measured))


def pair_rows(levels):
    whole = []
    shared = []
    spans = []
    offset = 0
    for m in range(levels):
        tile = ROWS * (m // ROWS)
        low = tile if m % ROWS < HALF else tile + ROWS
        if low < levels:
            whole.append((m, low, offset))
            spans.append((m, low, offset, levels - low))
            offset += levels - low
    for m in range(0, levels, 2):
        if m % ROWS >= HALF:
            low = ROWS * (m // ROWS) + HALF
            shared.append((m, low, offset))
            for n in range(2):
                spans.append((m + n, low, offset + n * HALF, HALF))
            offset += ROWS
    return whole, shared, spans, offset


def fill_pairs(target, k, lane, rows):
    levels = rows.shape[0]
    whole, shared, _, _ = pair_rows(levels)
    for m, low, offset in whole:
        target[k, offset : offset + levels - low, lane] = rows[low:, :] * rows[m : m + 1, :]
    upper = iota((ROWS, rows.shape[1]), 0) < HALF
    for m, low, offset in shared:
        half = rows[low : low + HALF, :]
        both = jnp.concatenate([half, half], axis=0)
        target[k, offset : offset + ROWS, lane] = both * jnp.where(upper, rows[m : m + 1, :], rows[m + 1 : m + 2, :])


def contracted(cols, projected, moment, k):
    levels = cols.shape[0]
    _, _, spans, _ = pair_rows(levels)
    lane = iota((levels, LANES), 1)
    gradient = jnp.sum(cols * projected, axis=1, keepdims=True)
    result = jnp.where(lane == levels, gradient, 0.0)
    columns = {}
    for m, low, offset, size in spans:
        scaled = cols[low : low + size, :] * cols[m : m + 1, :]
        column = jnp.sum(moment[k, offset : offset + size, :] * scaled, axis=1, keepdims=True)
        columns.setdefault(m, []).append((low, column))
    for m, found in columns.items():
        found = sorted(found, key=lambda part: part[0])
        low = found[0][0]
        stack = [column for _, column in found]
        if low:
            stack = [jnp.zeros((low, 1), jnp.float32), *stack]
        result = jnp.where(lane == m, jnp.concatenate(stack, axis=0) if len(stack) > 1 else stack[0], result)
    return result


def finish_kernel(base_ref, cols_ref, packed, projected, earlier, out_ref, pairs, weights, moment, *, opened, groups):
    levels = cols_ref.shape[0]
    high = 3 * levels
    parts = BLOCK // LANES
    moment[0] = earlier[HERE]

    def one_block(block, parts):
        wide = parts * LANES
        for p in range(parts):
            lane = slice(p * LANES, (p + 1) * LANES)
            weights[:, lane] = packed[block + p, high:, :]
            fill_pairs(pairs, 0, lane, packed[block + p, HERE * levels : (HERE + 1) * levels, :])
        moment[0] += nt_dot(pairs[0, :, :wide], weights[:, :wide])

    count = base_ref[groups, 0]
    ready = count // BLOCK
    lax.fori_loop(base_ref[opened, 0] // BLOCK, ready, lambda block, carry: (one_block(block * parts, parts), carry)[1], 0)
    left = count - ready * BLOCK

    @pl.when(left > BLOCK // 2)
    def _():
        one_block(ready * parts, parts)

    @pl.when((left > 0) & (left <= BLOCK // 2))
    def _():
        one_block(ready * parts, parts // 2)

    cols = cols_ref[...].astype(jnp.float32)
    out_ref[...] = contracted(cols, projected[HERE * levels : (HERE + 1) * levels, :], moment, 0)


def finish(base, cols, packed, projected, moment, opened, groups):
    levels, rays = cols.shape
    _, _, _, pair_count = pair_rows(levels)
    vmem = pl.BlockSpec(memory_space=pltpu.VMEM)
    return pl.pallas_call(
        functools.partial(finish_kernel, opened=opened, groups=groups),
        in_specs=[pl.BlockSpec(memory_space=pltpu.SMEM), vmem, vmem, vmem, vmem],
        out_shape=jax.ShapeDtypeStruct((levels, LANES), jnp.float32),
        scratch_shapes=[
            pltpu.VMEM((1, pair_count, BLOCK), jnp.bfloat16),
            pltpu.VMEM((rays, BLOCK), jnp.bfloat16),
            pltpu.VMEM((1, pair_count, rays), jnp.float32),
        ],
        compiler_params=pltpu.CompilerParams(vmem_limit_bytes=CHUNK_BYTES),
        cost_estimate=CHEAP,
        name="finish",
    )(base, cols, packed, projected, moment)


def chunk_kernel(*refs, spans_of, carrier, opens, closes):
    base_ref, place_ref, here_ref, measured_ref, cols_ref, carried_before, carried_after = refs[:7]
    refs = refs[7:]
    sources = []
    for _ in spans_of:
        sources.append(refs[:2])
        refs = refs[2:]
    refs = refs[2:] if opens else refs[4:]
    spectrum_ref, packed, moment, projected = refs[:4]
    refs = refs[4:]
    if closes:
        terms_refs = refs[:2]
        refs = refs[2:]
    table, modelled, pairs, weights, sems = refs
    levels = here_ref.shape[0]
    rays = measured_ref.shape[0]
    high = 3 * levels
    begin = spans_of[0][0]
    end = spans_of[-1][0] + spans_of[-1][1]
    _, _, spans, pair_count = pair_rows(levels)
    cols = [ref.astype(jnp.float32) for ref in (carried_before[:, carrier:], cols_ref[...], carried_after[:, carrier:])]
    rows = jnp.concatenate([c.T for c in cols], axis=1).astype(jnp.bfloat16)

    if opens:
        packed[0] = jnp.zeros(packed.shape[1:], packed.dtype)

    kinds = range(3) if opens else AWAY
    copies = []
    for (first, width), (before_ref, after_ref) in zip(spans_of, sources, strict=True):
        for low_lane in range(0, width, PIECE):
            size = min(PIECE, width - low_lane)
            local = slice(low_lane, low_lane + size)
            overall = slice(first + low_lane, first + low_lane + size)
            inside = slice(first + low_lane - begin, first + low_lane - begin + size)
            table[0:levels, inside] = before_ref[:, local]
            table[levels : 2 * levels, inside] = here_ref[:, overall]
            table[2 * levels : high, inside] = after_ref[:, local]
            depth = jnp.dot(rows, table[:high, inside], preferred_element_type=jnp.float32)
            spectrum = jnp.exp(-depth)
            modelled[:, inside] = spectrum
            copy = pltpu.make_async_copy(modelled.at[:, inside], spectrum_ref.at[:, overall], sems.at[len(copies)])
            copy.start()
            copies.append(copy)
            table[high:, inside] = (spectrum * spectrum).astype(jnp.bfloat16)
            groups = range(overall.start // LANES, overall.stop // LANES)
            places = [place_ref[g : g + 1, :] for g in groups]
            kept = jnp.concatenate(places, axis=1) >= 0
            error = jnp.where(kept, (measured_ref[:, overall] - spectrum) * spectrum, 0.0).astype(jnp.bfloat16)
            projected[...] += nt_dot(table[:high, inside], error)
            for n, (g, place) in enumerate(zip(groups, places, strict=True)):
                at = base_ref[g, 0] // LANES
                chosen = (iota((2 * LANES, LANES), 0) + at * LANES == place).astype(jnp.bfloat16)
                moved = nt_dot(table[:, inside.start + n * LANES : inside.start + (n + 1) * LANES], chosen).astype(jnp.bfloat16)
                packed[at] = packed[at] + moved[:, :LANES]
                packed[at + 1] = moved[:, LANES:]

    def one_block(block, parts):
        wide = parts * LANES
        for p in range(parts):
            lane = slice(p * LANES, (p + 1) * LANES)
            weights[:, lane] = packed[block + p, high:, :]
            for k in kinds:
                fill_pairs(pairs, k, lane, packed[block + p, k * levels : (k + 1) * levels, :])
        for k in kinds:
            moment[k] += nt_dot(pairs[k, :, :wide], weights[:, :wide])

    parts = BLOCK // LANES
    done = base_ref[begin // LANES, 0] // BLOCK
    count = base_ref[end // LANES, 0]
    ready = count // BLOCK
    lax.fori_loop(done, ready, lambda block, carry: (one_block(block * parts, parts), carry)[1], 0)

    if closes:
        last = base_ref[end // LANES - 1, 0] // LANES
        for d in range(2, parts + 1):
            packed[last + d] = jnp.zeros(packed.shape[1:], packed.dtype)
        left = count - ready * BLOCK
        @pl.when(left > BLOCK // 2)
        def _():
            one_block(ready * parts, parts)

        @pl.when((left > 0) & (left <= BLOCK // 2))
        def _():
            one_block(ready * parts, parts // 2)

        for terms_ref, k in zip(terms_refs, AWAY, strict=True):
            terms_ref[...] = contracted(cols[k], projected[k * levels : (k + 1) * levels, :], moment, k)
    for copy in copies:
        copy.wait()


def chunk(base, place, here, measured, cols, carried, carrier, spans_of, sources, state, closes):
    levels, points = here.shape
    rays = measured.shape[0]
    _, _, _, pair_count = pair_rows(levels)
    opens = len(state) == 2
    smem = pl.BlockSpec(memory_space=pltpu.SMEM)
    vmem = pl.BlockSpec(memory_space=pltpu.VMEM)
    hbm = pl.BlockSpec(memory_space=pltpu.HBM)
    width = sum(w for _, w in spans_of)
    args = [base, place, here, measured, cols, *carried]
    specs = [smem] + [vmem] * 6
    for pair in sources:
        args += pair
        specs += [vmem, vmem]
    aliases = {}
    aliases = {len(args) + n: 4 - len(state) + n for n in range(len(state))}
    args += state
    specs += [hbm, vmem, vmem, vmem][4 - len(state) :]
    shapes = [
        jax.ShapeDtypeStruct(measured.shape, jnp.float32),
        jax.ShapeDtypeStruct(((points + BLOCK) // LANES + 2, 3 * levels + rays, LANES), jnp.bfloat16),
        jax.ShapeDtypeStruct((3, pair_count, rays), jnp.float32),
        jax.ShapeDtypeStruct((3 * levels, rays), jnp.float32),
    ]
    out_specs = [hbm, vmem, vmem, vmem]
    if closes:
        shapes += [jax.ShapeDtypeStruct((levels, LANES), jnp.float32)] * 2
        out_specs += [vmem] * 2
    outs = pl.pallas_call(
        functools.partial(chunk_kernel, spans_of=spans_of, carrier=carrier, opens=opens, closes=closes),
        in_specs=specs,
        out_specs=out_specs,
        out_shape=shapes,
        scratch_shapes=[
            pltpu.VMEM((3 * levels + rays, width), jnp.bfloat16),
            pltpu.VMEM((rays, width), jnp.float32),
            pltpu.VMEM((3, pair_count, BLOCK), jnp.bfloat16),
            pltpu.VMEM((rays, BLOCK), jnp.bfloat16),
            pltpu.SemaphoreType.DMA((sum(pl.cdiv(w, PIECE) for _, w in spans_of),)),
        ],
        input_output_aliases=aliases,
        compiler_params=pltpu.CompilerParams(vmem_limit_bytes=CHUNK_BYTES),
        cost_estimate=CHEAP,
        name="chunk",
    )(*args)
    return outs[:4], outs[4:]


def quad_step(work, row, p):
    r = [work[p + i : p + i + 1, :] for i in range(4)]

    def entry(i, j):
        return jnp.broadcast_to(r[i][:, p + j : p + j + 1], r[i].shape)

    a, b, d = entry(0, 0), entry(0, 1), entry(1, 1)
    f0, f1, g0, g1 = entry(0, 2), entry(0, 3), entry(1, 2), entry(1, 3)
    h, q, v = entry(2, 2), entry(2, 3), entry(3, 3)
    inverse = 1.0 / (a * d - b * b)
    a, b, d = d * inverse, -b * inverse, a * inverse
    w00, w01 = a * f0 + b * g0, a * f1 + b * g1
    w10, w11 = b * f0 + d * g0, b * f1 + d * g1
    h, q, v = h - (f0 * w00 + g0 * w10), q - (f0 * w01 + g0 * w11), v - (f1 * w01 + g1 * w11)
    inverse = 1.0 / (h * v - q * q)
    h, q, v = v * inverse, -q * inverse, h * inverse
    t0, t1 = a * r[0] + b * r[1], b * r[0] + d * r[1]
    u0, u1 = r[2] - (f0 * t0 + g0 * t1), r[3] - (f1 * t0 + g1 * t1)
    s2, s3 = h * u0 + q * u1, q * u0 + v * u1
    s0, s1 = t0 - (w00 * s2 + w01 * s3), t1 - (w10 * s2 + w11 * s3)
    update = None
    for i, s in enumerate((s0, s1, s2, s3)):
        column = work[:, p + i : p + i + 1]
        term = jnp.where(row[:, :1] == p + i, column - 1.0, column) * s
        update = term if update is None else update + term
    return work - update


def solve_kernel(*refs, scale):
    parts = refs[:6]
    prior_ref, out_ref = refs[6:]
    levels = prior_ref.shape[1]
    total = parts[0][...]
    for part in parts[1:]:
        total = total + part[...]
    terms = total * scale
    row = iota((levels, LANES), 0)
    lane = iota((levels, LANES), 1)
    square = terms[:, :levels]
    flipped = jnp.concatenate([square.T, jnp.zeros((levels, LANES - levels), jnp.float32)], axis=1)
    lower = row // HALF >= lane // HALF
    work = jnp.where(lower | (lane >= levels), terms, flipped)
    diagonal = jnp.sum(jnp.where(row == lane, work, 0.0), axis=1, keepdims=True)
    mean = jnp.sum(diagonal, axis=0, keepdims=True) * (1.0 / levels) + 1e-06
    eye = iota((levels, levels), 0) == iota((levels, levels), 1)
    prior = jnp.sum(jnp.where(eye, prior_ref[...], 0.0), axis=1, keepdims=True)
    work = work + jnp.where(row == lane, prior * mean, 0.0)
    for p in range(0, levels, 4):
        work = quad_step(work, row, p)
    column = work[:, levels : levels + 1]
    out_ref[...] = -jnp.sum(jnp.where(eye, column, 0.0), axis=0, keepdims=True)


def solve(parts, prior_weight, scale):
    return pl.pallas_call(
        functools.partial(solve_kernel, scale=scale),
        out_shape=jax.ShapeDtypeStruct((1, prior_weight.shape[1]), jnp.float32),
        compiler_params=pltpu.CompilerParams(vmem_limit_bytes=SMALL_BYTES),
        cost_estimate=CHEAP,
        name="solve",
    )(*parts, prior_weight)


def swapped(block, axis):
    size = lax.axis_size(axis)
    return lax.ppermute(block, axis, [(i, size - 1 - i) for i in range(size)])


def shards(absorption, absorber, seg_level, seg_count, seg_length, measured, window_mask, prior_weight):
    table = absorption[0]
    levels, points = table.shape
    rays = measured.shape[1]
    unit = points // sum(WIDTHS)
    widths = [w * unit for w in WIDTHS]
    firsts = [sum(widths[:c]) for c in range(len(widths))]
    mask = window_mask.reshape(points // LANES, LANES)
    level = jnp.swapaxes(seg_level[0], 1, 2)
    length = jnp.swapaxes(seg_length[0], 1, 2)
    count = seg_count.reshape(3, 1, rays)
    first_send, second_send, cols = prepare(level, count, length, absorber, table, firsts[0], widths[0])
    carried = (traded(first_send, 0), traded(second_send, 1))
    place, base, table_here, measured_here, *sends, moment, projected = stage(cols, mask, table, measured[0], firsts[1:], widths[1:])
    base = base[:, :1]
    received = [carried, (traded(sends[0], 0), traded(sends[0], 1))]
    state = (moment, projected)
    for c, span in enumerate(zip(firsts, widths, strict=True)):
        closes = c == len(widths) - 1
        if c + 2 < len(widths):
            send, *arrived = lax.optimization_barrier((sends[c + 1], *received[c]))
            received[c] = tuple(arrived)
            received.append((traded(send, 0), traded(send, 1)))
        state, terms = chunk(
            base, place, table_here, measured_here, cols, received[0], widths[0], (span,), [received[c]], state, closes
        )
    spectrum = state[0]
    arriving = (traded(terms[0], 0), traded(terms[1], 1))
    mine = (finish(base, cols, state[1], state[3], state[2], widths[0] // LANES, points // LANES), *arriving)
    others = tuple(swapped(part, "spec") for part in mine)
    scale = 1.0 / (rays * points * lax.axis_size("spec"))
    state_step = solve(mine + others, prior_weight[None, :], scale)
    return (spectrum[None], state_step)


def solution(mesh):
    return jax.shard_map(
        shards,
        mesh=mesh,
        in_specs=(
            P(("orbits", "sector"), None, "spec"),
            P(("orbits", "sector"), None),
            P(("orbits", "sector"), None, None, None),
            P(("orbits", "sector"), None, None),
            P(("orbits", "sector"), None, None, None),
            P(("orbits", "sector"), None, "spec"),
            P("spec"),
            P(),
        ),
        out_specs=(P(("orbits", "sector"), None, "spec"), P(("orbits", "sector"), None)),
        check_vma=False,
    )
```
